32 devices in a mesh: lon: 8 (over z, x), lat: 4 (over y, core).
Axes of the slice: x: 2, y: 2, z: 4, core: 2. Of those that a mesh axis runs over, the one named last changes fastest.
Arguments:
- efield_north: float32 [128, 3072], P('lat', 'lon'), may hold values from -13 to 14
- efield_east: float32 [128, 3072], P('lat', 'lon'), may hold values from -13 to 14
- efield_up: float32 [128, 3072], P('lat', 'lon'), may hold values from -13 to 14
- hfield_north: float32 [128, 3072], P('lat', 'lon'), may hold values from -13 to 14
- hfield_east: float32 [128, 3072], P('lat', 'lon'), may hold values from -13 to 14
- hfield_up: float32 [128, 3072], P('lat', 'lon'), may hold values from -13 to 14
- sigma_profile: float32 [24], replicated, may hold values from 0.001 to 30
- flash_lat: int32 [64], replicated, may hold values from 0 to 126
- flash_lon: int32 [64], replicated, may hold values from 0 to 127
- flash_step: int32 [64], replicated, may hold values from 0 to 8
- flash_amp: float32 [64], replicated, may hold values from 20 to 60
Outputs:
- electric_north: float32 [128, 3072], P('lat', 'lon')
- electric_east: float32 [128, 3072], P('lat', 'lon')
- electric_up: float32 [128, 3072], P('lat', 'lon')
- magnetic_north: float32 [128, 3072], P('lat', 'lon')
- magnetic_east: float32 [128, 3072], P('lat', 'lon')
- magnetic_up: float32 [128, 3072], P('lat', 'lon')
- zonal_means: float32 [9, 2, 128, 24], P(None, None, 'lat')
The draws below stay inside these ranges and needn't reach their ends.
All inputs are finite; a program needn't handle non-finite values.
Results may differ from the reference program's by a relative error of at most 0.0003.
Values sent between devices are 32-bit elements; how exact they have to be, the bound alone decides.
A program may use at most 64 MiB of HBM per device.

```python
import math
import jax
import jax.numpy as jnp
from jax import lax

ALT = 24
CHANNEL = 3
STEPS = 9
FLASHES = 64
NLON = 128
NLAT = 128


def field_draw(key, salt_value):
    inner_key = jax.random.fold_in(key, salt_value)
    rough_key, scale_key = jax.random.split(inner_key)
    field_shape = (NLAT, NLON, ALT)
    spread = jnp.exp(jax.random.uniform(scale_key, field_shape, jnp.float32, math.log(0.3), math.log(3.0)))
    lon_place = (jnp.arange(NLON, dtype=jnp.float32) / NLON)[None, :, None]
    rough_part = jax.random.truncated_normal(rough_key, -4.0, 4.0, field_shape, jnp.float32)
    background = 0.5 + lon_place
    return (rough_part * spread + background).reshape(NLAT, NLON * ALT)


def draw_efield_north(key, part):
    return field_draw(key, 11)


def draw_efield_east(key, part):
    return field_draw(key, 12)


def draw_efield_up(key, part):
    return field_draw(key, 13)


def draw_hfield_north(key, part):
    return field_draw(key, 21)


def draw_hfield_east(key, part):
    return field_draw(key, 22)


def draw_hfield_up(key, part):
    return field_draw(key, 23)


def with_ends(entries, own_key, smallest, largest):
    spot = [jax.random.randint(jax.random.fold_in(own_key, axis), (), 0, length) for axis, length in enumerate(entries.shape)]
    main_axis = entries.shape.index(max(entries.shape))
    beside = spot[:main_axis] + [(spot[main_axis] + 1) % entries.shape[main_axis]] + spot[main_axis + 1:]
    return entries.at[tuple(spot)].set(smallest).at[tuple(beside)].set(largest)


def setup_inputs(seed: int = 0) -> dict:
    keys = jax.random.split(jax.random.key(seed), 12)
    return {
        "efield_north": draw_efield_north(jax.random.fold_in(keys[11], 71), 0),
        "efield_east": draw_efield_east(jax.random.fold_in(keys[11], 71), 0),
        "efield_up": draw_efield_up(jax.random.fold_in(keys[11], 71), 0),
        "hfield_north": draw_hfield_north(jax.random.fold_in(keys[11], 71), 0),
        "hfield_east": draw_hfield_east(jax.random.fold_in(keys[11], 71), 0),
        "hfield_up": draw_hfield_up(jax.random.fold_in(keys[11], 71), 0),
        "sigma_profile": jnp.clip(jnp.exp(jax.random.uniform(keys[6], (ALT,), jnp.float32, math.log(0.001), math.log(30.0))), 0.001, 30.0),
        "flash_lat": with_ends(jax.random.randint(keys[7], (FLASHES,), 0, NLAT - 1), jax.random.fold_in(keys[7], 1), 0, (NLAT - 1) - 1).astype(jnp.int32),
        "flash_lon": with_ends(jax.random.randint(keys[8], (FLASHES,), 0, NLON), jax.random.fold_in(keys[8], 1), 0, NLON - 1).astype(jnp.int32),
        "flash_step": with_ends(jax.random.randint(keys[9], (FLASHES,), 0, STEPS), jax.random.fold_in(keys[9], 1), 0, STEPS - 1).astype(jnp.int32),
        "flash_amp": jnp.clip(jax.random.uniform(keys[10], (FLASHES,), jnp.float32, 20.0, 60.0), 20.0, 60.0),
    }


RADIUS_CELLS = 1529.0
COURANT = 0.9

def time_step(lat_count, lon_count):
    lon_angle = 2.0 * math.pi / lon_count
    lat_angle = math.pi / lat_count
    narrowest = RADIUS_CELLS * lon_angle * math.sin(lat_angle)
    lat_length = RADIUS_CELLS * lat_angle
    return COURANT / math.sqrt(1.0 / narrowest ** 2 + 1.0 / lat_length ** 2 + 1.0)

def grid_terms(row_index, lat_count, lon_count):
    lon_angle = 2.0 * math.pi / lon_count
    lat_angle = math.pi / lat_count
    row_place = row_index.astype(jnp.float32)
    centre = -0.5 * math.pi + (row_place + 0.5) * lat_angle
    north_edge = centre + 0.5 * lat_angle
    south_edge = centre - 0.5 * lat_angle
    next_centre = centre + lat_angle
    at_pole = row_index == lat_count - 1
    at_south = row_index == 0
    scale_lon = RADIUS_CELLS * lon_angle
    band_area = 2.0 * RADIUS_CELLS * scale_lon * math.sin(0.5 * lat_angle)
    span_centre = scale_lon * jnp.cos(centre)
    span_next = scale_lon * jnp.cos(next_centre)
    span_edge = jnp.where(at_pole, 0.0, scale_lon * jnp.cos(north_edge))
    span_south = jnp.where(at_south, 0.0, scale_lon * jnp.cos(south_edge))
    area_centre = band_area * jnp.cos(centre)
    area_edge = jnp.where(at_pole, 1.0, band_area * jnp.cos(north_edge))
    safe_edge = jnp.where(at_pole, 1.0, span_edge)
    keeper = jnp.where(at_pole, 0.0, 1.0)
    return (span_centre, span_next, span_edge, span_south, area_centre, area_edge, safe_edge, keeper)

def level_above(values):
    return jnp.concatenate([values[1:], jnp.zeros_like(values[:1])], axis=0)

def level_below(values):
    return jnp.concatenate([jnp.zeros_like(values[:1]), values[:-1]], axis=0)

def from_south(values):
    return jnp.concatenate([jnp.zeros_like(values[:, :1]), values[:, :-1]], axis=1)

def from_north(values):
    return jnp.concatenate([values[:, 1:], jnp.zeros_like(values[:, :1])], axis=1)

def reference(efield_north, efield_east, efield_up, hfield_north, hfield_east, hfield_up, sigma_profile, flash_lat, flash_lon, flash_step, flash_amp):
    lat_count = efield_north.shape[0]
    lon_count = efield_north.shape[1] // ALT

    def to_cube(flat_field):
        return flat_field.reshape(lat_count, lon_count, ALT).transpose(2, 0, 1)

    def to_flat(cube_field):
        return cube_field.transpose(1, 2, 0).reshape(lat_count, lon_count * ALT)
    time_delta = time_step(lat_count, lon_count)
    lat_length = RADIUS_CELLS * math.pi / lat_count
    row_index = jnp.arange(lat_count, dtype=jnp.int32)
    metric_terms = [metric_term[None, :, None] for metric_term in grid_terms(row_index, lat_count, lon_count)]
    span_centre, span_next, span_edge, span_south, area_centre, area_edge, safe_edge, keeper = metric_terms
    half_loss = 0.5 * time_delta * sigma_profile
    decay_factor = ((1.0 - half_loss) / (1.0 + half_loss))[:, None, None]
    drive_factor = (time_delta / (1.0 + half_loss))[:, None, None]
    channel = (jnp.arange(ALT) < CHANNEL).astype(jnp.float32)[:, None, None]
    south_row = (row_index == 0)[None, :, None]
    north_row = (row_index == lat_count - 1)[None, :, None]
    e_north = to_cube(efield_north)
    e_east = keeper * to_cube(efield_east)
    e_up = keeper * to_cube(efield_up)
    h_north = keeper * to_cube(hfield_north)
    h_east = to_cube(hfield_east)
    h_up = to_cube(hfield_up)
    history = []
    for step_index in range(STEPS):
        mean_east = lax.optimization_barrier(jnp.mean(e_east, axis=2))
        mean_up = lax.optimization_barrier(jnp.mean(h_up, axis=2))
        history.append(jnp.stack([mean_east, mean_up]))
        north_next = jnp.roll(e_north, -1, axis=2)
        up_next = jnp.roll(e_up, -1, axis=2)
        circulation = span_south * from_south(e_east) - span_edge * e_east + lat_length * (north_next - e_north)
        up_new = h_up - time_delta * circulation / area_centre
        south_cap = mean_up[:, 0] + time_delta * span_edge[0, 0, 0] * mean_east[:, 0] / area_centre[0, 0, 0]
        north_cap = mean_up[:, -1] - time_delta * span_edge[0, -2, 0] * mean_east[:, -2] / area_centre[0, -1, 0]
        up_new = jnp.where(south_row, south_cap[:, None, None], up_new)
        up_new = jnp.where(north_row, north_cap[:, None, None], up_new)
        north_new = keeper * (h_north - time_delta * ((e_up - up_next) / safe_edge + level_above(e_east) - e_east))
        east_new = h_east - time_delta * ((e_up - from_south(e_up)) / lat_length - (level_above(e_north) - e_north))
        h_up, h_north, h_east = (up_new, north_new, east_new)
        e_north_new = decay_factor * e_north + drive_factor * (h_east - level_below(h_east) - (h_up - jnp.roll(h_up, 1, axis=2)) / span_centre)
        e_east_new = keeper * (decay_factor * e_east + drive_factor * ((from_north(h_up) - h_up) / lat_length - (h_north - level_below(h_north))))
        loop_flux = span_centre * h_east - span_next * from_north(h_east) + lat_length * (h_north - jnp.roll(h_north, 1, axis=2))
        strike = (flash_step == step_index).astype(jnp.float32) * flash_amp
        source = jnp.zeros((lat_count, lon_count), jnp.float32).at[flash_lat, flash_lon].add(strike)
        e_up_new = keeper * (decay_factor * e_up + drive_factor * loop_flux / area_edge) + drive_factor * channel * source[None]
        e_north, e_east, e_up = (e_north_new, e_east_new, e_up_new)
    zonal_out = jnp.stack(history).transpose(0, 1, 3, 2)
    return (to_flat(e_north), to_flat(e_east), to_flat(e_up), to_flat(h_north), to_flat(h_east), to_flat(h_up), zonal_out)
```

```python
import functools
import math

import jax
import jax.numpy as jnp
import numpy as np
from jax import lax
from jax.experimental import pallas as pl
from jax.experimental.pallas import tpu as pltpu
from jax.sharding import PartitionSpec as P

CHANNEL = 3
STEPS = 9
RADIUS_CELLS = 1529.0
COURANT = 0.9
VMEM_GRANT = 16 * 1024 * 1024

HALO_ROWS = 16
HALO_LANES = 256
MESH = pl.DeviceIdType.MESH
EN, EE, EU, HN, HE, HR = range(6)
(C_AS, C_BE, C_CN, C_DU, C_DT, C_GC, C_IC, C_JN, C_KL, C_LY) = range(10)
C_KEEP = 10
NINTH = ((EE, EU), (EN, EE, EU, HE, HR))


def time_step(lat_count, lon_count):
    lon_angle = 2.0 * math.pi / lon_count
    lat_angle = math.pi / lat_count
    narrowest = RADIUS_CELLS * lon_angle * math.sin(lat_angle)
    lat_length = RADIUS_CELLS * lat_angle
    return COURANT / math.sqrt(1.0 / narrowest**2 + 1.0 / lat_length**2 + 1.0)


def row_table(lat_count, lon_count):
    f = np.float32
    lon_angle = 2.0 * math.pi / lon_count
    lat_angle = math.pi / lat_count
    dt = time_step(lat_count, lon_count)
    ly = RADIUS_CELLS * math.pi / lat_count
    row = np.arange(lat_count)
    centre = f(-0.5 * math.pi) + (row.astype(f) + f(0.5)) * f(lat_angle)
    north = centre + f(0.5 * lat_angle)
    south = centre - f(0.5 * lat_angle)
    following = centre + f(lat_angle)
    pole = row == lat_count - 1
    scale = RADIUS_CELLS * lon_angle
    band = 2.0 * RADIUS_CELLS * scale * math.sin(0.5 * lat_angle)
    lc = f(scale) * np.cos(centre)
    ln = f(scale) * np.cos(following)
    le = np.where(pole, f(0), f(scale) * np.cos(north))
    ls = np.where(row == 0, f(0), f(scale) * np.cos(south))
    ls[-1] = le[-2]
    ac = f(band) * np.cos(centre)
    ae = np.where(pole, f(1), f(band) * np.cos(north))
    se = np.where(pole, f(1), le)
    keep = np.where(pole, f(0), f(1))
    table = np.zeros((lat_count + 2 * HALO_ROWS, 128), f)
    inner = table[HALO_ROWS:-HALO_ROWS]
    inner[:, C_AS] = dt * ls / ac
    inner[:, C_BE] = dt * le / ac
    inner[:, C_CN] = dt * ly / ac
    inner[:, C_DU] = keep * dt / se
    inner[:, C_DT] = keep * dt
    inner[:, C_GC] = 1.0 / lc
    inner[:, C_IC] = keep * lc / ae
    inner[:, C_JN] = keep * ln / ae
    inner[:, C_KL] = keep * ly / ae
    inner[:, C_LY] = keep / ly
    inner[:, C_KEEP] = keep
    return table


def turn(x, by):
    return pltpu.roll(x, by % x.shape[1], 1)


def div24(x):
    return lax.shift_right_logical(x * 2731, 16)


def spread(x, first, count):
    lane = lax.broadcasted_iota(jnp.int32, (8, 128), 1)
    out = []
    for v in range(first, first + count):
        off = (128 * v - HALO_LANES) % 24
        out.append(jnp.where(lane < 96, turn(x, -off), turn(x, 24 - off)))
    return jnp.concatenate(out, axis=1)


def exchange(
    dims,
    en, ee, eu, hn, he, hr, h_sigma, h_lat, h_lon, h_step, h_amp, h_table,
    ext, src, coef, lanes, zon,
    sums_out, sums_in, strip, small, sigma, f_lat, f_lon, f_step, f_amp, table,
    ninth_out, ninth_in,
    load, send_b, recv_b, send_l, recv_l, send_r, recv_r, send_s, recv_s, send_z, recv_z,
    send_n, recv_n,
    ack_lon, ack_lat,
):
    n_lat, n_lon, layers, dt, ly = dims
    fields = (en, ee, eu, hn, he, hr)
    rows, width = en.shape
    strokes = h_lat.shape[1]
    wide = width + 2 * HALO_LANES
    tall = rows + 2 * HALO_ROWS
    vregs = wide // 128
    low = HALO_ROWS
    lat, lon = lax.axis_index("lat"), lax.axis_index("lon")
    own_r = pl.ds(low, rows)
    own_c = pl.ds(HALO_LANES, width)

    def at(a, b):
        row = jnp.clip(lat + a, 0, n_lat - 1) if a else lat
        return {"lat": row, "lon": lax.rem(lon + b + n_lon, n_lon)}

    def there(a):
        return lat + a >= 0 if a < 0 else lat + a < n_lat

    def signal(sem, a, b):
        pl.semaphore_signal(sem, inc=1, device_id=at(a, b), device_id_type=MESH)

    barrier = pltpu.get_barrier_semaphore()
    for k in range(1, n_lon):
        pl.when(lon + k < n_lon)(lambda k=k: signal(barrier, 0, k))
    pl.when(there(1))(lambda: signal(barrier, 1, 0))

    loads = [
        pltpu.make_async_copy(x, ext.at[f, own_r, own_c], load.at[f])
        for f, x in enumerate(fields)
    ]
    here_rows = h_table.at[pl.ds(pl.multiple_of(lat * rows, 8), tall), :]
    pairs = (
        (here_rows, table), (h_sigma, sigma), (h_lat, f_lat), (h_lon, f_lon),
        (h_step, f_step), (h_amp, f_amp),
    )
    loads += [pltpu.make_async_copy(x, y, load.at[6 + i]) for i, (x, y) in enumerate(pairs)]
    for copy in loads:
        copy.start()

    def lon_copy(b, f):
        i = f if b > 0 else 6 + f
        cut = pl.ds(width - HALO_LANES, HALO_LANES) if b > 0 else pl.ds(0, HALO_LANES)
        land = pl.ds(0, HALO_LANES) if b > 0 else pl.ds(HALO_LANES + width, HALO_LANES)
        return pltpu.make_async_remote_copy(
            src_ref=fields[f].at[:, cut],
            dst_ref=ext.at[f, own_r, land],
            send_sem=send_b.at[i],
            recv_sem=recv_b.at[i],
            device_id=at(0, b),
            device_id_type=MESH,
        )

    def lat_cut(a):
        return (rows - 8, low - 8) if a > 0 else (0, low + rows)

    def lat_copy(a, f):
        i = f if a > 0 else 6 + f
        cut, land = lat_cut(a)
        return pltpu.make_async_remote_copy(
            src_ref=fields[f].at[pl.ds(cut, 8), :],
            dst_ref=ext.at[f, pl.ds(land, 8), own_c],
            send_sem=send_l.at[i],
            recv_sem=recv_l.at[i],
            device_id=at(a, 0),
            device_id_type=MESH,
        )

    def relay_copy(a, side, part):
        i = part + 2 * side + (0 if a > 0 else 4)
        cut, land = lat_cut(a)
        these = pl.ds(3 * part, 3)
        cols = pl.ds(side * (HALO_LANES + width), HALO_LANES)
        return pltpu.make_async_remote_copy(
            src_ref=ext.at[these, pl.ds(low + cut, 8), cols],
            dst_ref=ext.at[these, pl.ds(land, 8), cols],
            send_sem=send_r.at[i],
            recv_sem=recv_r.at[i],
            device_id=at(a, 0),
            device_id_type=MESH,
        )

    def sum_copy(k):
        return pltpu.make_async_remote_copy(
            src_ref=sums_out,
            dst_ref=sums_in.at[k],
            send_sem=send_s.at[k],
            recv_sem=recv_s.at[k],
            device_id=at(0, k),
            device_id_type=MESH,
        )

    def zone_copy(a):
        i = 0 if a > 0 else 1
        return pltpu.make_async_remote_copy(
            src_ref=strip.at[pl.ds(rows - 8, 8) if a > 0 else pl.ds(0, 8), :],
            dst_ref=sums_in.at[0, pl.ds(0, 8) if a > 0 else pl.ds(8, 8), :],
            send_sem=send_z.at[i],
            recv_sem=recv_z.at[i],
            device_id=at(a, 0),
            device_id_type=MESH,
        )

    def ninth_copy(a):
        i = 0 if a > 0 else 1
        return pltpu.make_async_remote_copy(
            src_ref=ninth_out.at[i],
            dst_ref=ninth_in.at[i],
            send_sem=send_n.at[i],
            recv_sem=recv_n.at[i],
            device_id=at(a, 0),
            device_id_type=MESH,
        )

    def all_fields(make, side, act):
        for f in range(6):
            getattr(make(side, f), act)()

    earlier = lon + (lat > 0).astype(jnp.int32)
    pl.when(earlier > 0)(lambda: pl.semaphore_wait(barrier, earlier))
    for k in range(n_lon - 1, 0, -1):
        pl.when(lon - k >= 0)(lambda k=k: signal(ack_lon.at[k], 0, -k))
    pl.when(there(-1))(lambda: signal(ack_lat, -1, 0))

    pl.when(lon == n_lon - 1)(lambda: all_fields(lon_copy, 1, "start"))
    pl.when(lon > 0)(lambda: all_fields(lon_copy, -1, "start"))
    pl.when(there(-1))(lambda: all_fields(lat_copy, -1, "start"))

    for a, first in ((-1, 0), (1, low + rows)):
        def clear(first=first):
            ext[:, first:first + low, :] = jnp.zeros((6, low, wide), jnp.float32)
        pl.when(jnp.logical_not(there(a)))(clear)

    for copy in loads[:7]:
        copy.wait()

    def fold(x):
        for by in (width // 2, width // 4, width // 8, width // 16):
            x = x + turn(x, by)
        return x[:, :128] * (1.0 / (n_lon * (width // layers)))

    lane = lax.broadcasted_iota(jnp.int32, (rows, 128), 1)
    kept = jnp.broadcast_to(table[low:low + rows, C_KEEP:C_KEEP + 1], (rows, 128))
    sums_out[...] = jnp.where(
        lane < layers,
        kept * fold(ext[EE, own_r, own_c]),
        jnp.where(
            lane < 2 * layers, kept * fold(ext[HN, own_r, own_c]), fold(ext[HR, own_r, own_c])
        ),
    )
    for k in range(1, n_lon):
        pl.when(lon + k >= n_lon)(lambda k=k: sum_copy(k).start())

    def to_north():
        pl.semaphore_wait(ack_lat, 1)
        all_fields(lat_copy, 1, "start")
    pl.when(there(1))(to_north)

    for k in range(1, n_lon):
        def to_later(k=k):
            pl.semaphore_wait(ack_lon.at[k], 1)
            if k == 1:
                all_fields(lon_copy, 1, "start")
            if k == n_lon - 1:
                all_fields(lon_copy, -1, "start")
            sum_copy(k).start()
        pl.when(lon + k < n_lon)(to_later)

    for copy in loads[7:]:
        copy.wait()
    rows_tab = table[...]
    for c in range(10):
        coef[c] = jnp.broadcast_to(rows_tab[:, c:c + 1], (tall, 128))
    small[...] = jnp.zeros((8, 128), jnp.float32)
    small[0:1, 0:layers] = sigma[...]
    one = jnp.broadcast_to(small[0:1, :], (8, 128))
    pair = one + turn(one, 24)
    sig = pair + turn(pair, 48) + turn(one, 96)
    half = 0.5 * dt * sig
    dec = (1.0 - half) / (1.0 + half)
    drv = dt / (1.0 + half)

    at_lane = lax.broadcasted_iota(jnp.int32, (8, wide), 1) + 8
    layer = at_lane - 24 * div24(at_lane)
    lanes[0] = spread(dec, 0, vregs)
    lanes[1] = spread(drv, 0, vregs)
    lanes[2] = jnp.where(layer < CHANNEL, lanes[1], 0.0)
    lanes[3] = jnp.where(layer == layers - 1, 0.0, 1.0)
    lanes[4] = jnp.where(layer == 0, 0.0, 1.0)

    place = lax.broadcasted_iota(jnp.int32, (wide, strokes), 0) + 8
    cell = div24(place) - 11 + lon * (width // layers)
    total_lon = n_lon * (width // layers)
    cell = jnp.where(cell < 0, cell + total_lon, cell)
    cell = jnp.where(cell >= total_lon, cell - total_lon, cell)
    cells = (cell == f_lon[...]).astype(jnp.float32).astype(jnp.bfloat16)
    row_no = lax.broadcasted_iota(jnp.int32, (tall, strokes), 0) + (lat * rows - low)
    in_row = jnp.where(row_no == f_lat[...], jnp.broadcast_to(f_amp[...], (tall, strokes)), 0.0)

    def sources(s, carry):
        amps = jnp.where(f_step[...] == s, in_row, 0.0)
        total = None
        for _ in range(3):
            part = amps.astype(jnp.bfloat16)
            amps = amps - part.astype(jnp.float32)
            term = lax.dot_general(
                part, cells, (((1,), (1,)), ((), ())), preferred_element_type=jnp.float32
            )
            total = term if total is None else total + term
        src[pl.ds(pl.multiple_of(s * tall, 8), tall), :] = total
        return carry
    lax.fori_loop(0, STEPS, sources, 0)

    for k in range(1, n_lon):
        sum_copy(k).wait()
    mean = sums_out[...]
    for k in range(1, n_lon):
        mean = mean + sums_in[k]
    strip[...] = mean
    for a in (-1, 1):
        pl.when(there(a))(lambda a=a: zone_copy(a).start())

    def unpack(x):
        out = []
        lane_no = lax.broadcasted_iota(jnp.int32, x.shape, 1)
        for f in range(3):
            y = jnp.where(lane_no < layers, turn(x, -layers * f), 0.0)
            p = y + turn(y, 24)
            out.append(p + turn(p, 48) + turn(y, 96))
        return out

    zon[:, 0:low, :] = jnp.zeros((3, low, 128), jnp.float32)
    zon[:, low + rows:, :] = jnp.zeros((3, low, 128), jnp.float32)
    for f, z in enumerate(unpack(mean)):
        zon[f, own_r, :] = z

    for part in (0, 1):
        for side in (0, 1):
            for f in range(3 * part, 3 * part + 3):
                lon_copy(1 if side == 0 else -1, f).wait_recv()
            for a in (-1, 1):
                pl.when(there(a))(lambda a=a, side=side, part=part: relay_copy(a, side, part).start())

    for a in (-1, 1):
        def spare(a=a):
            i, row = (0, low + rows - STEPS) if a > 0 else (1, low + STEPS - 1)
            ninth_out[i] = jnp.zeros((8, wide), jnp.float32)
            for f in NINTH[i]:
                ninth_out[i, f:f + 1, :] = ext[f, row:row + 1, :]
            ninth_copy(a).start()
        pl.when(there(a))(spare)

    for a in (-1, 1):
        def take(a=a):
            ninth_copy(a).wait_recv()
            i, row = (0, low - STEPS) if a > 0 else (1, low + rows + STEPS - 1)
            for f in NINTH[i]:
                ext[f, row:row + 1, :] = ninth_in[i, f:f + 1, :]
            zone_copy(a).wait_recv()
            if a > 0:
                for f, z in enumerate(unpack(sums_in[0, 0:8, :])):
                    zon[f, low - 8:low, :] = z
            else:
                for f, z in enumerate(unpack(sums_in[0, 8:16, :])):
                    zon[f, low + rows:low + rows + 8, :] = z
            all_fields(lat_copy, a, "wait_recv")
            for part in (0, 1):
                for side in (0, 1):
                    relay_copy(a, side, part).wait_recv()
        pl.when(there(-a))(take)

        def sent(a=a):
            zone_copy(a).wait_send()
            ninth_copy(a).wait_send()
            all_fields(lat_copy, a, "wait_send")
            for part in (0, 1):
                for side in (0, 1):
                    relay_copy(a, side, part).wait_send()
        pl.when(there(a))(sent)
    for b in (-1, 1):
        all_fields(lon_copy, b, "wait_send")

    def pole():
        last = pl.ds(low + rows - 8, 8)
        keep = jnp.broadcast_to(table[low + rows - 8:low + rows, C_KEEP:C_KEEP + 1], (8, wide))
        for f in (EE, EU, HN):
            ext[f, last, :] = keep * ext[f, last, :]
    pl.when(jnp.logical_not(there(1)))(pole)


def march(
    dims,
    ext, src, coef, lanes, zon_in,
    o_en, o_ee, o_eu, o_hn, o_he, o_hr, o_zon,
    buf, zon, zon_rows, done,
):
    n_lat, n_lon, layers, dt, ly = dims
    tall, wide = ext.shape[1:]
    rows, width = tall - 2 * HALO_ROWS, wide - 2 * HALO_LANES
    groups = tall // 8
    own_groups = range(HALO_ROWS // 8, groups - HALO_ROWS // 8)
    low = HALO_ROWS
    lat = lax.axis_index("lat")
    own_r = slice(low, low + rows)
    z_dec, z_drv, z_top, z_bot = [lanes.at[i, :, HALO_LANES:HALO_LANES + 128] for i in (0, 1, 3, 4)]
    zon[...] = zon_in[...]
    lane = lax.broadcasted_iota(jnp.int32, (rows, 128), 1)

    def record(s):
        both = jnp.where(lane < layers, zon[0, own_r, :], turn(zon[2, own_r, :], layers))
        both = jnp.transpose(both)
        zon_rows[s, 0] = both[0:layers]
        zon_rows[s, 1] = both[layers:2 * layers]

    def zonal_h():
        for g in range(1, groups - 1):
            r = 8 * g
            east = zon[0, r:r + 8, :]
            zon[2, r:r + 8, :] = (
                zon[2, r:r + 8, :]
                - coef[C_AS, r:r + 8] * zon[0, r - 1:r + 7, :]
                + coef[C_BE, r:r + 8] * east
            )
            zon[1, r:r + 8, :] = zon[1, r:r + 8, :] - coef[C_DT, r:r + 8] * (
                z_top[...] * turn(east, -1) - east
            )

    def zonal_e():
        for g in range(1, groups - 1):
            r = 8 * g
            up, north = zon[2, r:r + 8, :], zon[1, r:r + 8, :]
            zon[0, r:r + 8, :] = z_dec[...] * zon[0, r:r + 8, :] + z_drv[...] * (
                coef[C_LY, r:r + 8] * (zon[2, r + 1:r + 9, :] - up)
                - (north - z_bot[...] * turn(north, 1))
            )

    def magnetic(old, a, b, span, beyond):
        count = (b - a) // 128

        def rowc(c, g):
            return jnp.concatenate([coef[c, 8 * g:8 * g + 8]] * count, axis=1)

        top = lanes[3, :, a:b]
        for g in (*span, *beyond):
            r = 8 * g
            here, south = slice(r, r + 8), slice(r - 1, r + 7)
            e_n, e_e, e_u = old[EN, here, a:b], old[EE, here, a:b], old[EU, here, a:b]
            up = (
                old[HR, here, a:b]
                - rowc(C_AS, g) * old[EE, south, a:b]
                + rowc(C_BE, g) * e_e
                - rowc(C_CN, g) * (turn(e_n, -layers) - e_n)
            )
            if g in (own_groups[0], own_groups[-1]):
                row = lax.broadcasted_iota(jnp.int32, (8, b - a), 0) + (lat * rows - low + r)
                pole = 0 if g == own_groups[0] else n_lat * rows - 1
                up = jnp.where(row == pole, spread(zon[2, here], a // 128, count), up)
            buf[HR, here, a:b] = up
            buf[HE, here, a:b] = (
                old[HE, here, a:b]
                - (dt / ly) * (e_u - old[EU, south, a:b])
                + dt * (top * turn(e_n, -1) - e_n)
            )
            if g in span:
                buf[HN, here, a:b] = (
                    old[HN, here, a:b]
                    - rowc(C_DU, g) * (e_u - turn(e_u, -layers))
                    - rowc(C_DT, g) * (top * turn(e_e, -1) - e_e)
                )

    def electric(old, s, a, b, first, span):
        count = (b - first) // 128
        skip = first - a

        def rowc(c, g):
            return jnp.concatenate([coef[c, 8 * g:8 * g + 8]] * count, axis=1)

        def turned(x, by):
            return turn(x, by)[:, skip:]

        decay, drive, channel, bot = [lanes[i, :, first:b] for i in (0, 1, 2, 4)]
        for g in span:
            r = 8 * g
            here, north = slice(r, r + 8), slice(r + 1, r + 9)
            w_n, w_e, w_r = buf[HN, here, a:b], buf[HE, here, a:b], buf[HR, here, a:b]
            h_n, h_e, h_r = w_n[:, skip:], w_e[:, skip:], w_r[:, skip:]
            buf[EN, here, first:b] = decay * old[EN, here, first:b] + drive * (
                h_e - bot * turned(w_e, 1) - rowc(C_GC, g) * (h_r - turned(w_r, layers))
            )
            buf[EE, here, first:b] = decay * old[EE, here, first:b] + drive * (
                rowc(C_LY, g) * (buf[HR, north, first:b] - h_r) - (h_n - bot * turned(w_n, 1))
            )
            buf[EU, here, first:b] = (
                decay * old[EU, here, first:b]
                + drive
                * (
                    rowc(C_IC, g) * h_e
                    - rowc(C_JN, g) * buf[HE, north, first:b]
                    + rowc(C_KL, g) * (h_n - turned(w_n, layers))
                )
                + channel * src[pl.ds(pl.multiple_of(s * tall + r, 8), 8), first:b]
            )

    inner = range(1, groups - 1)

    def step(old, s, a, b, beyond):
        record(s)
        zonal_h()
        magnetic(old, a, b, inner, beyond)
        zonal_e()
        electric(old, s, a, b, a, inner)

    def steps(begin, end, a, b):
        def one_step(s, carry):
            step(buf, s, a, b, ())
            return carry
        lax.fori_loop(begin, end, one_step, 0)

    step(ext, 0, 0, wide, (groups - 1,))
    steps(1, 4, 0, wide)
    steps(4, STEPS - 1, 128, wide - 128)

    outs = {EN: o_en, EE: o_ee, EU: o_eu, HN: o_hn, HE: o_he, HR: o_hr}
    record(STEPS - 1)
    zonal_h()
    magnetic(buf, 128, wide - 128, own_groups, (own_groups[-1] + 1,))
    copies = [pltpu.make_async_copy(zon_rows, o_zon, done.at[6])]
    for f in (HN, HE, HR, EN, EE, EU):
        if f == EN:
            for copy in copies:
                copy.start()
            electric(buf, STEPS - 1, 128, wide - HALO_LANES, HALO_LANES, own_groups)
        copy = pltpu.make_async_copy(
            buf.at[f, pl.ds(low, rows), pl.ds(HALO_LANES, width)], outs[f], done.at[f]
        )
        if f <= EU:
            copy.start()
        copies.append(copy)
    for copy in copies:
        copy.wait()


def body(
    efield_north,
    efield_east,
    efield_up,
    hfield_north,
    hfield_east,
    hfield_up,
    sigma_profile,
    flash_lat,
    flash_lon,
    flash_step,
    flash_amp,
):
    rows, width = efield_north.shape
    layers = sigma_profile.shape[0]
    n_lat, n_lon = lax.axis_size("lat"), lax.axis_size("lon")
    lat_count, lon_count = rows * n_lat, (width // layers) * n_lon
    dims = (
        n_lat,
        n_lon,
        layers,
        time_step(lat_count, lon_count),
        RADIUS_CELLS * math.pi / lat_count,
    )
    wide, tall = width + 2 * HALO_LANES, rows + 2 * HALO_ROWS
    f32 = jnp.float32
    vmem = pl.BlockSpec(memory_space=pltpu.VMEM)
    dma = pltpu.SemaphoreType.DMA
    hbm = pl.BlockSpec(memory_space=pltpu.HBM)
    strokes = flash_lat.shape[0]
    middle = [
        jax.ShapeDtypeStruct(shape, f32)
        for shape in (
            (6, tall, wide), (STEPS * tall, wide), (10, tall, 128), (5, 8, wide), (3, tall, 128)
        )
    ]
    held = pl.pallas_call(
        functools.partial(exchange, dims),
        out_shape=middle,
        in_specs=[hbm] * 12,
        out_specs=[vmem] * 5,
        scratch_shapes=[
            pltpu.VMEM((rows, 128), f32),
            pltpu.VMEM((n_lon, rows, 128), f32),
            pltpu.VMEM((rows, 128), f32),
            pltpu.VMEM((8, 128), f32),
            pltpu.VMEM((1, layers), f32),
            pltpu.VMEM((1, strokes), jnp.int32),
            pltpu.VMEM((1, strokes), jnp.int32),
            pltpu.VMEM((1, strokes), jnp.int32),
            pltpu.VMEM((1, strokes), f32),
            pltpu.VMEM((tall, 128), f32),
            pltpu.VMEM((2, 8, wide), f32),
            pltpu.VMEM((2, 8, wide), f32),
            dma((12,)),
            dma((12,)), dma((12,)), dma((12,)), dma((12,)), dma((8,)), dma((8,)),
            dma((n_lon,)), dma((n_lon,)), dma((2,)), dma((2,)), dma((2,)), dma((2,)),
            pltpu.SemaphoreType.REGULAR((n_lon,)), pltpu.SemaphoreType.REGULAR,
        ],
        compiler_params=pltpu.CompilerParams(
            collective_id=0, has_side_effects=True, vmem_limit_bytes=VMEM_GRANT
        ),
    )(
        efield_north,
        efield_east,
        efield_up,
        hfield_north,
        hfield_east,
        hfield_up,
        sigma_profile[None, :],
        flash_lat[None, :],
        flash_lon[None, :],
        flash_step[None, :],
        flash_amp[None, :],
        jnp.asarray(row_table(lat_count, lon_count)),
    )
    outs = [jax.ShapeDtypeStruct((rows, width), f32)] * 6
    outs += [jax.ShapeDtypeStruct((STEPS, 2, layers, rows), f32)]
    results = pl.pallas_call(
        functools.partial(march, dims),
        out_shape=outs,
        in_specs=[vmem] * 5,
        out_specs=[hbm] * 7,
        scratch_shapes=[
            pltpu.VMEM((6, tall, wide), f32),
            pltpu.VMEM((3, tall, 128), f32),
            pltpu.VMEM((STEPS, 2, layers, rows), f32),
            dma((7,)),
        ],
        compiler_params=pltpu.CompilerParams(vmem_limit_bytes=VMEM_GRANT),
    )(*held)
    return (*results[:6], jnp.transpose(results[6], (0, 1, 3, 2)))


def solution(mesh):
    fields = P("lat", "lon")
    return jax.shard_map(
        body,
        mesh=mesh,
        in_specs=(fields,) * 6 + (P(),) * 5,
        out_specs=(fields,) * 6 + (P(None, None, "lat", None),),
        check_vma=False,
    )
```

```python
import functools
import math

import jax
import jax.numpy as jnp
import numpy as np
from jax import lax
from jax.experimental import pallas as pl
from jax.experimental.pallas import tpu as pltpu
from jax.sharding import PartitionSpec as P

CHANNEL = 3
STEPS = 9
RADIUS_CELLS = 1529.0
COURANT = 0.9
VMEM_GRANT = 16 * 1024 * 1024

HALO_ROWS = 16
HALO_LANES = 256
MESH = pl.DeviceIdType.MESH
EN, EE, EU, HN, HE, HR = range(6)
(C_AS, C_BE, C_CN, C_DU, C_DT, C_GC, C_IC, C_JN, C_KL, C_LY) = range(10)
C_KEEP = 10
NINTH = ((EE, EU), (EN, EE, EU, HE, HR))


def time_step(lat_count, lon_count):
    lon_angle = 2.0 * math.pi / lon_count
    lat_angle = math.pi / lat_count
    narrowest = RADIUS_CELLS * lon_angle * math.sin(lat_angle)
    lat_length = RADIUS_CELLS * lat_angle
    return COURANT / math.sqrt(1.0 / narrowest**2 + 1.0 / lat_length**2 + 1.0)


def row_table(lat_count, lon_count):
    f = np.float32
    lon_angle = 2.0 * math.pi / lon_count
    lat_angle = math.pi / lat_count
    dt = time_step(lat_count, lon_count)
    ly = RADIUS_CELLS * math.pi / lat_count
    row = np.arange(lat_count)
    centre = f(-0.5 * math.pi) + (row.astype(f) + f(0.5)) * f(lat_angle)
    north = centre + f(0.5 * lat_angle)
    south = centre - f(0.5 * lat_angle)
    following = centre + f(lat_angle)
    pole = row == lat_count - 1
    scale = RADIUS_CELLS * lon_angle
    band = 2.0 * RADIUS_CELLS * scale * math.sin(0.5 * lat_angle)
    lc = f(scale) * np.cos(centre)
    ln = f(scale) * np.cos(following)
    le = np.where(pole, f(0), f(scale) * np.cos(north))
    ls = np.where(row == 0, f(0), f(scale) * np.cos(south))
    ls[-1] = le[-2]
    ac = f(band) * np.cos(centre)
    ae = np.where(pole, f(1), f(band) * np.cos(north))
    se = np.where(pole, f(1), le)
    keep = np.where(pole, f(0), f(1))
    table = np.zeros((lat_count + 2 * HALO_ROWS, 128), f)
    inner = table[HALO_ROWS:-HALO_ROWS]
    inner[:, C_AS] = dt * ls / ac
    inner[:, C_BE] = dt * le / ac
    inner[:, C_CN] = dt * ly / ac
    inner[:, C_DU] = keep * dt / se
    inner[:, C_DT] = keep * dt
    inner[:, C_GC] = 1.0 / lc
    inner[:, C_IC] = keep * lc / ae
    inner[:, C_JN] = keep * ln / ae
    inner[:, C_KL] = keep * ly / ae
    inner[:, C_LY] = keep / ly
    inner[:, C_KEEP] = keep
    return table


def turn(x, by):
    return pltpu.roll(x, by % x.shape[1], 1)


def div24(x):
    return lax.shift_right_logical(x * 2731, 16)


def spread(x, first, count):
    lane = lax.broadcasted_iota(jnp.int32, (8, 128), 1)
    out = []
    for v in range(first, first + count):
        off = (128 * v - HALO_LANES) % 24
        out.append(jnp.where(lane < 96, turn(x, -off), turn(x, 24 - off)))
    return jnp.concatenate(out, axis=1)


def exchange(
    dims,
    en, ee, eu, hn, he, hr, h_sigma, h_lat, h_lon, h_step, h_amp, h_table,
    ext, src, coef, lanes, zon,
    sums_out, sums_in, strip, small, sigma, f_lat, f_lon, f_step, f_amp, table,
    ninth_out, ninth_in,
    load, send_b, recv_b, send_l, recv_l, send_r, recv_r, send_s, recv_s, send_z, recv_z,
    send_n, recv_n,
    ack_lon, ack_lat,
):
    n_lat, n_lon, layers, dt, ly = dims
    fields = (en, ee, eu, hn, he, hr)
    rows, width = en.shape
    strokes = h_lat.shape[1]
    wide = width + 2 * HALO_LANES
    tall = rows + 2 * HALO_ROWS
    vregs = wide // 128
    low = HALO_ROWS
    lat, lon = lax.axis_index("lat"), lax.axis_index("lon")
    own_r = pl.ds(low, rows)
    own_c = pl.ds(HALO_LANES, width)

    def at(a, b):
        row = jnp.clip(lat + a, 0, n_lat - 1) if a else lat
        return {"lat": row, "lon": lax.rem(lon + b + n_lon, n_lon)}

    def there(a):
        return lat + a >= 0 if a < 0 else lat + a < n_lat

    def signal(sem, a, b):
        pl.semaphore_signal(sem, inc=1, device_id=at(a, b), device_id_type=MESH)

    barrier = pltpu.get_barrier_semaphore()
    for k in range(1, n_lon):
        pl.when(lon + k < n_lon)(lambda k=k: signal(barrier, 0, k))
    pl.when(there(1))(lambda: signal(barrier, 1, 0))

    loads = [
        pltpu.make_async_copy(x, ext.at[f, own_r, own_c], load.at[f])
        for f, x in enumerate(fields)
    ]
    here_rows = h_table.at[pl.ds(pl.multiple_of(lat * rows, 8), tall), :]
    pairs = (
        (here_rows, table), (h_sigma, sigma), (h_lat, f_lat), (h_lon, f_lon),
        (h_step, f_step), (h_amp, f_amp),
    )
    loads += [pltpu.make_async_copy(x, y, load.at[6 + i]) for i, (x, y) in enumerate(pairs)]
    for copy in loads:
        copy.start()

    def lon_copy(b, f):
        i = f if b > 0 else 6 + f
        cut = pl.ds(width - HALO_LANES, HALO_LANES) if b > 0 else pl.ds(0, HALO_LANES)
        land = pl.ds(0, HALO_LANES) if b > 0 else pl.ds(HALO_LANES + width, HALO_LANES)
        return pltpu.make_async_remote_copy(
            src_ref=fields[f].at[:, cut],
            dst_ref=ext.at[f, own_r, land],
            send_sem=send_b.at[i],
            recv_sem=recv_b.at[i],
            device_id=at(0, b),
            device_id_type=MESH,
        )

    def lat_cut(a):
        return (rows - 8, low - 8) if a > 0 else (0, low + rows)

    def lat_copy(a, f):
        i = f if a > 0 else 6 + f
        cut, land = lat_cut(a)
        return pltpu.make_async_remote_copy(
            src_ref=fields[f].at[pl.ds(cut, 8), :],
            dst_ref=ext.at[f, pl.ds(land, 8), own_c],
            send_sem=send_l.at[i],
            recv_sem=recv_l.at[i],
            device_id=at(a, 0),
            device_id_type=MESH,
        )

    def relay_copy(a, side, part):
        i = part + 2 * side + (0 if a > 0 else 4)
        cut, land = lat_cut(a)
        these = pl.ds(3 * part, 3)
        cols = pl.ds(side * (HALO_LANES + width), HALO_LANES)
        return pltpu.make_async_remote_copy(
            src_ref=ext.at[these, pl.ds(low + cut, 8), cols],
            dst_ref=ext.at[these, pl.ds(land, 8), cols],
            send_sem=send_r.at[i],
            recv_sem=recv_r.at[i],
            device_id=at(a, 0),
            device_id_type=MESH,
        )

    def sum_copy(k):
        return pltpu.make_async_remote_copy(
            src_ref=sums_out,
            dst_ref=sums_in.at[k],
            send_sem=send_s.at[k],
            recv_sem=recv_s.at[k],
            device_id=at(0, k),
            device_id_type=MESH,
        )

    def zone_copy(a):
        i = 0 if a > 0 else 1
        return pltpu.make_async_remote_copy(
            src_ref=strip.at[pl.ds(rows - 8, 8) if a > 0 else pl.ds(0, 8), :],
            dst_ref=sums_in.at[0, pl.ds(0, 8) if a > 0 else pl.ds(8, 8), :],
            send_sem=send_z.at[i],
            recv_sem=recv_z.at[i],
            device_id=at(a, 0),
            device_id_type=MESH,
        )

    def ninth_copy(a):
        i = 0 if a > 0 else 1
        return pltpu.make_async_remote_copy(
            src_ref=ninth_out.at[i],
            dst_ref=ninth_in.at[i],
            send_sem=send_n.at[i],
            recv_sem=recv_n.at[i],
            device_id=at(a, 0),
            device_id_type=MESH,
        )

    def all_fields(make, side, act):
        for f in range(6):
            getattr(make(side, f), act)()

    earlier = lon + (lat > 0).astype(jnp.int32)
    pl.when(earlier > 0)(lambda: pl.semaphore_wait(barrier, earlier))
    for k in range(n_lon - 1, 0, -1):
        pl.when(lon - k >= 0)(lambda k=k: signal(ack_lon.at[k], 0, -k))
    pl.when(there(-1))(lambda: signal(ack_lat, -1, 0))

    pl.when(lon == n_lon - 1)(lambda: all_fields(lon_copy, 1, "start"))
    pl.when(lon > 0)(lambda: all_fields(lon_copy, -1, "start"))
    pl.when(there(-1))(lambda: all_fields(lat_copy, -1, "start"))

    for a, first in ((-1, 0), (1, low + rows)):
        def clear(first=first):
            ext[:, first:first + low, :] = jnp.zeros((6, low, wide), jnp.float32)
        pl.when(jnp.logical_not(there(a)))(clear)

    for copy in loads[:7]:
        copy.wait()

    def fold(x):
        for by in (width // 2, width // 4, width // 8, width // 16):
            x = x + turn(x, by)
        return x[:, :128] * (1.0 / (n_lon * (width // layers)))

    lane = lax.broadcasted_iota(jnp.int32, (rows, 128), 1)
    kept = jnp.broadcast_to(table[low:low + rows, C_KEEP:C_KEEP + 1], (rows, 128))
    sums_out[...] = jnp.where(
        lane < layers,
        kept * fold(ext[EE, own_r, own_c]),
        jnp.where(
            lane < 2 * layers, kept * fold(ext[HN, own_r, own_c]), fold(ext[HR, own_r, own_c])
        ),
    )
    for k in range(1, n_lon):
        pl.when(lon + k >= n_lon)(lambda k=k: sum_copy(k).start())

    def to_north():
        pl.semaphore_wait(ack_lat, 1)
        all_fields(lat_copy, 1, "start")
    pl.when(there(1))(to_north)

    for k in range(1, n_lon):
        def to_later(k=k):
            pl.semaphore_wait(ack_lon.at[k], 1)
            if k == 1:
                all_fields(lon_copy, 1, "start")
            if k == n_lon - 1:
                all_fields(lon_copy, -1, "start")
            sum_copy(k).start()
        pl.when(lon + k < n_lon)(to_later)

    for copy in loads[7:]:
        copy.wait()
    rows_tab = table[...]
    for c in range(10):
        coef[c] = jnp.broadcast_to(rows_tab[:, c:c + 1], (tall, 128))
    small[...] = jnp.zeros((8, 128), jnp.float32)
    small[0:1, 0:layers] = sigma[...]
    one = jnp.broadcast_to(small[0:1, :], (8, 128))
    pair = one + turn(one, 24)
    sig = pair + turn(pair, 48) + turn(one, 96)
    half = 0.5 * dt * sig
    dec = (1.0 - half) / (1.0 + half)
    drv = dt / (1.0 + half)

    at_lane = lax.broadcasted_iota(jnp.int32, (8, wide), 1) + 8
    layer = at_lane - 24 * div24(at_lane)
    lanes[0] = spread(dec, 0, vregs)
    lanes[1] = spread(drv, 0, vregs)
    lanes[2] = jnp.where(layer < CHANNEL, lanes[1], 0.0)
    lanes[3] = jnp.where(layer == layers - 1, 0.0, 1.0)
    lanes[4] = jnp.where(layer == 0, 0.0, 1.0)

    place = lax.broadcasted_iota(jnp.int32, (wide, strokes), 0) + 8
    cell = div24(place) - 11 + lon * (width // layers)
    total_lon = n_lon * (width // layers)
    cell = jnp.where(cell < 0, cell + total_lon, cell)
    cell = jnp.where(cell >= total_lon, cell - total_lon, cell)
    cells = (cell == f_lon[...]).astype(jnp.float32).astype(jnp.bfloat16)
    row_no = lax.broadcasted_iota(jnp.int32, (tall, strokes), 0) + (lat * rows - low)
    in_row = jnp.where(row_no == f_lat[...], jnp.broadcast_to(f_amp[...], (tall, strokes)), 0.0)

    def sources(s, carry):
        amps = jnp.where(f_step[...] == s, in_row, 0.0)
        total = None
        for _ in range(3):
            part = amps.astype(jnp.bfloat16)
            amps = amps - part.astype(jnp.float32)
            term = lax.dot_general(
                part, cells, (((1,), (1,)), ((), ())), preferred_element_type=jnp.float32
            )
            total = term if total is None else total + term
        src[pl.ds(pl.multiple_of(s * tall, 8), tall), :] = total
        return carry
    lax.fori_loop(0, STEPS, sources, 0)

    for k in range(1, n_lon):
        sum_copy(k).wait()
    mean = sums_out[...]
    for k in range(1, n_lon):
        mean = mean + sums_in[k]
    strip[...] = mean
    for a in (-1, 1):
        pl.when(there(a))(lambda a=a: zone_copy(a).start())

    def unpack(x):
        out = []
        lane_no = lax.broadcasted_iota(jnp.int32, x.shape, 1)
        for f in range(3):
            y = jnp.where(lane_no < layers, turn(x, -layers * f), 0.0)
            p = y + turn(y, 24)
            out.append(p + turn(p, 48) + turn(y, 96))
        return out

    zon[:, 0:low, :] = jnp.zeros((3, low, 128), jnp.float32)
    zon[:, low + rows:, :] = jnp.zeros((3, low, 128), jnp.float32)
    for f, z in enumerate(unpack(mean)):
        zon[f, own_r, :] = z

    for part in (0, 1):
        for side in (0, 1):
            for f in range(3 * part, 3 * part + 3):
                lon_copy(1 if side == 0 else -1, f).wait_recv()
            for a in (-1, 1):
                pl.when(there(a))(lambda a=a, side=side, part=part: relay_copy(a, side, part).start())

    for a in (-1, 1):
        def spare(a=a):
            i, row = (0, low + rows - STEPS) if a > 0 else (1, low + STEPS - 1)
            ninth_out[i] = jnp.zeros((8, wide), jnp.float32)
            for f in NINTH[i]:
                ninth_out[i, f:f + 1, :] = ext[f, row:row + 1, :]
            ninth_copy(a).start()
        pl.when(there(a))(spare)

    for a in (-1, 1):
        def take(a=a):
            ninth_copy(a).wait_recv()
            i, row = (0, low - STEPS) if a > 0 else (1, low + rows + STEPS - 1)
            for f in NINTH[i]:
                ext[f, row:row + 1, :] = ninth_in[i, f:f + 1, :]
            zone_copy(a).wait_recv()
            if a > 0:
                for f, z in enumerate(unpack(sums_in[0, 0:8, :])):
                    zon[f, low - 8:low, :] = z
            else:
                for f, z in enumerate(unpack(sums_in[0, 8:16, :])):
                    zon[f, low + rows:low + rows + 8, :] = z
            all_fields(lat_copy, a, "wait_recv")
            for part in (0, 1):
                for side in (0, 1):
                    relay_copy(a, side, part).wait_recv()
        pl.when(there(-a))(take)

        def sent(a=a):
            zone_copy(a).wait_send()
            ninth_copy(a).wait_send()
            all_fields(lat_copy, a, "wait_send")
            for part in (0, 1):
                for side in (0, 1):
                    relay_copy(a, side, part).wait_send()
        pl.when(there(a))(sent)
    for b in (-1, 1):
        all_fields(lon_copy, b, "wait_send")

    def pole():
        last = pl.ds(low + rows - 8, 8)
        keep = jnp.broadcast_to(table[low + rows - 8:low + rows, C_KEEP:C_KEEP + 1], (8, wide))
        for f in (EE, EU, HN):
            ext[f, last, :] = keep * ext[f, last, :]
    pl.when(jnp.logical_not(there(1)))(pole)


def march(
    dims,
    ext, src, coef, lanes, zon_in,
    o_en, o_ee, o_eu, o_hn, o_he, o_hr, o_zon,
    buf, zon, zon_rows, done,
):
    n_lat, n_lon, layers, dt, ly = dims
    tall, wide = ext.shape[1:]
    rows, width = tall - 2 * HALO_ROWS, wide - 2 * HALO_LANES
    groups = tall // 8
    own_groups = range(HALO_ROWS // 8, groups - HALO_ROWS // 8)
    low = HALO_ROWS
    lat = lax.axis_index("lat")
    own_r = slice(low, low + rows)
    z_dec, z_drv, z_top, z_bot = [lanes.at[i, :, HALO_LANES:HALO_LANES + 128] for i in (0, 1, 3, 4)]
    zon[...] = zon_in[...]
    lane = lax.broadcasted_iota(jnp.int32, (rows, 128), 1)

    def record(s):
        both = jnp.where(lane < layers, zon[0, own_r, :], turn(zon[2, own_r, :], layers))
        both = jnp.transpose(both)
        zon_rows[s, 0] = both[0:layers]
        zon_rows[s, 1] = both[layers:2 * layers]

    def zonal_h():
        for g in range(1, groups - 1):
            r = 8 * g
            east = zon[0, r:r + 8, :]
            zon[2, r:r + 8, :] = (
                zon[2, r:r + 8, :]
                - coef[C_AS, r:r + 8] * zon[0, r - 1:r + 7, :]
                + coef[C_BE, r:r + 8] * east
            )
            zon[1, r:r + 8, :] = zon[1, r:r + 8, :] - coef[C_DT, r:r + 8] * (
                z_top[...] * turn(east, -1) - east
            )

    def zonal_e():
        for g in range(1, groups - 1):
            r = 8 * g
            up, north = zon[2, r:r + 8, :], zon[1, r:r + 8, :]
            zon[0, r:r + 8, :] = z_dec[...] * zon[0, r:r + 8, :] + z_drv[...] * (
                coef[C_LY, r:r + 8] * (zon[2, r + 1:r + 9, :] - up)
                - (north - z_bot[...] * turn(north, 1))
            )

    def magnetic(old, a, b, span, beyond):
        count = (b - a) // 128

        def rowc(c, g):
            return jnp.concatenate([coef[c, 8 * g:8 * g + 8]] * count, axis=1)

        top = lanes[3, :, a:b]
        for g in (*span, *beyond):
            r = 8 * g
            here, south = slice(r, r + 8), slice(r - 1, r + 7)
            e_n, e_e, e_u = old[EN, here, a:b], old[EE, here, a:b], old[EU, here, a:b]
            up = (
                old[HR, here, a:b]
                - rowc(C_AS, g) * old[EE, south, a:b]
                + rowc(C_BE, g) * e_e
                - rowc(C_CN, g) * (turn(e_n, -layers) - e_n)
            )
            if g in (own_groups[0], own_groups[-1]):
                row = lax.broadcasted_iota(jnp.int32, (8, b - a), 0) + (lat * rows - low + r)
                pole = 0 if g == own_groups[0] else n_lat * rows - 1
                up = jnp.where(row == pole, spread(zon[2, here], a // 128, count), up)
            buf[HR, here, a:b] = up
            buf[HE, here, a:b] = (
                old[HE, here, a:b]
                - (dt / ly) * (e_u - old[EU, south, a:b])
                + dt * (top * turn(e_n, -1) - e_n)
            )
            if g in span:
                buf[HN, here, a:b] = (
                    old[HN, here, a:b]
                    - rowc(C_DU, g) * (e_u - turn(e_u, -layers))
                    - rowc(C_DT, g) * (top * turn(e_e, -1) - e_e)
                )

    def electric(old, s, a, b, first, span):
        count = (b - first) // 128
        skip = first - a

        def rowc(c, g):
            return jnp.concatenate([coef[c, 8 * g:8 * g + 8]] * count, axis=1)

        def turned(x, by):
            return turn(x, by)[:, skip:]

        decay, drive, channel, bot = [lanes[i, :, first:b] for i in (0, 1, 2, 4)]
        for g in span:
            r = 8 * g
            here, north = slice(r, r + 8), slice(r + 1, r + 9)
            w_n, w_e, w_r = buf[HN, here, a:b], buf[HE, here, a:b], buf[HR, here, a:b]
            h_n, h_e, h_r = w_n[:, skip:], w_e[:, skip:], w_r[:, skip:]
            buf[EN, here, first:b] = decay * old[EN, here, first:b] + drive * (
                h_e - bot * turned(w_e, 1) - rowc(C_GC, g) * (h_r - turned(w_r, layers))
            )
            buf[EE, here, first:b] = decay * old[EE, here, first:b] + drive * (
                rowc(C_LY, g) * (buf[HR, north, first:b] - h_r) - (h_n - bot * turned(w_n, 1))
            )
            buf[EU, here, first:b] = (
                decay * old[EU, here, first:b]
                + drive
                * (
                    rowc(C_IC, g) * h_e
                    - rowc(C_JN, g) * buf[HE, north, first:b]
                    + rowc(C_KL, g) * (h_n - turned(w_n, layers))
                )
                + channel * src[pl.ds(pl.multiple_of(s * tall + r, 8), 8), first:b]
            )

    inner = range(1, groups - 1)

    def step(old, s, a, b, beyond):
        record(s)
        zonal_h()
        magnetic(old, a, b, inner, beyond)
        zonal_e()
        electric(old, s, a, b, a, inner)

    def steps(begin, end, a, b):
        def one_step(s, carry):
            step(buf, s, a, b, ())
            return carry
        lax.fori_loop(begin, end, one_step, 0)

    step(ext, 0, 0, wide, (groups - 1,))
    steps(1, 4, 0, wide)
    steps(4, STEPS - 1, 128, wide - 128)

    outs = {EN: o_en, EE: o_ee, EU: o_eu, HN: o_hn, HE: o_he, HR: o_hr}
    record(STEPS - 1)
    zonal_h()
    magnetic(buf, 128, wide - 128, own_groups, (own_groups[-1] + 1,))
    copies = [pltpu.make_async_copy(zon_rows, o_zon, done.at[6])]
    for f in (HN, HE, HR, EN, EE, EU):
        if f == EN:
            for copy in copies:
                copy.start()
            electric(buf, STEPS - 1, 128, wide - HALO_LANES, HALO_LANES, own_groups)
        copy = pltpu.make_async_copy(
            buf.at[f, pl.ds(low, rows), pl.ds(HALO_LANES, width)], outs[f], done.at[f]
        )
        if f <= EU:
            copy.start()
        copies.append(copy)
    for copy in copies:
        copy.wait()


def body(
    efield_north,
    efield_east,
    efield_up,
    hfield_north,
    hfield_east,
    hfield_up,
    sigma_profile,
    flash_lat,
    flash_lon,
    flash_step,
    flash_amp,
):
    rows, width = efield_north.shape
    layers = sigma_profile.shape[0]
    n_lat, n_lon = lax.axis_size("lat"), lax.axis_size("lon")
    lat_count, lon_count = rows * n_lat, (width // layers) * n_lon
    dims = (
        n_lat,
        n_lon,
        layers,
        time_step(lat_count, lon_count),
        RADIUS_CELLS * math.pi / lat_count,
    )
    wide, tall = width + 2 * HALO_LANES, rows + 2 * HALO_ROWS
    f32 = jnp.float32
    vmem = pl.BlockSpec(memory_space=pltpu.VMEM)
    dma = pltpu.SemaphoreType.DMA
    hbm = pl.BlockSpec(memory_space=pltpu.HBM)
    strokes = flash_lat.shape[0]
    middle = [
        jax.ShapeDtypeStruct(shape, f32)
        for shape in (
            (6, tall, wide), (STEPS * tall, wide), (10, tall, 128), (5, 8, wide), (3, tall, 128)
        )
    ]
    held = pl.pallas_call(
        functools.partial(exchange, dims),
        out_shape=middle,
        in_specs=[hbm] * 12,
        out_specs=[vmem] * 5,
        scratch_shapes=[
            pltpu.VMEM((rows, 128), f32),
            pltpu.VMEM((n_lon, rows, 128), f32),
            pltpu.VMEM((rows, 128), f32),
            pltpu.VMEM((8, 128), f32),
            pltpu.VMEM((1, layers), f32),
            pltpu.VMEM((1, strokes), jnp.int32),
            pltpu.VMEM((1, strokes), jnp.int32),
            pltpu.VMEM((1, strokes), jnp.int32),
            pltpu.VMEM((1, strokes), f32),
            pltpu.VMEM((tall, 128), f32),
            pltpu.VMEM((2, 8, wide), f32),
            pltpu.VMEM((2, 8, wide), f32),
            dma((12,)),
            dma((12,)), dma((12,)), dma((12,)), dma((12,)), dma((8,)), dma((8,)),
            dma((n_lon,)), dma((n_lon,)), dma((2,)), dma((2,)), dma((2,)), dma((2,)),
            pltpu.SemaphoreType.REGULAR((n_lon,)), pltpu.SemaphoreType.REGULAR,
        ],
        compiler_params=pltpu.CompilerParams(
            collective_id=0, has_side_effects=True, vmem_limit_bytes=VMEM_GRANT
        ),
    )(*(pltpu.with_memory_space_constraint(x, pltpu.HBM) for x in (
        efield_north,
        efield_east,
        efield_up,
        hfield_north,
        hfield_east,
        hfield_up,
        sigma_profile[None, :],
        flash_lat[None, :],
        flash_lon[None, :],
        flash_step[None, :],
        flash_amp[None, :],
        jnp.asarray(row_table(lat_count, lon_count)),
    )))
    outs = [jax.ShapeDtypeStruct((rows, width), f32)] * 6
    outs += [jax.ShapeDtypeStruct((STEPS, 2, layers, rows), f32)]
    results = pl.pallas_call(
        functools.partial(march, dims),
        out_shape=outs,
        in_specs=[vmem] * 5,
        out_specs=[hbm] * 7,
        scratch_shapes=[
            pltpu.VMEM((6, tall, wide), f32),
            pltpu.VMEM((3, tall, 128), f32),
            pltpu.VMEM((STEPS, 2, layers, rows), f32),
            dma((7,)),
        ],
        compiler_params=pltpu.CompilerParams(vmem_limit_bytes=VMEM_GRANT),
    )(*held)
    return (*results[:6], jnp.transpose(results[6], (0, 1, 3, 2)))


def solution(mesh):
    fields = P("lat", "lon")
    return jax.shard_map(
        body,
        mesh=mesh,
        in_specs=(fields,) * 6 + (P(),) * 5,
        out_specs=(fields,) * 6 + (P(None, None, "lat", None),),
        check_vma=False,
    )
```

```python
import functools
import math

import jax
import jax.numpy as jnp
import numpy as np
from jax import lax
from jax.experimental import pallas as pl
from jax.experimental.pallas import tpu as pltpu
from jax.sharding import PartitionSpec as P

CHANNEL = 3
STEPS = 9
RADIUS_CELLS = 1529.0
COURANT = 0.9
VMEM_GRANT = 16 * 1024 * 1024

HALO_ROWS = 16
HALO_LANES = 256
MESH = pl.DeviceIdType.MESH
EN, EE, EU, HN, HE, HR = range(6)
(C_AS, C_BE, C_CN, C_DU, C_DT, C_GC, C_IC, C_JN, C_KL, C_LY) = range(10)
C_KEEP = 10
NINTH = ((EE, EU), (EN, EE, EU, HE, HR))


def time_step(lat_count, lon_count):
    lon_angle = 2.0 * math.pi / lon_count
    lat_angle = math.pi / lat_count
    narrowest = RADIUS_CELLS * lon_angle * math.sin(lat_angle)
    lat_length = RADIUS_CELLS * lat_angle
    return COURANT / math.sqrt(1.0 / narrowest**2 + 1.0 / lat_length**2 + 1.0)


def row_table(lat_count, lon_count):
    f = np.float32
    lon_angle = 2.0 * math.pi / lon_count
    lat_angle = math.pi / lat_count
    dt = time_step(lat_count, lon_count)
    ly = RADIUS_CELLS * math.pi / lat_count
    row = np.arange(lat_count)
    centre = f(-0.5 * math.pi) + (row.astype(f) + f(0.5)) * f(lat_angle)
    north = centre + f(0.5 * lat_angle)
    south = centre - f(0.5 * lat_angle)
    following = centre + f(lat_angle)
    pole = row == lat_count - 1
    scale = RADIUS_CELLS * lon_angle
    band = 2.0 * RADIUS_CELLS * scale * math.sin(0.5 * lat_angle)
    lc = f(scale) * np.cos(centre)
    ln = f(scale) * np.cos(following)
    le = np.where(pole, f(0), f(scale) * np.cos(north))
    ls = np.where(row == 0, f(0), f(scale) * np.cos(south))
    ls[-1] = le[-2]
    ac = f(band) * np.cos(centre)
    ae = np.where(pole, f(1), f(band) * np.cos(north))
    se = np.where(pole, f(1), le)
    keep = np.where(pole, f(0), f(1))
    table = np.zeros((lat_count + 2 * HALO_ROWS, 128), f)
    inner = table[HALO_ROWS:-HALO_ROWS]
    inner[:, C_AS] = dt * ls / ac
    inner[:, C_BE] = dt * le / ac
    inner[:, C_CN] = dt * ly / ac
    inner[:, C_DU] = keep * dt / se
    inner[:, C_DT] = keep * dt
    inner[:, C_GC] = 1.0 / lc
    inner[:, C_IC] = keep * lc / ae
    inner[:, C_JN] = keep * ln / ae
    inner[:, C_KL] = keep * ly / ae
    inner[:, C_LY] = keep / ly
    inner[:, C_KEEP] = keep
    return table


def turn(x, by):
    return pltpu.roll(x, by % x.shape[1], 1)


def div24(x):
    return lax.shift_right_logical(x * 2731, 16)


def spread(x, first, count):
    lane = lax.broadcasted_iota(jnp.int32, (8, 128), 1)
    out = []
    for v in range(first, first + count):
        off = (128 * v - HALO_LANES) % 24
        out.append(jnp.where(lane < 96, turn(x, -off), turn(x, 24 - off)))
    return jnp.concatenate(out, axis=1)


def exchange(
    dims,
    en, ee, eu, hn, he, hr, h_sigma, h_lat, h_lon, h_step, h_amp, h_table,
    ext, src, coef, lanes, zon,
    sums_out, sums_in, totals, zone_in, strip, small, sigma, f_lat, f_lon, f_step, f_amp, table,
    ninth_out, ninth_in,
    load, send_b, recv_b, send_l, recv_l, send_r, recv_r, send_s, recv_s, send_t, recv_t, send_z, recv_z,
    send_n, recv_n,
    ack_lon, ack_lat,
):
    n_lat, n_lon, layers, dt, ly = dims
    fields = (en, ee, eu, hn, he, hr)
    rows, width = en.shape
    strokes = h_lat.shape[1]
    wide = width + 2 * HALO_LANES
    tall = rows + 2 * HALO_ROWS
    vregs = wide // 128
    live = rows + 16
    low = HALO_ROWS
    lat, lon = lax.axis_index("lat"), lax.axis_index("lon")
    own_r = pl.ds(low, rows)
    own_c = pl.ds(HALO_LANES, width)

    def at(a, b):
        row = jnp.clip(lat + a, 0, n_lat - 1) if a else lat
        return {"lat": row, "lon": lax.rem(lon + b + n_lon, n_lon)}

    def there(a):
        return lat + a >= 0 if a < 0 else lat + a < n_lat

    def signal(sem, a, b):
        pl.semaphore_signal(sem, inc=1, device_id=at(a, b), device_id_type=MESH)

    barrier = pltpu.get_barrier_semaphore()
    for k in range(1, n_lon):
        pl.when(lon + k < n_lon)(lambda k=k: signal(barrier, 0, k))
    pl.when(there(1))(lambda: signal(barrier, 1, 0))

    loads = [
        pltpu.make_async_copy(x, ext.at[f, own_r, own_c], load.at[f])
        for f, x in enumerate(fields)
    ]
    here_rows = h_table.at[pl.ds(pl.multiple_of(lat * rows, 8), tall), :]
    pairs = (
        (here_rows, table), (h_sigma, sigma), (h_lat, f_lat), (h_lon, f_lon),
        (h_step, f_step), (h_amp, f_amp),
    )
    loads += [pltpu.make_async_copy(x, y, load.at[6 + i]) for i, (x, y) in enumerate(pairs)]
    for copy in loads:
        copy.start()

    def lon_copy(b, f):
        i = f if b > 0 else 6 + f
        cut = pl.ds(width - HALO_LANES, HALO_LANES) if b > 0 else pl.ds(0, HALO_LANES)
        land = pl.ds(0, HALO_LANES) if b > 0 else pl.ds(HALO_LANES + width, HALO_LANES)
        return pltpu.make_async_remote_copy(
            src_ref=fields[f].at[:, cut],
            dst_ref=ext.at[f, own_r, land],
            send_sem=send_b.at[i],
            recv_sem=recv_b.at[i],
            device_id=at(0, b),
            device_id_type=MESH,
        )

    def lat_cut(a):
        return (rows - 8, low - 8) if a > 0 else (0, low + rows)

    def lat_copy(a, f):
        i = f if a > 0 else 6 + f
        cut, land = lat_cut(a)
        return pltpu.make_async_remote_copy(
            src_ref=fields[f].at[pl.ds(cut, 8), :],
            dst_ref=ext.at[f, pl.ds(land, 8), own_c],
            send_sem=send_l.at[i],
            recv_sem=recv_l.at[i],
            device_id=at(a, 0),
            device_id_type=MESH,
        )

    def relay_copy(a, side, part):
        i = part + 2 * side + (0 if a > 0 else 4)
        cut, land = lat_cut(a)
        these = pl.ds(3 * part, 3)
        cols = pl.ds(side * (HALO_LANES + width), HALO_LANES)
        return pltpu.make_async_remote_copy(
            src_ref=ext.at[these, pl.ds(low + cut, 8), cols],
            dst_ref=ext.at[these, pl.ds(land, 8), cols],
            send_sem=send_r.at[i],
            recv_sem=recv_r.at[i],
            device_id=at(a, 0),
            device_id_type=MESH,
        )

    def sum_copy(k):
        return pltpu.make_async_remote_copy(
            src_ref=sums_out.at[lax.rem(lon + k, n_lon)],
            dst_ref=sums_in.at[k],
            send_sem=send_s.at[k],
            recv_sem=recv_s.at[k],
            device_id=at(0, k),
            device_id_type=MESH,
        )

    def total_copy(k):
        return pltpu.make_async_remote_copy(
            src_ref=totals.at[lon],
            dst_ref=totals.at[lon],
            send_sem=send_t.at[k],
            recv_sem=recv_t.at[k],
            device_id=at(0, k),
            device_id_type=MESH,
        )

    def total_from(k):
        there_lon = lax.rem(lon + n_lon - k, n_lon)
        return pltpu.make_async_remote_copy(
            src_ref=totals.at[there_lon],
            dst_ref=totals.at[there_lon],
            send_sem=send_t.at[k],
            recv_sem=recv_t.at[k],
            device_id=at(0, k),
            device_id_type=MESH,
        )

    def zone_copy(a):
        i = 0 if a > 0 else 1
        return pltpu.make_async_remote_copy(
            src_ref=strip.at[pl.ds(rows - 8, 8) if a > 0 else pl.ds(0, 8), :],
            dst_ref=zone_in.at[i],
            send_sem=send_z.at[i],
            recv_sem=recv_z.at[i],
            device_id=at(a, 0),
            device_id_type=MESH,
        )

    def ninth_copy(a):
        i = 0 if a > 0 else 1
        return pltpu.make_async_remote_copy(
            src_ref=ninth_out.at[i],
            dst_ref=ninth_in.at[i],
            send_sem=send_n.at[i],
            recv_sem=recv_n.at[i],
            device_id=at(a, 0),
            device_id_type=MESH,
        )

    def all_fields(make, side, act):
        for f in range(6):
            getattr(make(side, f), act)()

    earlier = lon + (lat > 0).astype(jnp.int32)
    pl.when(earlier > 0)(lambda: pl.semaphore_wait(barrier, earlier))
    for k in range(n_lon - 1, 0, -1):
        pl.when(lon - k >= 0)(lambda k=k: signal(ack_lon.at[k], 0, -k))
    pl.when(there(-1))(lambda: signal(ack_lat, -1, 0))

    pl.when(lon == n_lon - 1)(lambda: all_fields(lon_copy, 1, "start"))
    pl.when(lon > 0)(lambda: all_fields(lon_copy, -1, "start"))
    pl.when(there(-1))(lambda: all_fields(lat_copy, -1, "start"))

    for a, first in ((-1, 0), (1, low + rows)):
        def clear(first=first):
            ext[:, first:first + low, :] = jnp.zeros((6, low, wide), jnp.float32)
        pl.when(jnp.logical_not(there(a)))(clear)

    for copy in loads[:7]:
        copy.wait()

    def fold(x):
        for by in (width // 2, width // 4, width // 8, width // 16):
            x = x + turn(x, by)
        return x[:, :128] * (1.0 / (n_lon * (width // layers)))

    lane = lax.broadcasted_iota(jnp.int32, (rows, 128), 1)
    kept = jnp.broadcast_to(table[low:low + rows, C_KEEP:C_KEEP + 1], (rows, 128))
    partial = jnp.where(
        lane < layers,
        kept * fold(ext[EE, own_r, own_c]),
        jnp.where(
            lane < 2 * layers, kept * fold(ext[HN, own_r, own_c]), fold(ext[HR, own_r, own_c])
        ),
    )
    share = rows // n_lon
    for k in range(n_lon):
        sums_out[k] = partial[k * share:(k + 1) * share]
    for k in range(1, n_lon):
        pl.when(lon + k >= n_lon)(lambda k=k: sum_copy(k).start())

    def to_north():
        pl.semaphore_wait(ack_lat, 1)
        all_fields(lat_copy, 1, "start")
    pl.when(there(1))(to_north)

    def serve(k):
        def to_later():
            pl.semaphore_wait(ack_lon.at[k], 1)
            if k == 1:
                all_fields(lon_copy, 1, "start")
            if k == n_lon - 1:
                all_fields(lon_copy, -1, "start")
            sum_copy(k).start()
        pl.when(lon + k < n_lon)(to_later)

    serve(1)
    for copy in loads[7:]:
        copy.wait()
    rows_tab = table[...]
    for c in range(10):
        coef[c] = jnp.broadcast_to(rows_tab[:, c:c + 1], (tall, 128))
    small[...] = jnp.zeros((8, 128), jnp.float32)
    small[0:1, 0:layers] = sigma[...]
    one = jnp.broadcast_to(small[0:1, :], (8, 128))
    pair = one + turn(one, 24)
    sig = pair + turn(pair, 48) + turn(one, 96)
    half = 0.5 * dt * sig
    dec = (1.0 - half) / (1.0 + half)
    drv = dt / (1.0 + half)

    at_lane = lax.broadcasted_iota(jnp.int32, (8, wide), 1) + 8
    layer = at_lane - 24 * div24(at_lane)
    lanes[0] = spread(dec, 0, vregs)
    lanes[1] = spread(drv, 0, vregs)
    lanes[2] = jnp.where(layer == layers - 1, 0.0, 1.0)
    lanes[3] = jnp.where(layer == 0, 0.0, 1.0)

    half_lanes = lax.broadcasted_iota(jnp.int32, (1, 128), 1) < strokes

    def twice(x):
        return jnp.concatenate([x, x], axis=1)

    def column(x):
        return jnp.transpose(jnp.broadcast_to(x.astype(jnp.float32), (128, 2 * strokes)))

    cell = div24(at_lane[0:1]) - 11 + lon * (width // layers)
    total_lon = n_lon * (width // layers)
    cell = jnp.where(cell < 0, cell + total_lon, cell)
    cell = jnp.where(cell >= total_lon, cell - total_lon, cell)
    cell = jnp.where(layer[0:1] < CHANNEL, cell, -1).astype(jnp.float32)
    lon_of = jnp.concatenate([column(twice(f_lon[...]))] * vregs, axis=1)
    cells = (jnp.broadcast_to(cell, (2 * strokes, wide)) == lon_of).astype(jnp.float32)
    cells = cells.astype(jnp.bfloat16)
    row_no = lax.broadcasted_iota(jnp.int32, (live, 2 * strokes), 0) + (lat * rows - 8)
    in_row = jnp.where(
        row_no == twice(f_lat[...]),
        jnp.broadcast_to(twice(f_amp[...]), (live, 2 * strokes)),
        0.0,
    )
    steps_of = twice(f_step[...])
    left, right = [], []
    for s in range(STEPS):
        amps = jnp.where(steps_of == s, in_row, 0.0)
        upper = amps.astype(jnp.bfloat16).astype(jnp.float32)
        middle = (amps - upper).astype(jnp.bfloat16).astype(jnp.float32)
        left.append(jnp.where(half_lanes, upper, middle).astype(jnp.bfloat16))
        right.append(jnp.where(half_lanes, amps - upper - middle, 0.0).astype(jnp.bfloat16))
    total = None
    for part in (left, right):
        term = lax.dot_general(
            jnp.concatenate(part, axis=0), cells, (((1,), (0,)), ((), ())),
            preferred_element_type=jnp.float32,
        )
        total = term if total is None else total + term
    src[...] = total

    for k in range(2, n_lon):
        serve(k)

    for k in range(1, n_lon):
        sum_copy(k).wait()
    total = sums_out[lon]
    for k in range(1, n_lon):
        total = total + sums_in[k]
    totals[lon] = total
    for k in range(1, n_lon):
        total_copy(k).start()
    for k in range(1, n_lon):
        total_from(k).wait_recv()
    mean = jnp.concatenate([totals[k] for k in range(n_lon)], axis=0)
    strip[...] = mean
    for a in (-1, 1):
        pl.when(there(a))(lambda a=a: zone_copy(a).start())

    def unpack(x):
        out = []
        lane_no = lax.broadcasted_iota(jnp.int32, x.shape, 1)
        for f in range(3):
            y = jnp.where(lane_no < layers, turn(x, -layers * f), 0.0)
            p = y + turn(y, 24)
            out.append(p + turn(p, 48) + turn(y, 96))
        return out

    zon[:, 0:low, :] = jnp.zeros((3, low, 128), jnp.float32)
    zon[:, low + rows:, :] = jnp.zeros((3, low, 128), jnp.float32)
    for f, z in enumerate(unpack(mean)):
        zon[f, own_r, :] = z

    for part in (0, 1):
        for side in (0, 1):
            for f in range(3 * part, 3 * part + 3):
                lon_copy(1 if side == 0 else -1, f).wait_recv()
            for a in (-1, 1):
                pl.when(there(a))(lambda a=a, side=side, part=part: relay_copy(a, side, part).start())

    for a in (-1, 1):
        def spare(a=a):
            i, row = (0, low + rows - STEPS) if a > 0 else (1, low + STEPS - 1)
            ninth_out[i] = jnp.zeros((8, wide), jnp.float32)
            for f in NINTH[i]:
                ninth_out[i, f:f + 1, :] = ext[f, row:row + 1, :]
            ninth_copy(a).start()
        pl.when(there(a))(spare)

    for a in (-1, 1):
        def take(a=a):
            ninth_copy(a).wait_recv()
            i, row = (0, low - STEPS) if a > 0 else (1, low + rows + STEPS - 1)
            for f in NINTH[i]:
                ext[f, row:row + 1, :] = ninth_in[i, f:f + 1, :]
            zone_copy(a).wait_recv()
            if a > 0:
                for f, z in enumerate(unpack(zone_in[0])):
                    zon[f, low - 8:low, :] = z
            else:
                for f, z in enumerate(unpack(zone_in[1])):
                    zon[f, low + rows:low + rows + 8, :] = z
            all_fields(lat_copy, a, "wait_recv")
            for part in (0, 1):
                for side in (0, 1):
                    relay_copy(a, side, part).wait_recv()
        pl.when(there(-a))(take)

        def sent(a=a):
            zone_copy(a).wait_send()
            ninth_copy(a).wait_send()
            all_fields(lat_copy, a, "wait_send")
            for part in (0, 1):
                for side in (0, 1):
                    relay_copy(a, side, part).wait_send()
        pl.when(there(a))(sent)
    for k in range(1, n_lon):
        total_copy(k).wait_send()
    for b in (-1, 1):
        all_fields(lon_copy, b, "wait_send")

    def pole():
        last = pl.ds(low + rows - 8, 8)
        keep = jnp.broadcast_to(table[low + rows - 8:low + rows, C_KEEP:C_KEEP + 1], (8, wide))
        for f in (EE, EU, HN):
            ext[f, last, :] = keep * ext[f, last, :]
    pl.when(jnp.logical_not(there(1)))(pole)


def march(
    dims,
    ext, src, coef, lanes, zon_in,
    o_en, o_ee, o_eu, o_hn, o_he, o_hr, o_zon,
    buf, zon, zon_rows, done,
):
    n_lat, n_lon, layers, dt, ly = dims
    tall, wide = ext.shape[1:]
    rows, width = tall - 2 * HALO_ROWS, wide - 2 * HALO_LANES
    groups = tall // 8
    own_groups = range(HALO_ROWS // 8, groups - HALO_ROWS // 8)
    low = HALO_ROWS
    lat = lax.axis_index("lat")
    own_r = slice(low, low + rows)
    z_dec, z_drv, z_top, z_bot = [lanes.at[i, :, HALO_LANES:HALO_LANES + 128] for i in (0, 1, 2, 3)]
    zon[...] = zon_in[...]
    lane = lax.broadcasted_iota(jnp.int32, (rows, 128), 1)

    def record(s):
        both = jnp.where(lane < layers, zon[0, own_r, :], turn(zon[2, own_r, :], layers))
        both = jnp.transpose(both)
        zon_rows[s, 0] = both[0:layers]
        zon_rows[s, 1] = both[layers:2 * layers]

    def zonal_h():
        for g in range(1, groups - 1):
            r = 8 * g
            east = zon[0, r:r + 8, :]
            zon[2, r:r + 8, :] = (
                zon[2, r:r + 8, :]
                - coef[C_AS, r:r + 8] * zon[0, r - 1:r + 7, :]
                + coef[C_BE, r:r + 8] * east
            )
            zon[1, r:r + 8, :] = zon[1, r:r + 8, :] - coef[C_DT, r:r + 8] * (
                z_top[...] * turn(east, -1) - east
            )

    def zonal_e():
        for g in range(1, groups - 1):
            r = 8 * g
            up, north = zon[2, r:r + 8, :], zon[1, r:r + 8, :]
            zon[0, r:r + 8, :] = z_dec[...] * zon[0, r:r + 8, :] + z_drv[...] * (
                coef[C_LY, r:r + 8] * (zon[2, r + 1:r + 9, :] - up)
                - (north - z_bot[...] * turn(north, 1))
            )

    def magnetic(old, a, b, span, beyond):
        count = (b - a) // 128

        def rowc(c, g):
            return jnp.concatenate([coef[c, 8 * g:8 * g + 8]] * count, axis=1)

        top = lanes[2, :, a:b]
        for g in (*span, *beyond):
            r = 8 * g
            here, south = slice(r, r + 8), slice(r - 1, r + 7)
            e_n, e_e, e_u = old[EN, here, a:b], old[EE, here, a:b], old[EU, here, a:b]
            up = (
                old[HR, here, a:b]
                - rowc(C_AS, g) * old[EE, south, a:b]
                + rowc(C_BE, g) * e_e
                - rowc(C_CN, g) * (turn(e_n, -layers) - e_n)
            )
            if g in (own_groups[0], own_groups[-1]):
                row = lax.broadcasted_iota(jnp.int32, (8, b - a), 0) + (lat * rows - low + r)
                pole = 0 if g == own_groups[0] else n_lat * rows - 1
                up = jnp.where(row == pole, spread(zon[2, here], a // 128, count), up)
            buf[HR, here, a:b] = up
            buf[HE, here, a:b] = (
                old[HE, here, a:b]
                - (dt / ly) * (e_u - old[EU, south, a:b])
                + dt * (top * turn(e_n, -1) - e_n)
            )
            if g in span:
                buf[HN, here, a:b] = (
                    old[HN, here, a:b]
                    - rowc(C_DU, g) * (e_u - turn(e_u, -layers))
                    - rowc(C_DT, g) * (top * turn(e_e, -1) - e_e)
                )

    def electric(old, s, a, b, first, span):
        count = (b - first) // 128
        skip = first - a

        def rowc(c, g):
            return jnp.concatenate([coef[c, 8 * g:8 * g + 8]] * count, axis=1)

        def turned(x, by):
            return turn(x, by)[:, skip:]

        decay, drive, bot = [lanes[i, :, first:b] for i in (0, 1, 3)]
        for g in span:
            r = 8 * g
            here, north = slice(r, r + 8), slice(r + 1, r + 9)
            w_n, w_e, w_r = buf[HN, here, a:b], buf[HE, here, a:b], buf[HR, here, a:b]
            h_n, h_e, h_r = w_n[:, skip:], w_e[:, skip:], w_r[:, skip:]
            buf[EN, here, first:b] = decay * old[EN, here, first:b] + drive * (
                h_e - bot * turned(w_e, 1) - rowc(C_GC, g) * (h_r - turned(w_r, layers))
            )
            buf[EE, here, first:b] = decay * old[EE, here, first:b] + drive * (
                rowc(C_LY, g) * (buf[HR, north, first:b] - h_r) - (h_n - bot * turned(w_n, 1))
            )
            buf[EU, here, first:b] = (
                decay * old[EU, here, first:b]
                + drive
                * (
                    rowc(C_IC, g) * h_e
                    - rowc(C_JN, g) * buf[HE, north, first:b]
                    + rowc(C_KL, g) * (h_n - turned(w_n, layers))
                    + src[pl.ds(pl.multiple_of(s * (rows + 16) + r - 8, 8), 8), first:b]
                )
            )

    inner = range(1, groups - 1)

    def step(old, s, a, b, beyond):
        record(s)
        zonal_h()
        magnetic(old, a, b, inner, beyond)
        zonal_e()
        electric(old, s, a, b, a, inner)

    def steps(begin, end, a, b):
        def one_step(s, carry):
            step(buf, s, a, b, ())
            return carry
        lax.fori_loop(begin, end, one_step, 0)

    step(ext, 0, 0, wide, (groups - 1,))
    steps(1, 4, 0, wide)
    steps(4, STEPS - 1, 128, wide - 128)

    outs = {EN: o_en, EE: o_ee, EU: o_eu, HN: o_hn, HE: o_he, HR: o_hr}
    record(STEPS - 1)
    zonal_h()
    magnetic(buf, 128, wide - 128, own_groups, (own_groups[-1] + 1,))
    copies = [pltpu.make_async_copy(zon_rows, o_zon, done.at[6])]
    for f in (HN, HE, HR, EN, EE, EU):
        if f == EN:
            for copy in copies:
                copy.start()
            electric(buf, STEPS - 1, 128, wide - HALO_LANES, HALO_LANES, own_groups)
        copy = pltpu.make_async_copy(
            buf.at[f, pl.ds(low, rows), pl.ds(HALO_LANES, width)], outs[f], done.at[f]
        )
        if f <= EU:
            copy.start()
        copies.append(copy)
    for copy in copies:
        copy.wait()


def body(
    efield_north,
    efield_east,
    efield_up,
    hfield_north,
    hfield_east,
    hfield_up,
    sigma_profile,
    flash_lat,
    flash_lon,
    flash_step,
    flash_amp,
):
    rows, width = efield_north.shape
    layers = sigma_profile.shape[0]
    n_lat, n_lon = lax.axis_size("lat"), lax.axis_size("lon")
    lat_count, lon_count = rows * n_lat, (width // layers) * n_lon
    dims = (
        n_lat,
        n_lon,
        layers,
        time_step(lat_count, lon_count),
        RADIUS_CELLS * math.pi / lat_count,
    )
    wide, tall = width + 2 * HALO_LANES, rows + 2 * HALO_ROWS
    f32 = jnp.float32
    vmem = pl.BlockSpec(memory_space=pltpu.VMEM)
    dma = pltpu.SemaphoreType.DMA
    hbm = pl.BlockSpec(memory_space=pltpu.HBM)
    strokes = flash_lat.shape[0]
    middle = [
        jax.ShapeDtypeStruct(shape, f32)
        for shape in (
            (6, tall, wide), (STEPS * (rows + 16), wide), (10, tall, 128), (4, 8, wide), (3, tall, 128)
        )
    ]
    held = pl.pallas_call(
        functools.partial(exchange, dims),
        out_shape=middle,
        in_specs=[hbm] * 12,
        out_specs=[vmem] * 5,
        scratch_shapes=[
            pltpu.VMEM((n_lon, rows // n_lon, 128), f32),
            pltpu.VMEM((n_lon, rows // n_lon, 128), f32),
            pltpu.VMEM((n_lon, rows // n_lon, 128), f32),
            pltpu.VMEM((2, 8, 128), f32),
            pltpu.VMEM((rows, 128), f32),
            pltpu.VMEM((8, 128), f32),
            pltpu.VMEM((1, layers), f32),
            pltpu.VMEM((1, strokes), jnp.int32),
            pltpu.VMEM((1, strokes), jnp.int32),
            pltpu.VMEM((1, strokes), jnp.int32),
            pltpu.VMEM((1, strokes), f32),
            pltpu.VMEM((tall, 128), f32),
            pltpu.VMEM((2, 8, wide), f32),
            pltpu.VMEM((2, 8, wide), f32),
            dma((12,)),
            dma((12,)), dma((12,)), dma((12,)), dma((12,)), dma((8,)), dma((8,)),
            dma((n_lon,)), dma((n_lon,)), dma((n_lon,)), dma((n_lon,)), dma((2,)), dma((2,)), dma((2,)), dma((2,)),
            pltpu.SemaphoreType.REGULAR((n_lon,)), pltpu.SemaphoreType.REGULAR,
        ],
        compiler_params=pltpu.CompilerParams(
            collective_id=0, has_side_effects=True, vmem_limit_bytes=VMEM_GRANT
        ),
    )(*(pltpu.with_memory_space_constraint(x, pltpu.HBM) for x in (
        efield_north,
        efield_east,
        efield_up,
        hfield_north,
        hfield_east,
        hfield_up,
        sigma_profile[None, :],
        flash_lat[None, :],
        flash_lon[None, :],
        flash_step[None, :],
        flash_amp[None, :],
        jnp.asarray(row_table(lat_count, lon_count)),
    )))
    outs = [jax.ShapeDtypeStruct((rows, width), f32)] * 6
    outs += [jax.ShapeDtypeStruct((STEPS, 2, layers, rows), f32)]
    results = pl.pallas_call(
        functools.partial(march, dims),
        out_shape=outs,
        in_specs=[vmem] * 5,
        out_specs=[hbm] * 7,
        scratch_shapes=[
            pltpu.VMEM((6, tall, wide), f32),
            pltpu.VMEM((3, tall, 128), f32),
            pltpu.VMEM((STEPS, 2, layers, rows), f32),
            dma((7,)),
        ],
        compiler_params=pltpu.CompilerParams(vmem_limit_bytes=VMEM_GRANT),
    )(*held)
    return (*results[:6], jnp.transpose(results[6], (0, 1, 3, 2)))


def solution(mesh):
    fields = P("lat", "lon")
    return jax.shard_map(
        body,
        mesh=mesh,
        in_specs=(fields,) * 6 + (P(),) * 5,
        out_specs=(fields,) * 6 + (P(None, None, "lat", None),),
        check_vma=False,
    )
```

```python
import functools
import math

import jax
import jax.numpy as jnp
import numpy as np
from jax import lax
from jax.experimental import pallas as pl
from jax.experimental.pallas import tpu as pltpu
from jax.sharding import PartitionSpec as P

CHANNEL = 3
STEPS = 9
RADIUS_CELLS = 1529.0
COURANT = 0.9
VMEM_GRANT = 16 * 1024 * 1024

HALO_ROWS = 16
HALO_LANES = 256
MESH = pl.DeviceIdType.MESH
EN, EE, EU, HN, HE, HR = range(6)
(C_AS, C_BE, C_CN, C_DU, C_DT, C_GC, C_IC, C_JN, C_KL, C_LY) = range(10)
C_KEEP = 10


def time_step(lat_count, lon_count):
    lon_angle = 2.0 * math.pi / lon_count
    lat_angle = math.pi / lat_count
    narrowest = RADIUS_CELLS * lon_angle * math.sin(lat_angle)
    lat_length = RADIUS_CELLS * lat_angle
    return COURANT / math.sqrt(1.0 / narrowest**2 + 1.0 / lat_length**2 + 1.0)


def row_table(lat_count, lon_count):
    f = np.float32
    lon_angle = 2.0 * math.pi / lon_count
    lat_angle = math.pi / lat_count
    dt = time_step(lat_count, lon_count)
    ly = RADIUS_CELLS * math.pi / lat_count
    row = np.arange(lat_count)
    centre = f(-0.5 * math.pi) + (row.astype(f) + f(0.5)) * f(lat_angle)
    north = centre + f(0.5 * lat_angle)
    south = centre - f(0.5 * lat_angle)
    following = centre + f(lat_angle)
    pole = row == lat_count - 1
    scale = RADIUS_CELLS * lon_angle
    band = 2.0 * RADIUS_CELLS * scale * math.sin(0.5 * lat_angle)
    lc = f(scale) * np.cos(centre)
    ln = f(scale) * np.cos(following)
    le = np.where(pole, f(0), f(scale) * np.cos(north))
    ls = np.where(row == 0, f(0), f(scale) * np.cos(south))
    ls[-1] = le[-2]
    ac = f(band) * np.cos(centre)
    ae = np.where(pole, f(1), f(band) * np.cos(north))
    se = np.where(pole, f(1), le)
    keep = np.where(pole, f(0), f(1))
    table = np.zeros((lat_count + 2 * HALO_ROWS, 128), f)
    inner = table[HALO_ROWS:-HALO_ROWS]
    inner[:, C_AS] = dt * ls / ac
    inner[:, C_BE] = dt * le / ac
    inner[:, C_CN] = dt * ly / ac
    inner[:, C_DU] = keep * dt / se
    inner[:, C_DT] = keep * dt
    inner[:, C_GC] = 1.0 / lc
    inner[:, C_IC] = keep * lc / ae
    inner[:, C_JN] = keep * ln / ae
    inner[:, C_KL] = keep * ly / ae
    inner[:, C_LY] = keep / ly
    inner[:, C_KEEP] = keep
    return table


def turn(x, by):
    return pltpu.roll(x, by % x.shape[1], 1)


def div24(x):
    return lax.shift_right_logical(x * 2731, 16)


def spread(x, first, count):
    lane = lax.broadcasted_iota(jnp.int32, (8, 128), 1)
    out = []
    for v in range(first, first + count):
        off = (128 * v - HALO_LANES) % 24
        out.append(jnp.where(lane < 96, turn(x, -off), turn(x, 24 - off)))
    return jnp.concatenate(out, axis=1)


def kernel(
    dims,
    en, ee, eu, hn, he, hr, h_sigma, h_lat, h_lon, h_step, h_amp, h_table,
    o_en, o_ee, o_eu, o_hn, o_he, o_hr, o_zon,
    ext, buf, src, coef, lanes, zon,
    sums_out, sums_in, zone_in, strip, small, sigma, f_lat, f_lon, f_step, f_amp, table,
    load, send_b, recv_b, send_l, recv_l, send_c, recv_c, send_r, recv_r,
    send_s, recv_s, send_z, recv_z,
    ack_lon, ack_lat, ack_cross,
):
    n_lat, n_lon, layers, dt, ly = dims
    fields = (en, ee, eu, hn, he, hr)
    rows, width = en.shape
    strokes = h_lat.shape[1]
    wide = width + 2 * HALO_LANES
    tall = rows + 2 * HALO_ROWS
    vregs = wide // 128
    live = rows + 16
    low = HALO_ROWS
    lat, lon = lax.axis_index("lat"), lax.axis_index("lon")
    own_r = pl.ds(low, rows)
    own_c = pl.ds(HALO_LANES, width)

    def at(a, b):
        row = jnp.clip(lat + a, 0, n_lat - 1) if a else lat
        return {"lat": row, "lon": lax.rem(lon + b + n_lon, n_lon)}

    def there(a):
        return lat + a >= 0 if a < 0 else lat + a < n_lat

    def shared(a):
        return lax.rem(lat, 2) == (0 if a > 0 else 1)

    def across(a):
        return jnp.logical_and(there(a), jnp.logical_not(shared(a)))

    def signal(sem, a, b):
        pl.semaphore_signal(sem, inc=1, device_id=at(a, b), device_id_type=MESH)

    barrier = pltpu.get_barrier_semaphore()
    for k in range(1, n_lon):
        pl.when(lon + k < n_lon)(lambda k=k: signal(barrier, 0, k))
    pl.when(there(1))(lambda: signal(barrier, 1, 0))

    def crossing(a, b, later, act):
        wraps = lon == (n_lon - 1 if b > 0 else 0)
        is_later = jnp.logical_not(wraps) if b > 0 else wraps
        wanted = is_later if later else jnp.logical_not(is_later)
        pl.when(jnp.logical_and(across(a), wanted))(act)

    corners = [(a, b) for a in (-1, 1) for b in (-1, 1)]
    for a, b in corners:
        crossing(a, b, True, lambda a=a, b=b: signal(barrier, a, b))

    loads = [
        pltpu.make_async_copy(x, ext.at[f, own_r, own_c], load.at[f])
        for f, x in enumerate(fields)
    ]
    here_rows = h_table.at[pl.ds(pl.multiple_of(lat * rows, 8), tall), :]
    pairs = (
        (here_rows, table), (h_sigma, sigma), (h_lat, f_lat), (h_lon, f_lon),
        (h_step, f_step), (h_amp, f_amp),
    )
    loads += [pltpu.make_async_copy(x, y, load.at[6 + i]) for i, (x, y) in enumerate(pairs)]
    for copy in loads:
        copy.start()

    def lon_copy(b, f):
        i = f if b > 0 else 6 + f
        cut = pl.ds(width - HALO_LANES, HALO_LANES) if b > 0 else pl.ds(0, HALO_LANES)
        land = pl.ds(0, HALO_LANES) if b > 0 else pl.ds(HALO_LANES + width, HALO_LANES)
        return pltpu.make_async_remote_copy(
            src_ref=fields[f].at[:, cut],
            dst_ref=ext.at[f, own_r, land],
            send_sem=send_b.at[i],
            recv_sem=recv_b.at[i],
            device_id=at(0, b),
            device_id_type=MESH,
        )

    class Both:
        def __init__(self, a, cols, lands, these, sends, recvs, i, b=0):
            shift = rows if a > 0 else -rows
            self.copies = []
            for n, (row, count) in enumerate(
                ((low + rows - 8, 8), (low + rows - STEPS, 1))
                if a > 0
                else ((low, 8), (low + STEPS - 1, 1))
            ):
                self.copies.append(
                    pltpu.make_async_remote_copy(
                        src_ref=ext.at[these, pl.ds(row, count), cols],
                        dst_ref=ext.at[these, pl.ds(row - shift, count), lands],
                        send_sem=sends.at[2 * i + n],
                        recv_sem=recvs.at[2 * i + n],
                        device_id=at(a, b),
                        device_id_type=MESH,
                    )
                )

        def start(self):
            for copy in self.copies:
                copy.start()

        def wait_recv(self):
            for copy in self.copies:
                copy.wait_recv()

        def wait_send(self):
            for copy in self.copies:
                copy.wait_send()

    edge_copy = Both

    def lat_copy(a):
        return edge_copy(a, own_c, own_c, slice(None), send_l, recv_l, 0 if a > 0 else 1)

    def corner_copy(a, b):
        cols = pl.ds(width, HALO_LANES) if b > 0 else pl.ds(HALO_LANES, HALO_LANES)
        lands = pl.ds(0, HALO_LANES) if b > 0 else pl.ds(HALO_LANES + width, HALO_LANES)
        i = corners.index((a, b))
        return edge_copy(a, cols, lands, slice(None), send_c, recv_c, i, b)

    def relay_copy(a, side, part):
        cols = pl.ds(side * (HALO_LANES + width), HALO_LANES)
        i = part + 2 * side + (0 if a > 0 else 4)
        return edge_copy(a, cols, cols, pl.ds(3 * part, 3), send_r, recv_r, i)

    def sum_copy(k):
        return pltpu.make_async_remote_copy(
            src_ref=sums_out,
            dst_ref=sums_in.at[k],
            send_sem=send_s.at[k],
            recv_sem=recv_s.at[k],
            device_id=at(0, k),
            device_id_type=MESH,
        )

    def zone_copy(a):
        i = 0 if a > 0 else 1
        return pltpu.make_async_remote_copy(
            src_ref=strip.at[pl.ds(rows - 8, 8) if a > 0 else pl.ds(0, 8), :],
            dst_ref=zone_in.at[i],
            send_sem=send_z.at[i],
            recv_sem=recv_z.at[i],
            device_id=at(a, 0),
            device_id_type=MESH,
        )

    def all_fields(make, side, act):
        for f in range(6):
            getattr(make(side, f), act)()

    crossed = jnp.where(lon == n_lon - 1, 2, jnp.where(lon == 0, 0, 1))
    crossed = jnp.where(jnp.logical_or(across(-1), across(1)), crossed, 0)
    earlier = lon + (lat > 0).astype(jnp.int32) + crossed
    pl.when(earlier > 0)(lambda: pl.semaphore_wait(barrier, earlier))
    for k in range(n_lon - 1, 0, -1):
        pl.when(lon - k >= 0)(lambda k=k: signal(ack_lon.at[k], 0, -k))
    pl.when(there(-1))(lambda: signal(ack_lat, -1, 0))
    for a, b in corners:
        crossing(a, b, False, lambda a=a, b=b: signal(ack_cross.at[0 if b < 0 else 1], a, b))

    pl.when(lon == n_lon - 1)(lambda: all_fields(lon_copy, 1, "start"))
    pl.when(lon > 0)(lambda: all_fields(lon_copy, -1, "start"))

    for a, first in ((-1, 0), (1, low + rows)):
        def clear(first=first):
            ext[:, first:first + low, :] = jnp.zeros((6, low, wide), jnp.float32)
        pl.when(jnp.logical_not(there(a)))(clear)

    for copy in loads[:7]:
        copy.wait()

    pl.when(there(-1))(lambda: lat_copy(-1).start())
    for a, b in corners:
        crossing(a, b, False, lambda a=a, b=b: corner_copy(a, b).start())

    def fold(x):
        for by in (width // 2, width // 4, width // 8, width // 16):
            x = x + turn(x, by)
        return x[:, :128] * (1.0 / (n_lon * (width // layers)))

    lane = lax.broadcasted_iota(jnp.int32, (rows, 128), 1)
    kept = jnp.broadcast_to(table[low:low + rows, C_KEEP:C_KEEP + 1], (rows, 128))
    sums_out[...] = jnp.where(
        lane < layers,
        kept * fold(ext[EE, own_r, own_c]),
        jnp.where(
            lane < 2 * layers, kept * fold(ext[HN, own_r, own_c]), fold(ext[HR, own_r, own_c])
        ),
    )
    for k in range(1, n_lon):
        pl.when(lon + k >= n_lon)(lambda k=k: sum_copy(k).start())

    def to_north():
        pl.semaphore_wait(ack_lat, 1)
        lat_copy(1).start()
    pl.when(there(1))(to_north)

    def serve(k):
        def to_later():
            pl.semaphore_wait(ack_lon.at[k], 1)
            if k == 1:
                all_fields(lon_copy, 1, "start")
            if k == n_lon - 1:
                all_fields(lon_copy, -1, "start")
            sum_copy(k).start()
        pl.when(lon + k < n_lon)(to_later)

    serve(1)
    for a, b in corners:
        if b > 0:
            def corner_later(a=a, b=b):
                pl.semaphore_wait(ack_cross.at[0], 1)
                corner_copy(a, b).start()
            crossing(a, b, True, corner_later)
    for copy in loads[7:]:
        copy.wait()
    rows_tab = table[...]
    for c in range(10):
        coef[c] = jnp.broadcast_to(rows_tab[:, c:c + 1], (tall, 128))
    small[...] = jnp.zeros((8, 128), jnp.float32)
    small[0:1, 0:layers] = sigma[...]
    one = jnp.broadcast_to(small[0:1, :], (8, 128))
    pair = one + turn(one, 24)
    sig = pair + turn(pair, 48) + turn(one, 96)
    half = 0.5 * dt * sig
    dec = (1.0 - half) / (1.0 + half)
    drv = dt / (1.0 + half)

    at_lane = lax.broadcasted_iota(jnp.int32, (8, wide), 1) + 8
    layer = at_lane - 24 * div24(at_lane)
    lanes[0] = spread(dec, 0, vregs)
    lanes[1] = spread(drv, 0, vregs)
    lanes[2] = jnp.where(layer == layers - 1, 0.0, 1.0)
    lanes[3] = jnp.where(layer == 0, 0.0, 1.0)

    half_lanes = lax.broadcasted_iota(jnp.int32, (1, 128), 1) < strokes

    def twice(x):
        return jnp.concatenate([x, x], axis=1)

    def column(x):
        return jnp.transpose(jnp.broadcast_to(x.astype(jnp.float32), (128, 2 * strokes)))

    cell = div24(at_lane[0:1]) - 11 + lon * (width // layers)
    total_lon = n_lon * (width // layers)
    cell = jnp.where(cell < 0, cell + total_lon, cell)
    cell = jnp.where(cell >= total_lon, cell - total_lon, cell)
    cell = jnp.where(layer[0:1] < CHANNEL, cell, -1).astype(jnp.float32)
    lon_of = jnp.concatenate([column(twice(f_lon[...]))] * vregs, axis=1)
    cells = (jnp.broadcast_to(cell, (2 * strokes, wide)) == lon_of).astype(jnp.float32)
    cells = cells.astype(jnp.bfloat16)
    row_no = lax.broadcasted_iota(jnp.int32, (live, 2 * strokes), 0) + (lat * rows - 8)
    in_row = jnp.where(
        row_no == twice(f_lat[...]),
        jnp.broadcast_to(twice(f_amp[...]), (live, 2 * strokes)),
        0.0,
    )
    steps_of = twice(f_step[...])
    left, right = [], []
    for s in range(STEPS):
        amps = jnp.where(steps_of == s, in_row, 0.0)
        upper = amps.astype(jnp.bfloat16).astype(jnp.float32)
        middle = (amps - upper).astype(jnp.bfloat16).astype(jnp.float32)
        left.append(jnp.where(half_lanes, upper, middle).astype(jnp.bfloat16))
        right.append(jnp.where(half_lanes, amps - upper - middle, 0.0).astype(jnp.bfloat16))
    total = None
    for part in (left, right):
        term = lax.dot_general(
            jnp.concatenate(part, axis=0), cells, (((1,), (0,)), ((), ())),
            preferred_element_type=jnp.float32,
        )
        total = term if total is None else total + term
    src[...] = total

    for k in range(2, n_lon):
        serve(k)
    for a, b in corners:
        if b < 0:
            def corner_last(a=a, b=b):
                pl.semaphore_wait(ack_cross.at[1], 1)
                corner_copy(a, b).start()
            crossing(a, b, True, corner_last)

    for k in range(1, n_lon):
        sum_copy(k).wait_recv()
    mean = sums_out[...]
    for k in range(1, n_lon):
        mean = mean + sums_in[k]
    strip[...] = mean
    for a in (-1, 1):
        pl.when(there(a))(lambda a=a: zone_copy(a).start())

    def unpack(x):
        out = []
        lane_no = lax.broadcasted_iota(jnp.int32, x.shape, 1)
        for f in range(3):
            y = jnp.where(lane_no < layers, turn(x, -layers * f), 0.0)
            p = y + turn(y, 24)
            out.append(p + turn(p, 48) + turn(y, 96))
        return out

    zon[:, 0:low, :] = jnp.zeros((3, low, 128), jnp.float32)
    zon[:, low + rows:, :] = jnp.zeros((3, low, 128), jnp.float32)
    for f, z in enumerate(unpack(mean)):
        zon[f, own_r, :] = z

    for part in (0, 1):
        for side in (0, 1):
            for f in range(3 * part, 3 * part + 3):
                lon_copy(1 if side == 0 else -1, f).wait_recv()
            for a in (-1, 1):
                pl.when(shared(a))(
                    lambda a=a, side=side, part=part: relay_copy(a, side, part).start()
                )

    for a in (-1, 1):
        def take(a=a):
            zone_copy(a).wait_recv()
            if a > 0:
                for f, z in enumerate(unpack(zone_in[0])):
                    zon[f, low - 8:low, :] = z
            else:
                for f, z in enumerate(unpack(zone_in[1])):
                    zon[f, low + rows:low + rows + 8, :] = z
            lat_copy(a).wait_recv()
        pl.when(there(-a))(take)

        def take_corners(a=a):
            for b in (-1, 1):
                corner_copy(a, b).wait_recv()
        pl.when(across(-a))(take_corners)

        def take_relays(a=a):
            for part in (0, 1):
                for side in (0, 1):
                    relay_copy(a, side, part).wait_recv()
        pl.when(shared(-a))(take_relays)

    def pole():
        last = pl.ds(low + rows - 8, 8)
        keep = jnp.broadcast_to(table[low + rows - 8:low + rows, C_KEEP:C_KEEP + 1], (8, wide))
        for f in (EE, EU, HN):
            ext[f, last, :] = keep * ext[f, last, :]
    pl.when(jnp.logical_not(there(1)))(pole)

    march(dims, ext, buf, src, coef, lanes, zon, (o_en, o_ee, o_eu, o_hn, o_he, o_hr), o_zon)

    for a in (-1, 1):
        def sent(a=a):
            zone_copy(a).wait_send()
            lat_copy(a).wait_send()
        pl.when(there(a))(sent)

        def sent_corners(a=a):
            for b in (-1, 1):
                corner_copy(a, b).wait_send()
        pl.when(across(a))(sent_corners)

        def sent_relays(a=a):
            for part in (0, 1):
                for side in (0, 1):
                    relay_copy(a, side, part).wait_send()
        pl.when(shared(a))(sent_relays)
    for k in range(1, n_lon):
        sum_copy(k).wait_send()
    for b in (-1, 1):
        all_fields(lon_copy, b, "wait_send")


def march(dims, ext, buf, src, coef, lanes, zon, outs, o_zon):
    n_lat, n_lon, layers, dt, ly = dims
    tall, wide = buf.shape[1:]
    rows, width = tall - 2 * HALO_ROWS, wide - 2 * HALO_LANES
    groups = tall // 8
    own_groups = range(HALO_ROWS // 8, groups - HALO_ROWS // 8)
    low = HALO_ROWS
    lat = lax.axis_index("lat")
    own_r = slice(low, low + rows)
    z_dec, z_drv, z_top, z_bot = [lanes.at[i, :, HALO_LANES:HALO_LANES + 128] for i in (0, 1, 2, 3)]
    lane = lax.broadcasted_iota(jnp.int32, (rows, 128), 1)

    def record(s):
        both = jnp.where(lane < layers, zon[0, own_r, :], turn(zon[2, own_r, :], layers))
        both = jnp.transpose(both)
        o_zon[s, 0] = both[0:layers]
        o_zon[s, 1] = both[layers:2 * layers]

    def zonal_h():
        for g in range(1, groups - 1):
            r = 8 * g
            east = zon[0, r:r + 8, :]
            zon[2, r:r + 8, :] = (
                zon[2, r:r + 8, :]
                - coef[C_AS, r:r + 8] * zon[0, r - 1:r + 7, :]
                + coef[C_BE, r:r + 8] * east
            )
            zon[1, r:r + 8, :] = zon[1, r:r + 8, :] - coef[C_DT, r:r + 8] * (
                z_top[...] * turn(east, -1) - east
            )

    def zonal_e():
        for g in range(1, groups - 1):
            r = 8 * g
            up, north = zon[2, r:r + 8, :], zon[1, r:r + 8, :]
            zon[0, r:r + 8, :] = z_dec[...] * zon[0, r:r + 8, :] + z_drv[...] * (
                coef[C_LY, r:r + 8] * (zon[2, r + 1:r + 9, :] - up)
                - (north - z_bot[...] * turn(north, 1))
            )

    def magnetic(old, a, b, span, beyond, last=False):
        count = (b - a) // 128

        def rowc(c, g):
            return jnp.concatenate([coef[c, 8 * g:8 * g + 8]] * count, axis=1)

        top = lanes[2, :, a:b]
        for g in (*span, *beyond):
            r = 8 * g
            here, south = slice(r, r + 8), slice(r - 1, r + 7)
            e_n, e_e, e_u = old[EN, here, a:b], old[EE, here, a:b], old[EU, here, a:b]
            up = (
                old[HR, here, a:b]
                - rowc(C_AS, g) * old[EE, south, a:b]
                + rowc(C_BE, g) * e_e
                - rowc(C_CN, g) * (turn(e_n, -layers) - e_n)
            )
            if g in (own_groups[0], own_groups[-1]):
                row = lax.broadcasted_iota(jnp.int32, (8, b - a), 0) + (lat * rows - low + r)
                pole = 0 if g == own_groups[0] else n_lat * rows - 1
                up = jnp.where(row == pole, spread(zon[2, here], a // 128, count), up)
            fresh = {HR: up}
            fresh[HE] = (
                old[HE, here, a:b]
                - (dt / ly) * (e_u - old[EU, south, a:b])
                + dt * (top * turn(e_n, -1) - e_n)
            )
            if g in span:
                fresh[HN] = (
                    old[HN, here, a:b]
                    - rowc(C_DU, g) * (e_u - turn(e_u, -layers))
                    - rowc(C_DT, g) * (top * turn(e_e, -1) - e_e)
                )
            for f, x in fresh.items():
                buf[f, here, a:b] = x
                if last and g in span:
                    outs[f][r - low:r - low + 8, :] = x[:, HALO_LANES - a:HALO_LANES - a + width]

    def electric(old, s, a, b, first, span, last=False):
        count = (b - first) // 128
        skip = first - a

        def rowc(c, g):
            return jnp.concatenate([coef[c, 8 * g:8 * g + 8]] * count, axis=1)

        def turned(x, by):
            return turn(x, by)[:, skip:]

        decay, drive, bot = [lanes[i, :, first:b] for i in (0, 1, 3)]
        for g in span:
            r = 8 * g
            here, north = slice(r, r + 8), slice(r + 1, r + 9)
            w_n, w_e, w_r = buf[HN, here, a:b], buf[HE, here, a:b], buf[HR, here, a:b]
            h_n, h_e, h_r = w_n[:, skip:], w_e[:, skip:], w_r[:, skip:]
            fresh = {}
            fresh[EN] = decay * old[EN, here, first:b] + drive * (
                h_e - bot * turned(w_e, 1) - rowc(C_GC, g) * (h_r - turned(w_r, layers))
            )
            fresh[EE] = decay * old[EE, here, first:b] + drive * (
                rowc(C_LY, g) * (buf[HR, north, first:b] - h_r) - (h_n - bot * turned(w_n, 1))
            )
            fresh[EU] = (
                decay * old[EU, here, first:b]
                + drive
                * (
                    rowc(C_IC, g) * h_e
                    - rowc(C_JN, g) * buf[HE, north, first:b]
                    + rowc(C_KL, g) * (h_n - turned(w_n, layers))
                    + src[pl.ds(pl.multiple_of(s * (rows + 16) + r - 8, 8), 8), first:b]
                )
            )

            for f, x in fresh.items():
                if last:
                    outs[f][r - low:r - low + 8, :] = x
                else:
                    buf[f, here, first:b] = x

    inner = range(1, groups - 1)

    def step(old, s, a, b, beyond):
        record(s)
        zonal_h()
        magnetic(old, a, b, inner, beyond)
        zonal_e()
        electric(old, s, a, b, a, inner)

    def steps(begin, end, a, b):
        def one_step(s, carry):
            step(buf, s, a, b, ())
            return carry
        lax.fori_loop(begin, end, one_step, 0)

    step(ext, 0, 0, wide, (groups - 1,))
    steps(1, 4, 0, wide)
    steps(4, STEPS - 1, 128, wide - 128)
    record(STEPS - 1)
    zonal_h()
    magnetic(buf, 128, wide - 128, own_groups, (own_groups[-1] + 1,), last=True)
    electric(buf, STEPS - 1, 128, wide - HALO_LANES, HALO_LANES, own_groups, last=True)


def hand_over(*refs):
    count = len(refs) // 2
    copies = [
        pltpu.make_async_copy(refs[i], refs[count + i], refs[-1].at[i]) for i in range(count)
    ]
    for copy in copies:
        copy.start()
    for copy in copies:
        copy.wait()


def body(
    efield_north,
    efield_east,
    efield_up,
    hfield_north,
    hfield_east,
    hfield_up,
    sigma_profile,
    flash_lat,
    flash_lon,
    flash_step,
    flash_amp,
):
    rows, width = efield_north.shape
    layers = sigma_profile.shape[0]
    n_lat, n_lon = lax.axis_size("lat"), lax.axis_size("lon")
    lat_count, lon_count = rows * n_lat, (width // layers) * n_lon
    dims = (
        n_lat,
        n_lon,
        layers,
        time_step(lat_count, lon_count),
        RADIUS_CELLS * math.pi / lat_count,
    )
    wide, tall = width + 2 * HALO_LANES, rows + 2 * HALO_ROWS
    f32 = jnp.float32
    vmem = pl.BlockSpec(memory_space=pltpu.VMEM)
    dma = pltpu.SemaphoreType.DMA
    hbm = pl.BlockSpec(memory_space=pltpu.HBM)
    strokes = flash_lat.shape[0]
    n_live = rows + 16
    outs = [jax.ShapeDtypeStruct((rows, width), f32)] * 6
    outs += [jax.ShapeDtypeStruct((STEPS, 2, layers, rows), f32)]
    held = pl.pallas_call(
        functools.partial(kernel, dims),
        out_shape=outs,
        in_specs=[hbm] * 12,
        out_specs=[vmem] * 7,
        scratch_shapes=[
            pltpu.VMEM((6, tall, wide), f32),
            pltpu.VMEM((6, tall, wide), f32),
            pltpu.VMEM((STEPS * n_live, wide), f32),
            pltpu.VMEM((10, tall, 128), f32),
            pltpu.VMEM((4, 8, wide), f32),
            pltpu.VMEM((3, tall, 128), f32),
            pltpu.VMEM((rows, 128), f32),
            pltpu.VMEM((n_lon, rows, 128), f32),
            pltpu.VMEM((2, 8, 128), f32),
            pltpu.VMEM((rows, 128), f32),
            pltpu.VMEM((8, 128), f32),
            pltpu.VMEM((1, layers), f32),
            pltpu.VMEM((1, strokes), jnp.int32),
            pltpu.VMEM((1, strokes), jnp.int32),
            pltpu.VMEM((1, strokes), jnp.int32),
            pltpu.VMEM((1, strokes), f32),
            pltpu.VMEM((tall, 128), f32),
            dma((12,)),
            dma((12,)), dma((12,)), dma((4,)), dma((4,)), dma((8,)), dma((8,)),
            dma((16,)), dma((16,)),
            dma((n_lon,)), dma((n_lon,)), dma((2,)), dma((2,)),
            pltpu.SemaphoreType.REGULAR((n_lon,)),
            pltpu.SemaphoreType.REGULAR,
            pltpu.SemaphoreType.REGULAR((2,)),
        ],
        compiler_params=pltpu.CompilerParams(
            collective_id=0, has_side_effects=True, vmem_limit_bytes=VMEM_GRANT
        ),
    )(*(pltpu.with_memory_space_constraint(x, pltpu.HBM) for x in (
        efield_north,
        efield_east,
        efield_up,
        hfield_north,
        hfield_east,
        hfield_up,
        sigma_profile[None, :],
        flash_lat[None, :],
        flash_lon[None, :],
        flash_step[None, :],
        flash_amp[None, :],
        jnp.asarray(row_table(lat_count, lon_count)),
    )))
    results = pl.pallas_call(
        hand_over,
        out_shape=outs,
        in_specs=[vmem] * 7,
        out_specs=[hbm] * 7,
        scratch_shapes=[dma((7,))],
        compiler_params=pltpu.CompilerParams(vmem_limit_bytes=VMEM_GRANT),
    )(*held)
    return (*results[:6], jnp.transpose(results[6], (0, 1, 3, 2)))


def solution(mesh):
    fields = P("lat", "lon")
    return jax.shard_map(
        body,
        mesh=mesh,
        in_specs=(fields,) * 6 + (P(),) * 5,
        out_specs=(fields,) * 6 + (P(None, None, "lat", None),),
        check_vma=False,
    )
```

```python
import functools
import math

import jax
import jax.numpy as jnp
import numpy as np
from jax import lax
from jax.experimental import pallas as pl
from jax.experimental.pallas import tpu as pltpu
from jax.sharding import PartitionSpec as P

CHANNEL = 3
STEPS = 9
RADIUS_CELLS = 1529.0
COURANT = 0.9
VMEM_GRANT = 16 * 1024 * 1024

HALO_ROWS = 16
HALO_LANES = 256
MESH = pl.DeviceIdType.MESH
EN, EE, EU, HN, HE, HR = range(6)
(C_AS, C_BE, C_CN, C_DU, C_DT, C_GC, C_IC, C_JN, C_KL, C_LY) = range(10)
C_KEEP = 10


def time_step(lat_count, lon_count):
    lon_angle = 2.0 * math.pi / lon_count
    lat_angle = math.pi / lat_count
    narrowest = RADIUS_CELLS * lon_angle * math.sin(lat_angle)
    lat_length = RADIUS_CELLS * lat_angle
    return COURANT / math.sqrt(1.0 / narrowest**2 + 1.0 / lat_length**2 + 1.0)


def row_table(lat_count, lon_count):
    f = np.float32
    lon_angle = 2.0 * math.pi / lon_count
    lat_angle = math.pi / lat_count
    dt = time_step(lat_count, lon_count)
    ly = RADIUS_CELLS * math.pi / lat_count
    row = np.arange(lat_count)
    centre = f(-0.5 * math.pi) + (row.astype(f) + f(0.5)) * f(lat_angle)
    north = centre + f(0.5 * lat_angle)
    south = centre - f(0.5 * lat_angle)
    following = centre + f(lat_angle)
    pole = row == lat_count - 1
    scale = RADIUS_CELLS * lon_angle
    band = 2.0 * RADIUS_CELLS * scale * math.sin(0.5 * lat_angle)
    lc = f(scale) * np.cos(centre)
    ln = f(scale) * np.cos(following)
    le = np.where(pole, f(0), f(scale) * np.cos(north))
    ls = np.where(row == 0, f(0), f(scale) * np.cos(south))
    ls[-1] = le[-2]
    ac = f(band) * np.cos(centre)
    ae = np.where(pole, f(1), f(band) * np.cos(north))
    se = np.where(pole, f(1), le)
    keep = np.where(pole, f(0), f(1))
    table = np.zeros((lat_count + 2 * HALO_ROWS, 128), f)
    inner = table[HALO_ROWS:-HALO_ROWS]
    inner[:, C_AS] = dt * ls / ac
    inner[:, C_BE] = dt * le / ac
    inner[:, C_CN] = dt * ly / ac
    inner[:, C_DU] = keep * dt / se
    inner[:, C_DT] = keep * dt
    inner[:, C_GC] = 1.0 / lc
    inner[:, C_IC] = keep * lc / ae
    inner[:, C_JN] = keep * ln / ae
    inner[:, C_KL] = keep * ly / ae
    inner[:, C_LY] = keep / ly
    inner[:, C_KEEP] = keep
    return table


def turn(x, by):
    return pltpu.roll(x, by % x.shape[1], 1)


def div24(x):
    return lax.shift_right_logical(x * 2731, 16)


def spread(x, first, count):
    lane = lax.broadcasted_iota(jnp.int32, (8, 128), 1)
    out = []
    for v in range(first, first + count):
        off = (128 * v - HALO_LANES) % 24
        out.append(jnp.where(lane < 96, turn(x, -off), turn(x, 24 - off)))
    return jnp.concatenate(out, axis=1)


def kernel(
    dims,
    en, ee, eu, hn, he, hr, h_sigma, h_lat, h_lon, h_step, h_amp, h_table,
    o_en, o_ee, o_eu, o_hn, o_he, o_hr, o_zon,
    ext, buf, src, coef, lanes, zon, zon_cap,
    sums_out, sums_in, zone_in, strip, small, sigma, f_lat, f_lon, f_step, f_amp, table,
    load, send_b, recv_b, send_l, recv_l, send_c, recv_c, send_r, recv_r,
    send_s, recv_s, send_z, recv_z,
    ack_lon, ack_lat, ack_cross,
):
    n_lat, n_lon, layers, dt, ly = dims
    fields = (en, ee, eu, hn, he, hr)
    rows, width = en.shape
    strokes = h_lat.shape[1]
    wide = width + 2 * HALO_LANES
    tall = rows + 2 * HALO_ROWS
    vregs = wide // 128
    live = rows + 16
    low = HALO_ROWS
    lat, lon = lax.axis_index("lat"), lax.axis_index("lon")
    own_r = pl.ds(low, rows)
    own_c = pl.ds(HALO_LANES, width)

    def at(a, b):
        row = jnp.clip(lat + a, 0, n_lat - 1) if a else lat
        return {"lat": row, "lon": lax.rem(lon + b + n_lon, n_lon)}

    def there(a):
        return lat + a >= 0 if a < 0 else lat + a < n_lat

    def shared(a):
        return lax.rem(lat, 2) == (0 if a > 0 else 1)

    def across(a):
        return jnp.logical_and(there(a), jnp.logical_not(shared(a)))

    def signal(sem, a, b):
        pl.semaphore_signal(sem, inc=1, device_id=at(a, b), device_id_type=MESH)

    barrier = pltpu.get_barrier_semaphore()
    for k in range(1, n_lon):
        pl.when(lon + k < n_lon)(lambda k=k: signal(barrier, 0, k))
    pl.when(there(1))(lambda: signal(barrier, 1, 0))

    def crossing(a, b, later, act):
        wraps = lon == (n_lon - 1 if b > 0 else 0)
        is_later = jnp.logical_not(wraps) if b > 0 else wraps
        wanted = is_later if later else jnp.logical_not(is_later)
        pl.when(jnp.logical_and(across(a), wanted))(act)

    corners = [(a, b) for a in (-1, 1) for b in (-1, 1)]
    for a, b in corners:
        crossing(a, b, True, lambda a=a, b=b: signal(barrier, a, b))

    loads = [
        pltpu.make_async_copy(x, ext.at[f, own_r, own_c], load.at[f])
        for f, x in enumerate(fields)
    ]
    here_rows = h_table.at[pl.ds(pl.multiple_of(lat * rows, 8), tall), :]
    pairs = (
        (here_rows, table), (h_sigma, sigma), (h_lat, f_lat), (h_lon, f_lon),
        (h_step, f_step), (h_amp, f_amp),
    )
    loads += [pltpu.make_async_copy(x, y, load.at[6 + i]) for i, (x, y) in enumerate(pairs)]
    for copy in loads:
        copy.start()

    def lon_copy(b, f):
        i = f if b > 0 else 6 + f
        cut = pl.ds(width - HALO_LANES, HALO_LANES) if b > 0 else pl.ds(0, HALO_LANES)
        land = pl.ds(0, HALO_LANES) if b > 0 else pl.ds(HALO_LANES + width, HALO_LANES)
        return pltpu.make_async_remote_copy(
            src_ref=fields[f].at[:, cut],
            dst_ref=ext.at[f, own_r, land],
            send_sem=send_b.at[i],
            recv_sem=recv_b.at[i],
            device_id=at(0, b),
            device_id_type=MESH,
        )

    class Pieces:
        def __init__(self, a, parts, these, sends, recvs, i, b=0):
            shift = rows if a > 0 else -rows
            self.copies = [
                pltpu.make_async_remote_copy(
                    src_ref=ext.at[these, pl.ds(row, count), pl.ds(col, span)],
                    dst_ref=ext.at[these, pl.ds(row - shift, count), pl.ds(land, span)],
                    send_sem=sends.at[2 * i + n],
                    recv_sem=recvs.at[2 * i + n],
                    device_id=at(a, b),
                    device_id_type=MESH,
                )
                for n, (row, count, col, land, span) in enumerate(parts)
            ]

        def start(self):
            for copy in self.copies:
                copy.start()

        def wait_recv(self):
            for copy in self.copies:
                copy.wait_recv()

        def wait_send(self):
            for copy in self.copies:
                copy.wait_send()

    def nine(a, col, land, span):
        first, ninth = (low + rows - 8, low + rows - STEPS) if a > 0 else (low, low + STEPS - 1)
        return (first, 8, col, land, span), (ninth, 1, col, land, span)

    def lat_copy(a):
        parts = nine(a, HALO_LANES, HALO_LANES, width)
        return Pieces(a, parts, slice(None), send_l, recv_l, 0 if a > 0 else 1)

    def corner_copy(a, b):
        col, land = (width, 0) if b > 0 else (HALO_LANES, HALO_LANES + width)
        if a == b:
            parts = nine(a, col, land, HALO_LANES)
        else:
            near, far = (128, 0) if b > 0 else (0, 128)
            row = low + rows - 8 if a > 0 else low
            close = low + rows - 4 if a > 0 else low
            parts = (
                (row, 8, col + near, land + near, 128),
                (close, 4, col + far, land + far, 128),
            )
        return Pieces(a, parts, slice(None), send_c, recv_c, corners.index((a, b)), b)

    def relay_copy(a, side, part):
        col = side * (HALO_LANES + width)
        i = part + 2 * side + (0 if a > 0 else 4)
        return Pieces(a, nine(a, col, col, HALO_LANES), pl.ds(3 * part, 3), send_r, recv_r, i)

    def sum_copy(k):
        return pltpu.make_async_remote_copy(
            src_ref=sums_out,
            dst_ref=sums_in.at[k],
            send_sem=send_s.at[k],
            recv_sem=recv_s.at[k],
            device_id=at(0, k),
            device_id_type=MESH,
        )

    def zone_copy(a):
        i = 0 if a > 0 else 1
        return pltpu.make_async_remote_copy(
            src_ref=strip,
            dst_ref=zone_in.at[i],
            send_sem=send_z.at[i],
            recv_sem=recv_z.at[i],
            device_id=at(a, 0),
            device_id_type=MESH,
        )

    def all_fields(make, side, act):
        for f in range(6):
            getattr(make(side, f), act)()

    crossed = jnp.where(lon == n_lon - 1, 2, jnp.where(lon == 0, 0, 1))
    crossed = jnp.where(jnp.logical_or(across(-1), across(1)), crossed, 0)
    earlier = lon + (lat > 0).astype(jnp.int32) + crossed
    pl.when(earlier > 0)(lambda: pl.semaphore_wait(barrier, earlier))
    for k in range(n_lon - 1, 0, -1):
        pl.when(lon - k >= 0)(lambda k=k: signal(ack_lon.at[k], 0, -k))
    pl.when(there(-1))(lambda: signal(ack_lat, -1, 0))
    for a, b in corners:
        crossing(a, b, False, lambda a=a, b=b: signal(ack_cross.at[0 if b < 0 else 1], a, b))

    pl.when(lon == n_lon - 1)(lambda: all_fields(lon_copy, 1, "start"))
    pl.when(lon > 0)(lambda: all_fields(lon_copy, -1, "start"))

    for a, first in ((-1, 0), (1, low + rows)):
        def clear(first=first):
            ext[:, first:first + low, :] = jnp.zeros((6, low, wide), jnp.float32)
        pl.when(jnp.logical_not(there(a)))(clear)

    for copy in loads[:7]:
        copy.wait()

    pl.when(there(-1))(lambda: lat_copy(-1).start())
    for a, b in corners:
        crossing(a, b, False, lambda a=a, b=b: corner_copy(a, b).start())

    def fold(x):
        for by in (width // 2, width // 4, width // 8, width // 16):
            x = x + turn(x, by)
        return x[:, :128] * (1.0 / (n_lon * (width // layers)))

    lane = lax.broadcasted_iota(jnp.int32, (8, 128), 1)
    kept = jnp.broadcast_to(table[low:low + rows, C_KEEP:C_KEEP + 1], (rows, 128))
    bands = rows // 8
    for n, f in enumerate((EE, HN, HR)):
        folded = fold(ext[f, own_r, own_c])
        if f != HR:
            folded = kept * folded
        packed = folded[0:8]
        for band in range(1, bands):
            packed = jnp.where(lane < layers * band, packed, folded[8 * band:8 * band + 8])
        sums_out[8 * n:8 * n + 8, :] = packed
    for k in range(1, n_lon):
        pl.when(lon + k >= n_lon)(lambda k=k: sum_copy(k).start())

    def to_north():
        pl.semaphore_wait(ack_lat, 1)
        lat_copy(1).start()
    pl.when(there(1))(to_north)

    def serve(k):
        def to_later():
            pl.semaphore_wait(ack_lon.at[k], 1)
            if k == 1:
                all_fields(lon_copy, 1, "start")
            if k == n_lon - 1:
                all_fields(lon_copy, -1, "start")
            sum_copy(k).start()
        pl.when(lon + k < n_lon)(to_later)

    serve(1)
    for a, b in corners:
        if b > 0:
            def corner_later(a=a, b=b):
                pl.semaphore_wait(ack_cross.at[0], 1)
                corner_copy(a, b).start()
            crossing(a, b, True, corner_later)
    for copy in loads[7:]:
        copy.wait()
    rows_tab = table[...]
    for c in range(10):
        coef[c] = jnp.broadcast_to(rows_tab[:, c:c + 1], (tall, 128))
    small[...] = jnp.zeros((8, 128), jnp.float32)
    small[0:1, 0:layers] = sigma[...]
    one = jnp.broadcast_to(small[0:1, :], (8, 128))
    pair = one + turn(one, 24)
    sig = pair + turn(pair, 48) + turn(one, 96)
    half = 0.5 * dt * sig
    dec = (1.0 - half) / (1.0 + half)
    drv = dt / (1.0 + half)

    at_lane = lax.broadcasted_iota(jnp.int32, (8, wide), 1) + 8
    layer = at_lane - 24 * div24(at_lane)
    lanes[0] = spread(dec, 0, vregs)
    lanes[1] = spread(drv, 0, vregs)
    lanes[2] = jnp.where(layer == layers - 1, 0.0, 1.0)
    lanes[3] = jnp.where(layer == 0, 0.0, 1.0)

    half_lanes = lax.broadcasted_iota(jnp.int32, (1, 128), 1) < strokes

    def twice(x):
        return jnp.concatenate([x, x], axis=1)

    def column(x):
        return jnp.transpose(jnp.broadcast_to(x.astype(jnp.float32), (128, 2 * strokes)))

    cell = div24(at_lane[0:1]) - 11 + lon * (width // layers)
    total_lon = n_lon * (width // layers)
    cell = jnp.where(cell < 0, cell + total_lon, cell)
    cell = jnp.where(cell >= total_lon, cell - total_lon, cell)
    cell = jnp.where(layer[0:1] < CHANNEL, cell, -1).astype(jnp.float32)
    lon_of = jnp.concatenate([column(twice(f_lon[...]))] * vregs, axis=1)
    cells = (jnp.broadcast_to(cell, (2 * strokes, wide)) == lon_of).astype(jnp.float32)
    cells = cells.astype(jnp.bfloat16)
    row_no = lax.broadcasted_iota(jnp.int32, (live, 2 * strokes), 0) + (lat * rows - 8)
    in_row = jnp.where(
        row_no == twice(f_lat[...]),
        jnp.broadcast_to(twice(f_amp[...]), (live, 2 * strokes)),
        0.0,
    )
    steps_of = twice(f_step[...])
    left, right = [], []
    for s in range(STEPS):
        amps = jnp.where(steps_of == s, in_row, 0.0)
        upper = amps.astype(jnp.bfloat16).astype(jnp.float32)
        middle = (amps - upper).astype(jnp.bfloat16).astype(jnp.float32)
        left.append(jnp.where(half_lanes, upper, middle).astype(jnp.bfloat16))
        right.append(jnp.where(half_lanes, amps - upper - middle, 0.0).astype(jnp.bfloat16))
    total = None
    for part in (left, right):
        term = lax.dot_general(
            jnp.concatenate(part, axis=0), cells, (((1,), (0,)), ((), ())),
            preferred_element_type=jnp.float32,
        )
        total = term if total is None else total + term
    src[...] = total

    for k in range(2, n_lon):
        serve(k)
    for a, b in corners:
        if b < 0:
            def corner_last(a=a, b=b):
                pl.semaphore_wait(ack_cross.at[1], 1)
                corner_copy(a, b).start()
            crossing(a, b, True, corner_last)

    for k in range(1, n_lon):
        sum_copy(k).wait_recv()
    mean = sums_out[...]
    for k in range(1, n_lon):
        mean = mean + sums_in[k]
    strip[...] = mean
    for a in (-1, 1):
        pl.when(there(a))(lambda a=a: zone_copy(a).start())

    def unpack(x, band):
        y = jnp.where(lane < layers, turn(x, -layers * band), 0.0)
        p = y + turn(y, 24)
        return p + turn(p, 48) + turn(y, 96)

    edge = jnp.zeros((3, low, 128), jnp.float32)
    for z in (zon, zon_cap):
        z[:, 0:low, :] = edge
        z[:, low + rows:, :] = edge
    for f in range(3):
        for band in range(bands):
            own = unpack(mean[8 * f:8 * f + 8], band)
            for z in (zon, zon_cap):
                z[f, low + 8 * band:low + 8 * band + 8, :] = own

    for part in (0, 1):
        for side in (0, 1):
            for f in range(3 * part, 3 * part + 3):
                lon_copy(1 if side == 0 else -1, f).wait_recv()
            for a in (-1, 1):
                pl.when(shared(a))(
                    lambda a=a, side=side, part=part: relay_copy(a, side, part).start()
                )

    for a in (-1, 1):
        def take(a=a):
            lat_copy(a).wait_recv()
        pl.when(there(-a))(take)

        def take_corners(a=a):
            for b in (-1, 1):
                corner_copy(a, b).wait_recv()
        pl.when(across(-a))(take_corners)

        def take_relays(a=a):
            for part in (0, 1):
                for side in (0, 1):
                    relay_copy(a, side, part).wait_recv()
        pl.when(shared(-a))(take_relays)

    def pole():
        last = pl.ds(low + rows - 8, 8)
        keep = jnp.broadcast_to(table[low + rows - 8:low + rows, C_KEEP:C_KEEP + 1], (8, wide))
        for f in (EE, EU, HN):
            ext[f, last, :] = keep * ext[f, last, :]
    pl.when(jnp.logical_not(there(1)))(pole)

    def zone_rows():
        for a in (-1, 1):
            def take_zone(a=a):
                zone_copy(a).wait_recv()
                i, row, band = (0, low - 8, bands - 1) if a > 0 else (1, low + rows, 0)
                for f in range(3):
                    zon[f, row:row + 8, :] = unpack(zone_in[i, 8 * f:8 * f + 8, :], band)
            pl.when(there(-a))(take_zone)

    outs = (o_en, o_ee, o_eu, o_hn, o_he, o_hr)
    march(dims, ext, buf, src, coef, lanes, zon, zon_cap, outs, o_zon, zone_rows)

    for a in (-1, 1):
        def sent(a=a):
            zone_copy(a).wait_send()
            lat_copy(a).wait_send()
        pl.when(there(a))(sent)

        def sent_corners(a=a):
            for b in (-1, 1):
                corner_copy(a, b).wait_send()
        pl.when(across(a))(sent_corners)

        def sent_relays(a=a):
            for part in (0, 1):
                for side in (0, 1):
                    relay_copy(a, side, part).wait_send()
        pl.when(shared(a))(sent_relays)
    for k in range(1, n_lon):
        sum_copy(k).wait_send()
    for b in (-1, 1):
        all_fields(lon_copy, b, "wait_send")


def march(dims, ext, buf, src, coef, lanes, zon, zon_cap, outs, o_zon, zone_rows):
    n_lat, n_lon, layers, dt, ly = dims
    tall, wide = buf.shape[1:]
    rows, width = tall - 2 * HALO_ROWS, wide - 2 * HALO_LANES
    groups = tall // 8
    own_groups = range(HALO_ROWS // 8, groups - HALO_ROWS // 8)
    low = HALO_ROWS
    lat = lax.axis_index("lat")
    own_r = slice(low, low + rows)
    z_dec, z_drv, z_top, z_bot = [lanes.at[i, :, HALO_LANES:HALO_LANES + 128] for i in (0, 1, 2, 3)]
    lane = lax.broadcasted_iota(jnp.int32, (rows, 128), 1)

    def record(s):
        both = jnp.where(lane < layers, zon[0, own_r, :], turn(zon[2, own_r, :], layers))
        both = jnp.transpose(both)
        o_zon[s, 0] = both[0:layers]
        o_zon[s, 1] = both[layers:2 * layers]

    def zonal_h(zon, span):
        for g in span:
            r = 8 * g
            east = zon[0, r:r + 8, :]
            zon[2, r:r + 8, :] = (
                zon[2, r:r + 8, :]
                - coef[C_AS, r:r + 8] * zon[0, r - 1:r + 7, :]
                + coef[C_BE, r:r + 8] * east
            )
            zon[1, r:r + 8, :] = zon[1, r:r + 8, :] - coef[C_DT, r:r + 8] * (
                z_top[...] * turn(east, -1) - east
            )

    def zonal_e(zon, span):
        for g in span:
            r = 8 * g
            up, north = zon[2, r:r + 8, :], zon[1, r:r + 8, :]
            zon[0, r:r + 8, :] = z_dec[...] * zon[0, r:r + 8, :] + z_drv[...] * (
                coef[C_LY, r:r + 8] * (zon[2, r + 1:r + 9, :] - up)
                - (north - z_bot[...] * turn(north, 1))
            )

    def magnetic(old, a, b, span, beyond, last=False):
        count = (b - a) // 128

        def rowc(c, g):
            return jnp.concatenate([coef[c, 8 * g:8 * g + 8]] * count, axis=1)

        top = lanes[2, :, a:b]
        for g in (*span, *beyond):
            r = 8 * g
            here, south = slice(r, r + 8), slice(r - 1, r + 7)
            e_n, e_e, e_u = old[EN, here, a:b], old[EE, here, a:b], old[EU, here, a:b]
            up = (
                old[HR, here, a:b]
                - rowc(C_AS, g) * old[EE, south, a:b]
                + rowc(C_BE, g) * e_e
                - rowc(C_CN, g) * (turn(e_n, -layers) - e_n)
            )
            if g in (own_groups[0], own_groups[-1]):
                row = lax.broadcasted_iota(jnp.int32, (8, b - a), 0) + (lat * rows - low + r)
                pole = 0 if g == own_groups[0] else n_lat * rows - 1
                up = jnp.where(row == pole, spread(zon_cap[2, here], a // 128, count), up)
            fresh = {HR: up}
            fresh[HE] = (
                old[HE, here, a:b]
                - (dt / ly) * (e_u - old[EU, south, a:b])
                + dt * (top * turn(e_n, -1) - e_n)
            )
            if g in span:
                fresh[HN] = (
                    old[HN, here, a:b]
                    - rowc(C_DU, g) * (e_u - turn(e_u, -layers))
                    - rowc(C_DT, g) * (top * turn(e_e, -1) - e_e)
                )
            for f, x in fresh.items():
                buf[f, here, a:b] = x
                if last and g in span:
                    outs[f][r - low:r - low + 8, :] = x[:, HALO_LANES - a:HALO_LANES - a + width]

    def electric(old, s, a, b, first, span, last=False):
        count = (b - first) // 128
        skip = first - a

        def rowc(c, g):
            return jnp.concatenate([coef[c, 8 * g:8 * g + 8]] * count, axis=1)

        def turned(x, by):
            return turn(x, by)[:, skip:]

        decay, drive, bot = [lanes[i, :, first:b] for i in (0, 1, 3)]
        for g in span:
            r = 8 * g
            here, north = slice(r, r + 8), slice(r + 1, r + 9)
            w_n, w_e, w_r = buf[HN, here, a:b], buf[HE, here, a:b], buf[HR, here, a:b]
            h_n, h_e, h_r = w_n[:, skip:], w_e[:, skip:], w_r[:, skip:]
            fresh = {}
            fresh[EN] = decay * old[EN, here, first:b] + drive * (
                h_e - bot * turned(w_e, 1) - rowc(C_GC, g) * (h_r - turned(w_r, layers))
            )
            fresh[EE] = decay * old[EE, here, first:b] + drive * (
                rowc(C_LY, g) * (buf[HR, north, first:b] - h_r) - (h_n - bot * turned(w_n, 1))
            )
            fresh[EU] = (
                decay * old[EU, here, first:b]
                + drive
                * (
                    rowc(C_IC, g) * h_e
                    - rowc(C_JN, g) * buf[HE, north, first:b]
                    + rowc(C_KL, g) * (h_n - turned(w_n, layers))
                    + src[pl.ds(pl.multiple_of(s * (rows + 16) + r - 8, 8), 8), first:b]
                )
            )

            for f, x in fresh.items():
                if last:
                    outs[f][r - low:r - low + 8, :] = x
                else:
                    buf[f, here, first:b] = x

    inner = range(1, groups - 1)

    def step(old, s, a, b, beyond):
        zonal_h(zon_cap, own_groups)
        magnetic(old, a, b, inner, beyond)
        zonal_e(zon_cap, own_groups)
        electric(old, s, a, b, a, inner)

    def means(s):
        record(s)
        zonal_h(zon, inner)
        zonal_e(zon, inner)

    middle = STEPS - 1 - STEPS // 2

    def early(s, carry):
        step(buf, s, 0, wide, ())
        return carry

    def late(s, carry):
        means(2 * (s - middle))
        means(2 * (s - middle) + 1)
        step(buf, s, 128, wide - 128, ())
        return carry

    step(ext, 0, 0, wide, (groups - 1,))
    lax.fori_loop(1, middle, early, 0)
    zone_rows()
    lax.fori_loop(middle, STEPS - 1, late, 0)
    record(STEPS - 1)
    zonal_h(zon_cap, own_groups)
    magnetic(buf, 128, wide - 128, own_groups, (own_groups[-1] + 1,), last=True)
    electric(buf, STEPS - 1, 128, wide - HALO_LANES, HALO_LANES, own_groups, last=True)


def hand_over(*refs):
    count = len(refs) // 2
    copies = [
        pltpu.make_async_copy(refs[i], refs[count + i], refs[-1].at[i]) for i in range(count)
    ]
    for copy in copies:
        copy.start()
    for copy in copies:
        copy.wait()


def body(
    efield_north,
    efield_east,
    efield_up,
    hfield_north,
    hfield_east,
    hfield_up,
    sigma_profile,
    flash_lat,
    flash_lon,
    flash_step,
    flash_amp,
):
    rows, width = efield_north.shape
    layers = sigma_profile.shape[0]
    n_lat, n_lon = lax.axis_size("lat"), lax.axis_size("lon")
    lat_count, lon_count = rows * n_lat, (width // layers) * n_lon
    dims = (
        n_lat,
        n_lon,
        layers,
        time_step(lat_count, lon_count),
        RADIUS_CELLS * math.pi / lat_count,
    )
    wide, tall = width + 2 * HALO_LANES, rows + 2 * HALO_ROWS
    f32 = jnp.float32
    vmem = pl.BlockSpec(memory_space=pltpu.VMEM)
    dma = pltpu.SemaphoreType.DMA
    hbm = pl.BlockSpec(memory_space=pltpu.HBM)
    strokes = flash_lat.shape[0]
    n_live = rows + 16
    outs = [jax.ShapeDtypeStruct((rows, width), f32)] * 6
    outs += [jax.ShapeDtypeStruct((STEPS, 2, layers, rows), f32)]
    held = pl.pallas_call(
        functools.partial(kernel, dims),
        out_shape=outs,
        in_specs=[hbm] * 12,
        out_specs=[vmem] * 7,
        scratch_shapes=[
            pltpu.VMEM((6, tall, wide), f32),
            pltpu.VMEM((6, tall, wide), f32),
            pltpu.VMEM((STEPS * n_live, wide), f32),
            pltpu.VMEM((10, tall, 128), f32),
            pltpu.VMEM((4, 8, wide), f32),
            pltpu.VMEM((3, tall, 128), f32),
            pltpu.VMEM((3, tall, 128), f32),
            pltpu.VMEM((24, 128), f32),
            pltpu.VMEM((n_lon, 24, 128), f32),
            pltpu.VMEM((2, 24, 128), f32),
            pltpu.VMEM((24, 128), f32),
            pltpu.VMEM((8, 128), f32),
            pltpu.VMEM((1, layers), f32),
            pltpu.VMEM((1, strokes), jnp.int32),
            pltpu.VMEM((1, strokes), jnp.int32),
            pltpu.VMEM((1, strokes), jnp.int32),
            pltpu.VMEM((1, strokes), f32),
            pltpu.VMEM((tall, 128), f32),
            dma((12,)),
            dma((12,)), dma((12,)), dma((4,)), dma((4,)), dma((8,)), dma((8,)),
            dma((16,)), dma((16,)),
            dma((n_lon,)), dma((n_lon,)), dma((2,)), dma((2,)),
            pltpu.SemaphoreType.REGULAR((n_lon,)),
            pltpu.SemaphoreType.REGULAR,
            pltpu.SemaphoreType.REGULAR((2,)),
        ],
        compiler_params=pltpu.CompilerParams(
            collective_id=0, has_side_effects=True, vmem_limit_bytes=VMEM_GRANT
        ),
    )(*(pltpu.with_memory_space_constraint(x, pltpu.HBM) for x in (
        efield_north,
        efield_east,
        efield_up,
        hfield_north,
        hfield_east,
        hfield_up,
        sigma_profile[None, :],
        flash_lat[None, :],
        flash_lon[None, :],
        flash_step[None, :],
        flash_amp[None, :],
        jnp.asarray(row_table(lat_count, lon_count)),
    )))
    results = pl.pallas_call(
        hand_over,
        out_shape=outs,
        in_specs=[vmem] * 7,
        out_specs=[hbm] * 7,
        scratch_shapes=[dma((7,))],
        compiler_params=pltpu.CompilerParams(vmem_limit_bytes=VMEM_GRANT),
    )(*held)
    return (*results[:6], jnp.transpose(results[6], (0, 1, 3, 2)))


def solution(mesh):
    fields = P("lat", "lon")
    return jax.shard_map(
        body,
        mesh=mesh,
        in_specs=(fields,) * 6 + (P(),) * 5,
        out_specs=(fields,) * 6 + (P(None, None, "lat", None),),
        check_vma=False,
    )
```

```python
import functools
import math

import jax
import jax.numpy as jnp
import numpy as np
from jax import lax
from jax.experimental import pallas as pl
from jax.experimental.pallas import tpu as pltpu
from jax.sharding import PartitionSpec as P

CHANNEL = 3
STEPS = 9
RADIUS_CELLS = 1529.0
COURANT = 0.9
VMEM_GRANT = 16 * 1024 * 1024

HALO_ROWS = 16
HALO_LANES = 256
MESH = pl.DeviceIdType.MESH
EN, EE, EU, HN, HE, HR = range(6)
(C_AS, C_BE, C_CN, C_DU, C_DT, C_GC, C_IC, C_JN, C_KL, C_LY) = range(10)
C_KEEP = 10
NINTH = (EN, EE, EU, HN, HR)


def time_step(lat_count, lon_count):
    lon_angle = 2.0 * math.pi / lon_count
    lat_angle = math.pi / lat_count
    narrowest = RADIUS_CELLS * lon_angle * math.sin(lat_angle)
    lat_length = RADIUS_CELLS * lat_angle
    return COURANT / math.sqrt(1.0 / narrowest**2 + 1.0 / lat_length**2 + 1.0)


def row_table(lat_count, lon_count):
    f = np.float32
    lon_angle = 2.0 * math.pi / lon_count
    lat_angle = math.pi / lat_count
    dt = time_step(lat_count, lon_count)
    ly = RADIUS_CELLS * math.pi / lat_count
    row = np.arange(lat_count)
    centre = f(-0.5 * math.pi) + (row.astype(f) + f(0.5)) * f(lat_angle)
    north = centre + f(0.5 * lat_angle)
    south = centre - f(0.5 * lat_angle)
    following = centre + f(lat_angle)
    pole = row == lat_count - 1
    scale = RADIUS_CELLS * lon_angle
    band = 2.0 * RADIUS_CELLS * scale * math.sin(0.5 * lat_angle)
    lc = f(scale) * np.cos(centre)
    ln = f(scale) * np.cos(following)
    le = np.where(pole, f(0), f(scale) * np.cos(north))
    ls = np.where(row == 0, f(0), f(scale) * np.cos(south))
    ls[-1] = le[-2]
    ac = f(band) * np.cos(centre)
    ae = np.where(pole, f(1), f(band) * np.cos(north))
    se = np.where(pole, f(1), le)
    keep = np.where(pole, f(0), f(1))
    table = np.zeros((lat_count + 2 * HALO_ROWS, 128), f)
    inner = table[HALO_ROWS:-HALO_ROWS]
    inner[:, C_AS] = dt * ls / ac
    inner[:, C_BE] = dt * le / ac
    inner[:, C_CN] = dt * ly / ac
    inner[:, C_DU] = keep * dt / se
    inner[:, C_DT] = keep * dt
    inner[:, C_GC] = 1.0 / lc
    inner[:, C_IC] = keep * lc / ae
    inner[:, C_JN] = keep * ln / ae
    inner[:, C_KL] = keep * ly / ae
    inner[:, C_LY] = keep / ly
    inner[:, C_KEEP] = keep
    return table


def turn(x, by):
    return pltpu.roll(x, by % x.shape[1], 1)


def div24(x):
    return lax.shift_right_logical(x * 2731, 16)


def spread(x, first, count):
    lane = lax.broadcasted_iota(jnp.int32, (8, 128), 1)
    out = []
    for v in range(first, first + count):
        off = (128 * v - HALO_LANES) % 24
        out.append(jnp.where(lane < 96, turn(x, -off), turn(x, 24 - off)))
    return jnp.concatenate(out, axis=1)


def kernel(
    dims,
    en, ee, eu, hn, he, hr, h_sigma, h_lat, h_lon, h_step, h_amp, h_table,
    o_en, o_ee, o_eu, o_hn, o_he, o_hr, o_zon,
    ext, far_out, far_in, buf, src, coef, lanes, zon, zon_cap,
    sums_out, sums_in, zone_in, strip, small, sigma, f_lat, f_lon, f_step, f_amp, table,
    load, send_b, recv_b, send_f, recv_f, send_l, recv_l, send_c, recv_c, send_r, recv_r,
    send_s, recv_s, send_z, recv_z,
    ack_lon, ack_lat, ack_cross,
):
    n_lat, n_lon, layers, dt, ly = dims
    fields = (en, ee, eu, hn, he, hr)
    rows, width = en.shape
    strokes = h_lat.shape[1]
    wide = width + 2 * HALO_LANES
    tall = rows + 2 * HALO_ROWS
    vregs = wide // 128
    live = rows + 16
    low = HALO_ROWS
    lat, lon = lax.axis_index("lat"), lax.axis_index("lon")
    own_r = pl.ds(low, rows)
    own_c = pl.ds(HALO_LANES, width)

    def at(a, b):
        row = jnp.clip(lat + a, 0, n_lat - 1) if a else lat
        return {"lat": row, "lon": lax.rem(lon + b + n_lon, n_lon)}

    def there(a):
        return lat + a >= 0 if a < 0 else lat + a < n_lat

    def shared(a):
        return lax.rem(lat, 2) == (0 if a > 0 else 1)

    def across(a):
        return jnp.logical_and(there(a), jnp.logical_not(shared(a)))

    def signal(sem, a, b):
        pl.semaphore_signal(sem, inc=1, device_id=at(a, b), device_id_type=MESH)

    barrier = pltpu.get_barrier_semaphore()
    for k in range(1, n_lon):
        pl.when(lon + k < n_lon)(lambda k=k: signal(barrier, 0, k))
    pl.when(there(1))(lambda: signal(barrier, 1, 0))

    def crossing(a, b, later, act):
        wraps = lon == (n_lon - 1 if b > 0 else 0)
        is_later = jnp.logical_not(wraps) if b > 0 else wraps
        wanted = is_later if later else jnp.logical_not(is_later)
        pl.when(jnp.logical_and(across(a), wanted))(act)

    corners = [(a, b) for a in (-1, 1) for b in (-1, 1)]
    for a, b in corners:
        crossing(a, b, True, lambda a=a, b=b: signal(barrier, a, b))

    loads = [
        pltpu.make_async_copy(x, ext.at[f, own_r, own_c], load.at[f])
        for f, x in enumerate(fields)
    ]
    here_rows = h_table.at[pl.ds(pl.multiple_of(lat * rows, 8), tall), :]
    pairs = (
        (here_rows, table), (h_sigma, sigma), (h_lat, f_lat), (h_lon, f_lon),
        (h_step, f_step), (h_amp, f_amp),
    )
    loads += [pltpu.make_async_copy(x, y, load.at[6 + i]) for i, (x, y) in enumerate(pairs)]
    for copy in loads:
        copy.start()

    def lon_copy(b, f):
        i = f if b > 0 else 6 + f
        cut = pl.ds(width - 128, 128) if b > 0 else pl.ds(0, 128)
        land = pl.ds(HALO_LANES - 128, 128) if b > 0 else pl.ds(HALO_LANES + width, 128)
        return pltpu.make_async_remote_copy(
            src_ref=fields[f].at[:, cut],
            dst_ref=ext.at[f, own_r, land],
            send_sem=send_b.at[i],
            recv_sem=recv_b.at[i],
            device_id=at(0, b),
            device_id_type=MESH,
        )

    def far_copy(b):
        i = 0 if b > 0 else 1
        return pltpu.make_async_remote_copy(
            src_ref=far_out.at[i],
            dst_ref=far_in.at[i, :, own_r, :],
            send_sem=send_f.at[i],
            recv_sem=recv_f.at[i],
            device_id=at(0, b),
            device_id_type=MESH,
        )

    class Pieces:
        def __init__(self, a, parts, here, there, sends, recvs, i, b=0, off=0):
            shift = rows if a > 0 else -rows
            self.copies = [
                pltpu.make_async_remote_copy(
                    src_ref=here(pl.ds(row - off, count), pl.ds(col, span)),
                    dst_ref=there(pl.ds(row - shift, count), pl.ds(land, span)),
                    send_sem=sends.at[2 * i + n],
                    recv_sem=recvs.at[2 * i + n],
                    device_id=at(a, b),
                    device_id_type=MESH,
                )
                for n, (row, count, col, land, span) in enumerate(parts)
            ]

        def start(self):
            for copy in self.copies:
                copy.start()

        def wait_recv(self):
            for copy in self.copies:
                copy.wait_recv()

        def wait_send(self):
            for copy in self.copies:
                copy.wait_send()

    def nine(a, col, land, span):
        first, ninth = (low + rows - 8, low + rows - STEPS) if a > 0 else (low, low + STEPS - 1)
        return (first, 8, col, land, span), (ninth, 1, col, land, span)

    def whole(r, c):
        return ext.at[:, r, c]

    def lat_copy(a):
        parts = nine(a, HALO_LANES, HALO_LANES, width)
        return Pieces(a, parts, whole, whole, send_l, recv_l, 0 if a > 0 else 1)

    def corner_near(a, b):
        col = HALO_LANES + width - 128 if b > 0 else HALO_LANES
        land = HALO_LANES - 128 if b > 0 else HALO_LANES + width
        parts = nine(a, col, land, 128)
        parts = parts if a == b else parts[:1]
        return Pieces(a, parts, whole, whole, send_c, recv_c, corners.index((a, b)), b)

    def corner_far(a, b):
        i = 0 if b > 0 else 1
        parts = nine(a, 0, 0, 128)
        if a != b:
            parts = ((low + rows - 4 if a > 0 else low, 4, 0, 0, 128),)

        def here(r, c):
            return far_out.at[i, :, r, c]

        def there(r, c):
            return far_in.at[i, :, r, c]
        return Pieces(
            a, parts, here, there, send_c, recv_c, 4 + corners.index((a, b)), b, off=low
        )

    def relay_near(a, side, part):
        col = HALO_LANES - 128 if side == 0 else HALO_LANES + width
        i = part + 2 * side + (0 if a > 0 else 4)

        def these(r, c):
            return ext.at[pl.ds(3 * part, 3), r, c]
        return Pieces(a, nine(a, col, col, 128), these, these, send_r, recv_r, i)

    def relay_far(a, side):
        def these(r, c):
            return far_in.at[side, :, r, c]
        i = 8 + side + (0 if a > 0 else 2)
        return Pieces(a, nine(a, 0, 0, 128), these, these, send_r, recv_r, i)

    def sum_copy(k):
        return pltpu.make_async_remote_copy(
            src_ref=sums_out,
            dst_ref=sums_in.at[k],
            send_sem=send_s.at[k],
            recv_sem=recv_s.at[k],
            device_id=at(0, k),
            device_id_type=MESH,
        )

    def zone_copy(a):
        i = 0 if a > 0 else 1
        return pltpu.make_async_remote_copy(
            src_ref=strip,
            dst_ref=zone_in.at[i],
            send_sem=send_z.at[i],
            recv_sem=recv_z.at[i],
            device_id=at(a, 0),
            device_id_type=MESH,
        )

    def all_fields(make, side, act):
        for f in range(6):
            getattr(make(side, f), act)()

    crossed = jnp.where(lon == n_lon - 1, 2, jnp.where(lon == 0, 0, 1))
    crossed = jnp.where(jnp.logical_or(across(-1), across(1)), crossed, 0)
    earlier = lon + (lat > 0).astype(jnp.int32) + crossed
    pl.when(earlier > 0)(lambda: pl.semaphore_wait(barrier, earlier))
    for k in range(n_lon - 1, 0, -1):
        pl.when(lon - k >= 0)(lambda k=k: signal(ack_lon.at[k], 0, -k))
    pl.when(there(-1))(lambda: signal(ack_lat, -1, 0))
    for a, b in corners:
        crossing(a, b, False, lambda a=a, b=b: signal(ack_cross.at[0 if b < 0 else 1], a, b))

    pl.when(lon == n_lon - 1)(lambda: all_fields(lon_copy, 1, "start"))
    pl.when(lon > 0)(lambda: all_fields(lon_copy, -1, "start"))

    for a, first in ((-1, 0), (1, low + rows)):
        def clear(first=first):
            ext[:, first:first + low, :] = jnp.zeros((6, low, wide), jnp.float32)
            far_in[:, :, first:first + low, :] = jnp.zeros((2, 4, low, 128), jnp.float32)
        pl.when(jnp.logical_not(there(a)))(clear)

    for copy in loads[:7]:
        copy.wait()

    pl.when(there(-1))(lambda: lat_copy(-1).start())
    for a, b in corners:
        crossing(a, b, False, lambda a=a, b=b: corner_near(a, b).start())

    half = lax.broadcasted_iota(jnp.int32, (rows, 128), 1)
    mid = [ext[f, own_r, pl.ds(HALO_LANES + 128, 128)] for f in range(6)]
    end = [ext[f, own_r, pl.ds(HALO_LANES + width - 256, 128)] for f in range(6)]
    far_out[0, 0] = jnp.where(half >= 64, end[EN], turn(end[EE], 64))
    far_out[0, 1] = jnp.where(half >= 64, end[EU], turn(end[HN], 64))
    far_out[0, 2] = jnp.where(half >= 64, end[HE], turn(end[HR], 64))
    outer = turn(end[NINTH[0]], -40)
    for m in range(1, len(NINTH)):
        outer = jnp.where(half < 24 * m, outer, turn(end[NINTH[m]], 24 * m - 40))
    far_out[0, 3] = outer
    far_out[1, 0] = mid[EN]
    far_out[1, 1] = mid[EU]
    far_out[1, 2] = jnp.where(half < 64, mid[EE], turn(mid[HN], 64))
    far_out[1, 3] = jnp.where(half < 64, mid[HE], turn(mid[HR], 64))
    for a, b in corners:
        crossing(a, b, False, lambda a=a, b=b: corner_far(a, b).start())
    pl.when(lon == n_lon - 1)(lambda: far_copy(1).start())
    pl.when(lon > 0)(lambda: far_copy(-1).start())

    def fold(x):
        for by in (width // 2, width // 4, width // 8, width // 16):
            x = x + turn(x, by)
        return x[:, :128] * (1.0 / (n_lon * (width // layers)))

    lane = lax.broadcasted_iota(jnp.int32, (8, 128), 1)
    kept = jnp.broadcast_to(table[low:low + rows, C_KEEP:C_KEEP + 1], (rows, 128))
    bands = rows // 8
    for n, f in enumerate((EE, HN, HR)):
        folded = fold(ext[f, own_r, own_c])
        if f != HR:
            folded = kept * folded
        packed = folded[0:8]
        for band in range(1, bands):
            packed = jnp.where(lane < layers * band, packed, folded[8 * band:8 * band + 8])
        sums_out[8 * n:8 * n + 8, :] = packed
    for k in range(1, n_lon):
        pl.when(lon + k >= n_lon)(lambda k=k: sum_copy(k).start())

    def to_north():
        pl.semaphore_wait(ack_lat, 1)
        lat_copy(1).start()
    pl.when(there(1))(to_north)

    def serve(k):
        def to_later():
            pl.semaphore_wait(ack_lon.at[k], 1)
            if k == 1:
                all_fields(lon_copy, 1, "start")
                far_copy(1).start()
            if k == n_lon - 1:
                all_fields(lon_copy, -1, "start")
                far_copy(-1).start()
            sum_copy(k).start()
        pl.when(lon + k < n_lon)(to_later)

    serve(1)
    for a, b in corners:
        if b > 0:
            def corner_later(a=a, b=b):
                pl.semaphore_wait(ack_cross.at[0], 1)
                corner_near(a, b).start()
                corner_far(a, b).start()
            crossing(a, b, True, corner_later)
    for copy in loads[7:]:
        copy.wait()
    rows_tab = table[...]
    for c in range(10):
        coef[c] = jnp.broadcast_to(rows_tab[:, c:c + 1], (tall, 128))
    small[...] = jnp.zeros((8, 128), jnp.float32)
    small[0:1, 0:layers] = sigma[...]
    one = jnp.broadcast_to(small[0:1, :], (8, 128))
    pair = one + turn(one, 24)
    sig = pair + turn(pair, 48) + turn(one, 96)
    half = 0.5 * dt * sig
    dec = (1.0 - half) / (1.0 + half)
    drv = dt / (1.0 + half)

    at_lane = lax.broadcasted_iota(jnp.int32, (8, wide), 1) + 8
    layer = at_lane - 24 * div24(at_lane)
    lanes[0] = spread(dec, 0, vregs)
    lanes[1] = spread(drv, 0, vregs)
    lanes[2] = jnp.where(layer == layers - 1, 0.0, 1.0)
    lanes[3] = jnp.where(layer == 0, 0.0, 1.0)

    half_lanes = lax.broadcasted_iota(jnp.int32, (1, 128), 1) < strokes

    def twice(x):
        return jnp.concatenate([x, x], axis=1)

    def column(x):
        return jnp.transpose(jnp.broadcast_to(x.astype(jnp.float32), (128, 2 * strokes)))

    cell = div24(at_lane[0:1]) - 11 + lon * (width // layers)
    total_lon = n_lon * (width // layers)
    cell = jnp.where(cell < 0, cell + total_lon, cell)
    cell = jnp.where(cell >= total_lon, cell - total_lon, cell)
    cell = jnp.where(layer[0:1] < CHANNEL, cell, -1).astype(jnp.float32)
    lon_of = jnp.concatenate([column(twice(f_lon[...]))] * vregs, axis=1)
    cells = (jnp.broadcast_to(cell, (2 * strokes, wide)) == lon_of).astype(jnp.float32)
    cells = cells.astype(jnp.bfloat16)
    row_no = lax.broadcasted_iota(jnp.int32, (live, 2 * strokes), 0) + (lat * rows - 8)
    in_row = jnp.where(
        row_no == twice(f_lat[...]),
        jnp.broadcast_to(twice(f_amp[...]), (live, 2 * strokes)),
        0.0,
    )
    steps_of = twice(f_step[...])
    left, right = [], []
    for s in range(STEPS):
        amps = jnp.where(steps_of == s, in_row, 0.0)
        upper = amps.astype(jnp.bfloat16).astype(jnp.float32)
        middle = (amps - upper).astype(jnp.bfloat16).astype(jnp.float32)
        left.append(jnp.where(half_lanes, upper, middle).astype(jnp.bfloat16))
        right.append(jnp.where(half_lanes, amps - upper - middle, 0.0).astype(jnp.bfloat16))
    total = None
    for part in (left, right):
        term = lax.dot_general(
            jnp.concatenate(part, axis=0), cells, (((1,), (0,)), ((), ())),
            preferred_element_type=jnp.float32,
        )
        total = term if total is None else total + term
    src[...] = total

    for k in range(2, n_lon):
        serve(k)
    for a, b in corners:
        if b < 0:
            def corner_last(a=a, b=b):
                pl.semaphore_wait(ack_cross.at[1], 1)
                corner_near(a, b).start()
                corner_far(a, b).start()
            crossing(a, b, True, corner_last)

    for k in range(1, n_lon):
        sum_copy(k).wait_recv()
    mean = sums_out[...]
    for k in range(1, n_lon):
        mean = mean + sums_in[k]
    strip[...] = mean
    for a in (-1, 1):
        pl.when(there(a))(lambda a=a: zone_copy(a).start())

    def unpack(x, band):
        y = jnp.where(lane < layers, turn(x, -layers * band), 0.0)
        p = y + turn(y, 24)
        return p + turn(p, 48) + turn(y, 96)

    edge = jnp.zeros((3, low, 128), jnp.float32)
    for z in (zon, zon_cap):
        z[:, 0:low, :] = edge
        z[:, low + rows:, :] = edge
    for f in range(3):
        for band in range(bands):
            own = unpack(mean[8 * f:8 * f + 8], band)
            for z in (zon, zon_cap):
                z[f, low + 8 * band:low + 8 * band + 8, :] = own

    for part in (0, 1):
        for side in (0, 1):
            for f in range(3 * part, 3 * part + 3):
                lon_copy(1 if side == 0 else -1, f).wait_recv()
            for a in (-1, 1):
                pl.when(shared(a))(
                    lambda a=a, side=side, part=part: relay_near(a, side, part).start()
                )
    for side in (0, 1):
        far_copy(1 if side == 0 else -1).wait_recv()
        for a in (-1, 1):
            pl.when(shared(a))(lambda a=a, side=side: relay_far(a, side).start())

    for a in (-1, 1):
        def take(a=a):
            lat_copy(a).wait_recv()
        pl.when(there(-a))(take)

        def take_corners(a=a):
            for b in (-1, 1):
                corner_near(a, b).wait_recv()
                corner_far(a, b).wait_recv()
        pl.when(across(-a))(take_corners)

        def take_relays(a=a):
            for side in (0, 1):
                for part in (0, 1):
                    relay_near(a, side, part).wait_recv()
                relay_far(a, side).wait_recv()
        pl.when(shared(-a))(take_relays)

    half = lax.broadcasted_iota(jnp.int32, (8, 128), 1)
    for r in range(0, tall, 8):
        here = slice(r, r + 8)
        one, two, three, outer = [far_in[0, n, here, :] for n in range(4)]
        inside = {
            EN: one, EE: turn(one, 64), EU: two, HN: turn(two, 64), HE: three, HR: turn(three, 64)
        }
        for m, f in enumerate(NINTH):
            inside[f] = jnp.where(half >= 64, inside[f], turn(outer, 40 - 24 * m))
        for f, x in inside.items():
            ext[f, here, 0:128] = x
        one, two, three, outer = [far_in[1, n, here, :] for n in range(4)]
        inside = {
            EN: one, EE: three, EU: two, HN: turn(three, 64), HE: outer, HR: turn(outer, 64)
        }
        for f, x in inside.items():
            ext[f, here, wide - 128:wide] = x

    def pole():
        last = pl.ds(low + rows - 8, 8)
        keep = jnp.broadcast_to(table[low + rows - 8:low + rows, C_KEEP:C_KEEP + 1], (8, wide))
        for f in (EE, EU, HN):
            ext[f, last, :] = keep * ext[f, last, :]
    pl.when(jnp.logical_not(there(1)))(pole)

    def zone_rows():
        for a in (-1, 1):
            def take_zone(a=a):
                zone_copy(a).wait_recv()
                i, row, band = (0, low - 8, bands - 1) if a > 0 else (1, low + rows, 0)
                for f in range(3):
                    zon[f, row:row + 8, :] = unpack(zone_in[i, 8 * f:8 * f + 8, :], band)
            pl.when(there(-a))(take_zone)

    outs = (o_en, o_ee, o_eu, o_hn, o_he, o_hr)
    march(dims, ext, buf, src, coef, lanes, zon, zon_cap, outs, o_zon, zone_rows)

    for a in (-1, 1):
        def sent(a=a):
            zone_copy(a).wait_send()
            lat_copy(a).wait_send()
        pl.when(there(a))(sent)

        def sent_corners(a=a):
            for b in (-1, 1):
                corner_near(a, b).wait_send()
                corner_far(a, b).wait_send()
        pl.when(across(a))(sent_corners)

        def sent_relays(a=a):
            for side in (0, 1):
                for part in (0, 1):
                    relay_near(a, side, part).wait_send()
                relay_far(a, side).wait_send()
        pl.when(shared(a))(sent_relays)
    for k in range(1, n_lon):
        sum_copy(k).wait_send()
    for b in (-1, 1):
        all_fields(lon_copy, b, "wait_send")
        far_copy(b).wait_send()


def march(dims, ext, buf, src, coef, lanes, zon, zon_cap, outs, o_zon, zone_rows):
    n_lat, n_lon, layers, dt, ly = dims
    tall, wide = buf.shape[1:]
    rows, width = tall - 2 * HALO_ROWS, wide - 2 * HALO_LANES
    groups = tall // 8
    own_groups = range(HALO_ROWS // 8, groups - HALO_ROWS // 8)
    low = HALO_ROWS
    lat = lax.axis_index("lat")
    own_r = slice(low, low + rows)
    z_dec, z_drv, z_top, z_bot = [lanes.at[i, :, HALO_LANES:HALO_LANES + 128] for i in (0, 1, 2, 3)]
    lane = lax.broadcasted_iota(jnp.int32, (rows, 128), 1)

    def record(s):
        both = jnp.where(lane < layers, zon[0, own_r, :], turn(zon[2, own_r, :], layers))
        both = jnp.transpose(both)
        o_zon[s, 0] = both[0:layers]
        o_zon[s, 1] = both[layers:2 * layers]

    def zonal_h(zon, span):
        for g in span:
            r = 8 * g
            east = zon[0, r:r + 8, :]
            zon[2, r:r + 8, :] = (
                zon[2, r:r + 8, :]
                - coef[C_AS, r:r + 8] * zon[0, r - 1:r + 7, :]
                + coef[C_BE, r:r + 8] * east
            )
            zon[1, r:r + 8, :] = zon[1, r:r + 8, :] - coef[C_DT, r:r + 8] * (
                z_top[...] * turn(east, -1) - east
            )

    def zonal_e(zon, span):
        for g in span:
            r = 8 * g
            up, north = zon[2, r:r + 8, :], zon[1, r:r + 8, :]
            zon[0, r:r + 8, :] = z_dec[...] * zon[0, r:r + 8, :] + z_drv[...] * (
                coef[C_LY, r:r + 8] * (zon[2, r + 1:r + 9, :] - up)
                - (north - z_bot[...] * turn(north, 1))
            )

    def magnetic(old, a, b, span, beyond, last=False):
        count = (b - a) // 128

        def rowc(c, g):
            return jnp.concatenate([coef[c, 8 * g:8 * g + 8]] * count, axis=1)

        top = lanes[2, :, a:b]
        for g in (*span, *beyond):
            r = 8 * g
            here, south = slice(r, r + 8), slice(r - 1, r + 7)
            e_n, e_e, e_u = old[EN, here, a:b], old[EE, here, a:b], old[EU, here, a:b]
            up = (
                old[HR, here, a:b]
                - rowc(C_AS, g) * old[EE, south, a:b]
                + rowc(C_BE, g) * e_e
                - rowc(C_CN, g) * (turn(e_n, -layers) - e_n)
            )
            if g in (own_groups[0], own_groups[-1]):
                row = lax.broadcasted_iota(jnp.int32, (8, b - a), 0) + (lat * rows - low + r)
                pole = 0 if g == own_groups[0] else n_lat * rows - 1
                up = jnp.where(row == pole, spread(zon_cap[2, here], a // 128, count), up)
            fresh = {HR: up}
            fresh[HE] = (
                old[HE, here, a:b]
                - (dt / ly) * (e_u - old[EU, south, a:b])
                + dt * (top * turn(e_n, -1) - e_n)
            )
            if g in span:
                fresh[HN] = (
                    old[HN, here, a:b]
                    - rowc(C_DU, g) * (e_u - turn(e_u, -layers))
                    - rowc(C_DT, g) * (top * turn(e_e, -1) - e_e)
                )
            for f, x in fresh.items():
                buf[f, here, a:b] = x
                if last and g in span:
                    outs[f][r - low:r - low + 8, :] = x[:, HALO_LANES - a:HALO_LANES - a + width]

    def electric(old, s, a, b, first, span, last=False):
        count = (b - first) // 128
        skip = first - a

        def rowc(c, g):
            return jnp.concatenate([coef[c, 8 * g:8 * g + 8]] * count, axis=1)

        def turned(x, by):
            return turn(x, by)[:, skip:]

        decay, drive, bot = [lanes[i, :, first:b] for i in (0, 1, 3)]
        for g in span:
            r = 8 * g
            here, north = slice(r, r + 8), slice(r + 1, r + 9)
            w_n, w_e, w_r = buf[HN, here, a:b], buf[HE, here, a:b], buf[HR, here, a:b]
            h_n, h_e, h_r = w_n[:, skip:], w_e[:, skip:], w_r[:, skip:]
            fresh = {}
            fresh[EN] = decay * old[EN, here, first:b] + drive * (
                h_e - bot * turned(w_e, 1) - rowc(C_GC, g) * (h_r - turned(w_r, layers))
            )
            fresh[EE] = decay * old[EE, here, first:b] + drive * (
                rowc(C_LY, g) * (buf[HR, north, first:b] - h_r) - (h_n - bot * turned(w_n, 1))
            )
            fresh[EU] = (
                decay * old[EU, here, first:b]
                + drive
                * (
                    rowc(C_IC, g) * h_e
                    - rowc(C_JN, g) * buf[HE, north, first:b]
                    + rowc(C_KL, g) * (h_n - turned(w_n, layers))
                    + src[pl.ds(pl.multiple_of(s * (rows + 16) + r - 8, 8), 8), first:b]
                )
            )

            for f, x in fresh.items():
                if last:
                    outs[f][r - low:r - low + 8, :] = x
                else:
                    buf[f, here, first:b] = x

    inner = range(1, groups - 1)

    def step(old, s, a, b, beyond):
        zonal_h(zon_cap, own_groups)
        magnetic(old, a, b, inner, beyond)
        zonal_e(zon_cap, own_groups)
        electric(old, s, a, b, a, inner)

    def means(s):
        record(s)
        zonal_h(zon, inner)
        zonal_e(zon, inner)

    middle = STEPS - 1 - STEPS // 2

    def early(s, carry):
        step(buf, s, 0, wide, ())
        return carry

    def late(s, carry):
        means(2 * (s - middle))
        means(2 * (s - middle) + 1)
        step(buf, s, 128, wide - 128, ())
        return carry

    step(ext, 0, 0, wide, (groups - 1,))
    lax.fori_loop(1, middle, early, 0)
    zone_rows()
    lax.fori_loop(middle, STEPS - 1, late, 0)
    record(STEPS - 1)
    zonal_h(zon_cap, own_groups)
    magnetic(buf, 128, wide - 128, own_groups, (own_groups[-1] + 1,), last=True)
    electric(buf, STEPS - 1, 128, wide - HALO_LANES, HALO_LANES, own_groups, last=True)


def hand_over(*refs):
    count = len(refs) // 2
    copies = [
        pltpu.make_async_copy(refs[i], refs[count + i], refs[-1].at[i]) for i in range(count)
    ]
    for copy in copies:
        copy.start()
    for copy in copies:
        copy.wait()


def body(
    efield_north,
    efield_east,
    efield_up,
    hfield_north,
    hfield_east,
    hfield_up,
    sigma_profile,
    flash_lat,
    flash_lon,
    flash_step,
    flash_amp,
):
    rows, width = efield_north.shape
    layers = sigma_profile.shape[0]
    n_lat, n_lon = lax.axis_size("lat"), lax.axis_size("lon")
    lat_count, lon_count = rows * n_lat, (width // layers) * n_lon
    dims = (
        n_lat,
        n_lon,
        layers,
        time_step(lat_count, lon_count),
        RADIUS_CELLS * math.pi / lat_count,
    )
    wide, tall = width + 2 * HALO_LANES, rows + 2 * HALO_ROWS
    f32 = jnp.float32
    vmem = pl.BlockSpec(memory_space=pltpu.VMEM)
    dma = pltpu.SemaphoreType.DMA
    hbm = pl.BlockSpec(memory_space=pltpu.HBM)
    strokes = flash_lat.shape[0]
    n_live = rows + 16
    outs = [jax.ShapeDtypeStruct((rows, width), f32)] * 6
    outs += [jax.ShapeDtypeStruct((STEPS, 2, layers, rows), f32)]
    held = pl.pallas_call(
        functools.partial(kernel, dims),
        out_shape=outs,
        in_specs=[hbm] * 12,
        out_specs=[vmem] * 7,
        scratch_shapes=[
            pltpu.VMEM((6, tall, wide), f32),
            pltpu.VMEM((2, 4, rows, 128), f32),
            pltpu.VMEM((2, 4, tall, 128), f32),
            pltpu.VMEM((6, tall, wide), f32),
            pltpu.VMEM((STEPS * n_live, wide), f32),
            pltpu.VMEM((10, tall, 128), f32),
            pltpu.VMEM((4, 8, wide), f32),
            pltpu.VMEM((3, tall, 128), f32),
            pltpu.VMEM((3, tall, 128), f32),
            pltpu.VMEM((24, 128), f32),
            pltpu.VMEM((n_lon, 24, 128), f32),
            pltpu.VMEM((2, 24, 128), f32),
            pltpu.VMEM((24, 128), f32),
            pltpu.VMEM((8, 128), f32),
            pltpu.VMEM((1, layers), f32),
            pltpu.VMEM((1, strokes), jnp.int32),
            pltpu.VMEM((1, strokes), jnp.int32),
            pltpu.VMEM((1, strokes), jnp.int32),
            pltpu.VMEM((1, strokes), f32),
            pltpu.VMEM((tall, 128), f32),
            dma((12,)),
            dma((12,)), dma((12,)), dma((2,)), dma((2,)), dma((4,)), dma((4,)),
            dma((16,)), dma((16,)), dma((24,)), dma((24,)),
            dma((n_lon,)), dma((n_lon,)), dma((2,)), dma((2,)),
            pltpu.SemaphoreType.REGULAR((n_lon,)),
            pltpu.SemaphoreType.REGULAR,
            pltpu.SemaphoreType.REGULAR((2,)),
        ],
        compiler_params=pltpu.CompilerParams(
            collective_id=0, has_side_effects=True, vmem_limit_bytes=VMEM_GRANT
        ),
    )(*(pltpu.with_memory_space_constraint(x, pltpu.HBM) for x in (
        efield_north,
        efield_east,
        efield_up,
        hfield_north,
        hfield_east,
        hfield_up,
        sigma_profile[None, :],
        flash_lat[None, :],
        flash_lon[None, :],
        flash_step[None, :],
        flash_amp[None, :],
        jnp.asarray(row_table(lat_count, lon_count)),
    )))
    results = pl.pallas_call(
        hand_over,
        out_shape=outs,
        in_specs=[vmem] * 7,
        out_specs=[hbm] * 7,
        scratch_shapes=[dma((7,))],
        compiler_params=pltpu.CompilerParams(vmem_limit_bytes=VMEM_GRANT),
    )(*held)
    return (*results[:6], jnp.transpose(results[6], (0, 1, 3, 2)))


def solution(mesh):
    fields = P("lat", "lon")
    return jax.shard_map(
        body,
        mesh=mesh,
        in_specs=(fields,) * 6 + (P(),) * 5,
        out_specs=(fields,) * 6 + (P(None, None, "lat", None),),
        check_vma=False,
    )
```

```python
import functools
import math

import jax
import jax.numpy as jnp
import numpy as np
from jax import lax
from jax.experimental import pallas as pl
from jax.experimental.pallas import tpu as pltpu
from jax.sharding import PartitionSpec as P

CHANNEL = 3
STEPS = 9
RADIUS_CELLS = 1529.0
COURANT = 0.9
VMEM_GRANT = 16 * 1024 * 1024

HALO_ROWS = 16
HALO_LANES = 256
MESH = pl.DeviceIdType.MESH
EN, EE, EU, HN, HE, HR = range(6)
(C_AS, C_BE, C_CN, C_DU, C_DT, C_GC, C_IC, C_JN, C_KL, C_LY) = range(10)
C_KEEP = 10
NINTH = (EN, EE, EU, HN, HR)


def time_step(lat_count, lon_count):
    lon_angle = 2.0 * math.pi / lon_count
    lat_angle = math.pi / lat_count
    narrowest = RADIUS_CELLS * lon_angle * math.sin(lat_angle)
    lat_length = RADIUS_CELLS * lat_angle
    return COURANT / math.sqrt(1.0 / narrowest**2 + 1.0 / lat_length**2 + 1.0)


def row_table(lat_count, lon_count):
    f = np.float32
    lon_angle = 2.0 * math.pi / lon_count
    lat_angle = math.pi / lat_count
    dt = time_step(lat_count, lon_count)
    ly = RADIUS_CELLS * math.pi / lat_count
    row = np.arange(lat_count)
    centre = f(-0.5 * math.pi) + (row.astype(f) + f(0.5)) * f(lat_angle)
    north = centre + f(0.5 * lat_angle)
    south = centre - f(0.5 * lat_angle)
    following = centre + f(lat_angle)
    pole = row == lat_count - 1
    scale = RADIUS_CELLS * lon_angle
    band = 2.0 * RADIUS_CELLS * scale * math.sin(0.5 * lat_angle)
    lc = f(scale) * np.cos(centre)
    ln = f(scale) * np.cos(following)
    le = np.where(pole, f(0), f(scale) * np.cos(north))
    ls = np.where(row == 0, f(0), f(scale) * np.cos(south))
    ls[-1] = le[-2]
    ac = f(band) * np.cos(centre)
    ae = np.where(pole, f(1), f(band) * np.cos(north))
    se = np.where(pole, f(1), le)
    keep = np.where(pole, f(0), f(1))
    table = np.zeros((lat_count + 2 * HALO_ROWS, 128), f)
    inner = table[HALO_ROWS:-HALO_ROWS]
    inner[:, C_AS] = dt * ls / ac
    inner[:, C_BE] = dt * le / ac
    inner[:, C_CN] = dt * ly / ac
    inner[:, C_DU] = keep * dt / se
    inner[:, C_DT] = keep * dt
    inner[:, C_GC] = 1.0 / lc
    inner[:, C_IC] = keep * lc / ae
    inner[:, C_JN] = keep * ln / ae
    inner[:, C_KL] = keep * ly / ae
    inner[:, C_LY] = keep / ly
    inner[:, C_KEEP] = keep
    return table


def turn(x, by):
    return pltpu.roll(x, by % x.shape[1], 1)


def div24(x):
    return lax.shift_right_logical(x * 2731, 16)


def spread(x, first, count):
    lane = lax.broadcasted_iota(jnp.int32, (8, 128), 1)
    out = []
    for v in range(first, first + count):
        off = (128 * v - HALO_LANES) % 24
        out.append(jnp.where(lane < 96, turn(x, -off), turn(x, 24 - off)))
    return jnp.concatenate(out, axis=1)


def kernel(
    dims,
    en, ee, eu, hn, he, hr, h_sigma, h_lat, h_lon, h_step, h_amp, h_table,
    o_en, o_ee, o_eu, o_hn, o_he, o_hr, o_zon,
    ext, far_out, far_in, buf, src, coef, lanes, zon, zon_cap,
    sums_out, sums_in, zone_in, strip, small, sigma, f_lat, f_lon, f_step, f_amp, table,
    load, send_b, recv_b, send_f, recv_f, send_l, recv_l, send_c, recv_c, send_r, recv_r,
    send_s, recv_s, send_z, recv_z,
    ack_lon, ack_lat, ack_cross,
):
    n_lat, n_lon, layers, dt, ly = dims
    fields = (en, ee, eu, hn, he, hr)
    rows, width = en.shape
    strokes = h_lat.shape[1]
    wide = width + 2 * HALO_LANES
    tall = rows + 2 * HALO_ROWS
    vregs = wide // 128
    live = rows + 16
    low = HALO_ROWS
    lat, lon = lax.axis_index("lat"), lax.axis_index("lon")
    own_r = pl.ds(low, rows)
    own_c = pl.ds(HALO_LANES, width)

    def at(a, b):
        row = jnp.clip(lat + a, 0, n_lat - 1) if a else lat
        return {"lat": row, "lon": lax.rem(lon + b + n_lon, n_lon)}

    def there(a):
        return lat + a >= 0 if a < 0 else lat + a < n_lat

    def shared(a):
        return lax.rem(lat, 2) == (0 if a > 0 else 1)

    def across(a):
        return jnp.logical_and(there(a), jnp.logical_not(shared(a)))

    def signal(sem, a, b):
        pl.semaphore_signal(sem, inc=1, device_id=at(a, b), device_id_type=MESH)

    barrier = pltpu.get_barrier_semaphore()
    for k in range(1, n_lon):
        pl.when(lon + k < n_lon)(lambda k=k: signal(barrier, 0, k))
    pl.when(there(1))(lambda: signal(barrier, 1, 0))

    def crossing(a, b, later, act):
        wraps = lon == (n_lon - 1 if b > 0 else 0)
        is_later = jnp.logical_not(wraps) if b > 0 else wraps
        wanted = is_later if later else jnp.logical_not(is_later)
        pl.when(jnp.logical_and(across(a), wanted))(act)

    corners = [(a, b) for a in (-1, 1) for b in (-1, 1)]
    for a, b in corners:
        crossing(a, b, True, lambda a=a, b=b: signal(barrier, a, b))

    loads = [
        pltpu.make_async_copy(x, ext.at[f, own_r, own_c], load.at[f])
        for f, x in enumerate(fields)
    ]
    here_rows = h_table.at[pl.ds(pl.multiple_of(lat * rows, 8), tall), :]
    pairs = (
        (here_rows, table), (h_sigma, sigma), (h_lat, f_lat), (h_lon, f_lon),
        (h_step, f_step), (h_amp, f_amp),
    )
    loads += [pltpu.make_async_copy(x, y, load.at[6 + i]) for i, (x, y) in enumerate(pairs)]
    for copy in loads:
        copy.start()

    def lon_copy(b, f):
        i = f if b > 0 else 6 + f
        cut = pl.ds(width - 128, 128) if b > 0 else pl.ds(0, 128)
        land = pl.ds(HALO_LANES - 128, 128) if b > 0 else pl.ds(HALO_LANES + width, 128)
        return pltpu.make_async_remote_copy(
            src_ref=fields[f].at[:, cut],
            dst_ref=ext.at[f, own_r, land],
            send_sem=send_b.at[i],
            recv_sem=recv_b.at[i],
            device_id=at(0, b),
            device_id_type=MESH,
        )

    def far_copy(b):
        i = 0 if b > 0 else 1
        return pltpu.make_async_remote_copy(
            src_ref=far_out.at[i],
            dst_ref=far_in.at[i, :, own_r, :],
            send_sem=send_f.at[i],
            recv_sem=recv_f.at[i],
            device_id=at(0, b),
            device_id_type=MESH,
        )

    class Pieces:
        def __init__(self, a, parts, here, there, sends, recvs, i, b=0, off=0):
            shift = rows if a > 0 else -rows
            self.copies = [
                pltpu.make_async_remote_copy(
                    src_ref=here(pl.ds(row - off, count), pl.ds(col, span)),
                    dst_ref=there(pl.ds(row - shift, count), pl.ds(land, span)),
                    send_sem=sends.at[2 * i + n],
                    recv_sem=recvs.at[2 * i + n],
                    device_id=at(a, b),
                    device_id_type=MESH,
                )
                for n, (row, count, col, land, span) in enumerate(parts)
            ]

        def start(self):
            for copy in self.copies:
                copy.start()

        def wait_recv(self):
            for copy in self.copies:
                copy.wait_recv()

        def wait_send(self):
            for copy in self.copies:
                copy.wait_send()

    def nine(a, col, land, span):
        first, ninth = (low + rows - 8, low + rows - STEPS) if a > 0 else (low, low + STEPS - 1)
        return (first, 8, col, land, span), (ninth, 1, col, land, span)

    def whole(r, c):
        return ext.at[:, r, c]

    def lat_copy(a):
        parts = nine(a, HALO_LANES, HALO_LANES, width)
        return Pieces(a, parts, whole, whole, send_l, recv_l, 0 if a > 0 else 1)

    def corner_near(a, b):
        col = HALO_LANES + width - 128 if b > 0 else HALO_LANES
        land = HALO_LANES - 128 if b > 0 else HALO_LANES + width
        parts = nine(a, col, land, 128)
        parts = parts if a == b else parts[:1]
        return Pieces(a, parts, whole, whole, send_c, recv_c, corners.index((a, b)), b)

    def corner_far(a, b):
        i = 0 if b > 0 else 1
        parts = nine(a, 0, 0, 128)
        if a != b:
            parts = ((low + rows - 4 if a > 0 else low, 4, 0, 0, 128),)

        def here(r, c):
            return far_out.at[i, :, r, c]

        def there(r, c):
            return far_in.at[i, :, r, c]
        return Pieces(
            a, parts, here, there, send_c, recv_c, 4 + corners.index((a, b)), b, off=low
        )

    def relay_near(a, side, part):
        col = HALO_LANES - 128 if side == 0 else HALO_LANES + width
        i = part + 2 * side + (0 if a > 0 else 4)

        def these(r, c):
            return ext.at[pl.ds(3 * part, 3), r, c]
        return Pieces(a, nine(a, col, col, 128), these, these, send_r, recv_r, i)

    def relay_far(a, side):
        def these(r, c):
            return far_in.at[side, :, r, c]
        i = 8 + side + (0 if a > 0 else 2)
        return Pieces(a, nine(a, 0, 0, 128), these, these, send_r, recv_r, i)

    def sum_copy(k):
        return pltpu.make_async_remote_copy(
            src_ref=sums_out,
            dst_ref=sums_in.at[k],
            send_sem=send_s.at[k],
            recv_sem=recv_s.at[k],
            device_id=at(0, k),
            device_id_type=MESH,
        )

    def zone_copy(a):
        i = 0 if a > 0 else 1
        return pltpu.make_async_remote_copy(
            src_ref=strip,
            dst_ref=zone_in.at[i],
            send_sem=send_z.at[i],
            recv_sem=recv_z.at[i],
            device_id=at(a, 0),
            device_id_type=MESH,
        )

    def all_fields(make, side, act):
        for f in range(6):
            getattr(make(side, f), act)()

    crossed = jnp.where(lon == n_lon - 1, 2, jnp.where(lon == 0, 0, 1))
    crossed = jnp.where(jnp.logical_or(across(-1), across(1)), crossed, 0)
    earlier = lon + (lat > 0).astype(jnp.int32) + crossed
    pl.when(earlier > 0)(lambda: pl.semaphore_wait(barrier, earlier))
    for k in range(n_lon - 1, 0, -1):
        pl.when(lon - k >= 0)(lambda k=k: signal(ack_lon.at[k], 0, -k))
    pl.when(there(-1))(lambda: signal(ack_lat, -1, 0))
    for a, b in corners:
        crossing(a, b, False, lambda a=a, b=b: signal(ack_cross.at[0 if b < 0 else 1], a, b))

    pl.when(lon == n_lon - 1)(lambda: all_fields(lon_copy, 1, "start"))
    pl.when(lon > 0)(lambda: all_fields(lon_copy, -1, "start"))

    for a, first in ((-1, 0), (1, low + rows)):
        def clear(first=first):
            ext[:, first:first + low, :] = jnp.zeros((6, low, wide), jnp.float32)
            far_in[:, :, first:first + low, :] = jnp.zeros((2, 4, low, 128), jnp.float32)
        pl.when(jnp.logical_not(there(a)))(clear)

    for copy in loads[:7]:
        copy.wait()

    pl.when(there(-1))(lambda: lat_copy(-1).start())
    for a, b in corners:
        crossing(a, b, False, lambda a=a, b=b: corner_near(a, b).start())

    half = lax.broadcasted_iota(jnp.int32, (rows, 128), 1)
    mid = [ext[f, own_r, pl.ds(HALO_LANES + 128, 128)] for f in range(6)]
    end = [ext[f, own_r, pl.ds(HALO_LANES + width - 256, 128)] for f in range(6)]
    far_out[0, 0] = jnp.where(half >= 64, end[EN], turn(end[EE], 64))
    far_out[0, 1] = jnp.where(half >= 64, end[EU], turn(end[HN], 64))
    far_out[0, 2] = jnp.where(half >= 64, end[HE], turn(end[HR], 64))
    outer = turn(end[NINTH[0]], -40)
    for m in range(1, len(NINTH)):
        outer = jnp.where(half < 24 * m, outer, turn(end[NINTH[m]], 24 * m - 40))
    far_out[0, 3] = outer
    far_out[1, 0] = mid[EN]
    far_out[1, 1] = mid[EU]
    far_out[1, 2] = jnp.where(half < 64, mid[EE], turn(mid[HN], 64))
    far_out[1, 3] = jnp.where(half < 64, mid[HE], turn(mid[HR], 64))
    for a, b in corners:
        crossing(a, b, False, lambda a=a, b=b: corner_far(a, b).start())
    pl.when(lon == n_lon - 1)(lambda: far_copy(1).start())
    pl.when(lon > 0)(lambda: far_copy(-1).start())

    def fold(x):
        for by in (width // 2, width // 4, width // 8, width // 16):
            x = x + turn(x, by)
        return x[:, :128] * (1.0 / (n_lon * (width // layers)))

    lane = lax.broadcasted_iota(jnp.int32, (8, 128), 1)
    kept = jnp.broadcast_to(table[low:low + rows, C_KEEP:C_KEEP + 1], (rows, 128))
    bands = rows // 8
    for n, f in enumerate((EE, HN, HR)):
        folded = fold(ext[f, own_r, own_c])
        if f != HR:
            folded = kept * folded
        packed = folded[0:8]
        for band in range(1, bands):
            packed = jnp.where(lane < layers * band, packed, folded[8 * band:8 * band + 8])
        sums_out[8 * n:8 * n + 8, :] = packed
    for k in range(1, n_lon):
        pl.when(lon + k >= n_lon)(lambda k=k: sum_copy(k).start())

    def to_north():
        pl.semaphore_wait(ack_lat, 1)
        lat_copy(1).start()
    pl.when(there(1))(to_north)

    def serve(k):
        def to_later():
            pl.semaphore_wait(ack_lon.at[k], 1)
            if k == 1:
                all_fields(lon_copy, 1, "start")
                far_copy(1).start()
            if k == n_lon - 1:
                all_fields(lon_copy, -1, "start")
                far_copy(-1).start()
            sum_copy(k).start()
        pl.when(lon + k < n_lon)(to_later)

    serve(1)
    for a, b in corners:
        if b > 0:
            def corner_later(a=a, b=b):
                pl.semaphore_wait(ack_cross.at[0], 1)
                corner_near(a, b).start()
                corner_far(a, b).start()
            crossing(a, b, True, corner_later)
    for copy in loads[7:]:
        copy.wait()
    rows_tab = table[...]
    for c in range(10):
        coef[c] = jnp.broadcast_to(rows_tab[:, c:c + 1], (tall, 128))
    small[...] = jnp.zeros((8, 128), jnp.float32)
    small[0:1, 0:layers] = sigma[...]
    one = jnp.broadcast_to(small[0:1, :], (8, 128))
    pair = one + turn(one, 24)
    sig = pair + turn(pair, 48) + turn(one, 96)
    half = 0.5 * dt * sig
    dec = (1.0 - half) / (1.0 + half)
    drv = dt / (1.0 + half)

    at_lane = lax.broadcasted_iota(jnp.int32, (8, wide), 1) + 8
    layer = at_lane - 24 * div24(at_lane)
    lanes[0] = spread(dec, 0, vregs)
    lanes[1] = spread(drv, 0, vregs)
    lanes[2] = jnp.where(layer == layers - 1, 0.0, 1.0)
    lanes[3] = jnp.where(layer == 0, 0.0, 1.0)

    half_lanes = lax.broadcasted_iota(jnp.int32, (1, 128), 1) < strokes

    def twice(x):
        return jnp.concatenate([x, x], axis=1)

    def column(x):
        return jnp.transpose(jnp.broadcast_to(x.astype(jnp.float32), (128, 2 * strokes)))

    cell = div24(at_lane[0:1]) - 11 + lon * (width // layers)
    total_lon = n_lon * (width // layers)
    cell = jnp.where(cell < 0, cell + total_lon, cell)
    cell = jnp.where(cell >= total_lon, cell - total_lon, cell)
    cell = jnp.where(layer[0:1] < CHANNEL, cell, -1).astype(jnp.float32)
    lon_of = jnp.concatenate([column(twice(f_lon[...]))] * vregs, axis=1)
    cells = (jnp.broadcast_to(cell, (2 * strokes, wide)) == lon_of).astype(jnp.float32)
    cells = cells.astype(jnp.bfloat16)
    row_no = lax.broadcasted_iota(jnp.int32, (live, 2 * strokes), 0) + (lat * rows - 8)
    in_row = jnp.where(
        row_no == twice(f_lat[...]),
        jnp.broadcast_to(twice(f_amp[...]), (live, 2 * strokes)),
        0.0,
    )
    steps_of = twice(f_step[...])
    left, right = [], []
    for s in range(STEPS):
        amps = jnp.where(steps_of == s, in_row, 0.0)
        upper = amps.astype(jnp.bfloat16).astype(jnp.float32)
        middle = (amps - upper).astype(jnp.bfloat16).astype(jnp.float32)
        left.append(jnp.where(half_lanes, upper, middle).astype(jnp.bfloat16))
        right.append(jnp.where(half_lanes, amps - upper - middle, 0.0).astype(jnp.bfloat16))
    total = None
    for part in (left, right):
        term = lax.dot_general(
            jnp.concatenate(part, axis=0), cells, (((1,), (0,)), ((), ())),
            preferred_element_type=jnp.float32,
        )
        total = term if total is None else total + term
    src[...] = total

    for k in range(2, n_lon):
        serve(k)
    for a, b in corners:
        if b < 0:
            def corner_last(a=a, b=b):
                pl.semaphore_wait(ack_cross.at[1], 1)
                corner_near(a, b).start()
                corner_far(a, b).start()
            crossing(a, b, True, corner_last)

    for k in range(1, n_lon):
        sum_copy(k).wait_recv()
    mean = sums_out[...]
    for k in range(1, n_lon):
        mean = mean + sums_in[k]
    strip[...] = mean
    for a in (-1, 1):
        pl.when(there(a))(lambda a=a: zone_copy(a).start())

    def unpack(x, band):
        y = jnp.where(lane < layers, turn(x, -layers * band), 0.0)
        p = y + turn(y, 24)
        return p + turn(p, 48) + turn(y, 96)

    edge = jnp.zeros((3, low, 128), jnp.float32)
    for z in (zon, zon_cap):
        z[:, 0:low, :] = edge
        z[:, low + rows:, :] = edge
    for f in range(3):
        for band in range(bands):
            own = unpack(mean[8 * f:8 * f + 8], band)
            for z in (zon, zon_cap):
                z[f, low + 8 * band:low + 8 * band + 8, :] = own

    for part in (0, 1):
        for side in (0, 1):
            for f in range(3 * part, 3 * part + 3):
                lon_copy(1 if side == 0 else -1, f).wait_recv()
            for a in (-1, 1):
                pl.when(shared(a))(
                    lambda a=a, side=side, part=part: relay_near(a, side, part).start()
                )
    for side in (0, 1):
        far_copy(1 if side == 0 else -1).wait_recv()
        for a in (-1, 1):
            pl.when(shared(a))(lambda a=a, side=side: relay_far(a, side).start())

    for a in (-1, 1):
        def take(a=a):
            lat_copy(a).wait_recv()
        pl.when(there(-a))(take)

        def take_corners(a=a):
            for b in (-1, 1):
                corner_near(a, b).wait_recv()
                corner_far(a, b).wait_recv()
        pl.when(across(-a))(take_corners)

        def take_relays(a=a):
            for side in (0, 1):
                for part in (0, 1):
                    relay_near(a, side, part).wait_recv()
                relay_far(a, side).wait_recv()
        pl.when(shared(-a))(take_relays)

    half = lax.broadcasted_iota(jnp.int32, (8, 128), 1)
    for r in range(0, tall, 8):
        here = slice(r, r + 8)
        one, two, three, outer = [far_in[0, n, here, :] for n in range(4)]
        inside = {
            EN: one, EE: turn(one, 64), EU: two, HN: turn(two, 64), HE: three, HR: turn(three, 64)
        }
        for m, f in enumerate(NINTH):
            inside[f] = jnp.where(half >= 64, inside[f], turn(outer, 40 - 24 * m))
        for f, x in inside.items():
            ext[f, here, 0:128] = x
        one, two, three, outer = [far_in[1, n, here, :] for n in range(4)]
        inside = {
            EN: one, EE: three, EU: two, HN: turn(three, 64), HE: outer, HR: turn(outer, 64)
        }
        for f, x in inside.items():
            ext[f, here, wide - 128:wide] = x

    def pole():
        last = pl.ds(low + rows - 8, 8)
        keep = jnp.broadcast_to(table[low + rows - 8:low + rows, C_KEEP:C_KEEP + 1], (8, wide))
        for f in (EE, EU, HN):
            ext[f, last, :] = keep * ext[f, last, :]
    pl.when(jnp.logical_not(there(1)))(pole)

    def zone_rows():
        for a in (-1, 1):
            def take_zone(a=a):
                zone_copy(a).wait_recv()
                i, row, band = (0, low - 8, bands - 1) if a > 0 else (1, low + rows, 0)
                for f in range(3):
                    zon[f, row:row + 8, :] = unpack(zone_in[i, 8 * f:8 * f + 8, :], band)
            pl.when(there(-a))(take_zone)

    outs = (o_en, o_ee, o_eu, o_hn, o_he, o_hr)
    march(dims, ext, buf, src, coef, lanes, zon, zon_cap, outs, o_zon, zone_rows)

    for a in (-1, 1):
        def sent(a=a):
            zone_copy(a).wait_send()
            lat_copy(a).wait_send()
        pl.when(there(a))(sent)

        def sent_corners(a=a):
            for b in (-1, 1):
                corner_near(a, b).wait_send()
                corner_far(a, b).wait_send()
        pl.when(across(a))(sent_corners)

        def sent_relays(a=a):
            for side in (0, 1):
                for part in (0, 1):
                    relay_near(a, side, part).wait_send()
                relay_far(a, side).wait_send()
        pl.when(shared(a))(sent_relays)
    for k in range(1, n_lon):
        sum_copy(k).wait_send()
    for b in (-1, 1):
        all_fields(lon_copy, b, "wait_send")
        far_copy(b).wait_send()


def march(dims, ext, buf, src, coef, lanes, zon, zon_cap, outs, o_zon, zone_rows):
    n_lat, n_lon, layers, dt, ly = dims
    tall, wide = buf.shape[1:]
    rows, width = tall - 2 * HALO_ROWS, wide - 2 * HALO_LANES
    groups = tall // 8
    own_groups = range(HALO_ROWS // 8, groups - HALO_ROWS // 8)
    low = HALO_ROWS
    lat = lax.axis_index("lat")
    own_r = slice(low, low + rows)
    z_dec, z_drv, z_top, z_bot = [lanes.at[i, :, HALO_LANES:HALO_LANES + 128] for i in (0, 1, 2, 3)]
    lane = lax.broadcasted_iota(jnp.int32, (rows, 128), 1)

    def record(s):
        both = jnp.where(lane < layers, zon[0, own_r, :], turn(zon[2, own_r, :], layers))
        both = jnp.transpose(both)
        o_zon[s, 0] = both[0:layers]
        o_zon[s, 1] = both[layers:2 * layers]

    def zonal_h(zon, span):
        for g in span:
            r = 8 * g
            east = zon[0, r:r + 8, :]
            zon[2, r:r + 8, :] = (
                zon[2, r:r + 8, :]
                - coef[C_AS, r:r + 8] * zon[0, r - 1:r + 7, :]
                + coef[C_BE, r:r + 8] * east
            )
            zon[1, r:r + 8, :] = zon[1, r:r + 8, :] - coef[C_DT, r:r + 8] * (
                z_top[...] * turn(east, -1) - east
            )

    def zonal_e(zon, span):
        for g in span:
            r = 8 * g
            up, north = zon[2, r:r + 8, :], zon[1, r:r + 8, :]
            zon[0, r:r + 8, :] = z_dec[...] * zon[0, r:r + 8, :] + z_drv[...] * (
                coef[C_LY, r:r + 8] * (zon[2, r + 1:r + 9, :] - up)
                - (north - z_bot[...] * turn(north, 1))
            )

    def magnetic(old, a, b, span, beyond, last=False):
        count = (b - a) // 128

        def rowc(c, g):
            return jnp.concatenate([coef[c, 8 * g:8 * g + 8]] * count, axis=1)

        top = lanes[2, :, a:b]
        for g in (*span, *beyond):
            r = 8 * g
            here, south = slice(r, r + 8), slice(r - 1, r + 7)
            e_n, e_e, e_u = old[EN, here, a:b], old[EE, here, a:b], old[EU, here, a:b]
            up = (
                old[HR, here, a:b]
                - rowc(C_AS, g) * old[EE, south, a:b]
                + rowc(C_BE, g) * e_e
                - rowc(C_CN, g) * (turn(e_n, -layers) - e_n)
            )
            if g in (own_groups[0], own_groups[-1]):
                row = lax.broadcasted_iota(jnp.int32, (8, b - a), 0) + (lat * rows - low + r)
                pole = 0 if g == own_groups[0] else n_lat * rows - 1
                up = jnp.where(row == pole, spread(zon_cap[2, here], a // 128, count), up)
            fresh = {HR: up}
            fresh[HE] = (
                old[HE, here, a:b]
                - (dt / ly) * (e_u - old[EU, south, a:b])
                + dt * (top * turn(e_n, -1) - e_n)
            )
            if g in span:
                fresh[HN] = (
                    old[HN, here, a:b]
                    - rowc(C_DU, g) * (e_u - turn(e_u, -layers))
                    - rowc(C_DT, g) * (top * turn(e_e, -1) - e_e)
                )
            for f, x in fresh.items():
                buf[f, here, a:b] = x
                if last and g in span:
                    outs[f][r - low:r - low + 8, :] = x[:, HALO_LANES - a:HALO_LANES - a + width]

    def electric(old, s, a, b, first, span, last=False):
        count = (b - first) // 128
        skip = first - a

        def rowc(c, g):
            return jnp.concatenate([coef[c, 8 * g:8 * g + 8]] * count, axis=1)

        def turned(x, by):
            return turn(x, by)[:, skip:]

        decay, drive, bot = [lanes[i, :, first:b] for i in (0, 1, 3)]
        for g in span:
            r = 8 * g
            here, north = slice(r, r + 8), slice(r + 1, r + 9)
            w_n, w_e, w_r = buf[HN, here, a:b], buf[HE, here, a:b], buf[HR, here, a:b]
            h_n, h_e, h_r = w_n[:, skip:], w_e[:, skip:], w_r[:, skip:]
            fresh = {}
            fresh[EN] = decay * old[EN, here, first:b] + drive * (
                h_e - bot * turned(w_e, 1) - rowc(C_GC, g) * (h_r - turned(w_r, layers))
            )
            fresh[EE] = decay * old[EE, here, first:b] + drive * (
                rowc(C_LY, g) * (buf[HR, north, first:b] - h_r) - (h_n - bot * turned(w_n, 1))
            )
            fresh[EU] = (
                decay * old[EU, here, first:b]
                + drive
                * (
                    rowc(C_IC, g) * h_e
                    - rowc(C_JN, g) * buf[HE, north, first:b]
                    + rowc(C_KL, g) * (h_n - turned(w_n, layers))
                    + src[pl.ds(pl.multiple_of(s * (rows + 16) + r - 8, 8), 8), first:b]
                )
            )

            for f, x in fresh.items():
                if last:
                    outs[f][r - low:r - low + 8, :] = x
                else:
                    buf[f, here, first:b] = x

    inner = range(1, groups - 1)

    def step(old, s, a, b, beyond):
        zonal_h(zon_cap, own_groups)
        magnetic(old, a, b, inner, beyond)
        zonal_e(zon_cap, own_groups)
        electric(old, s, a, b, a, inner)

    def means(s):
        record(s)
        zonal_h(zon, inner)
        zonal_e(zon, inner)

    middle = STEPS - 1 - STEPS // 2

    def early(s, carry):
        step(buf, s, 0, wide, ())
        return carry

    def late(s, carry):
        means(2 * (s - middle))
        means(2 * (s - middle) + 1)
        step(buf, s, 128, wide - 128, ())
        return carry

    step(ext, 0, 0, wide, (groups - 1,))
    for s in range(1, middle):
        early(s, 0)
    zone_rows()
    for s in range(middle, STEPS - 1):
        late(s, 0)
    record(STEPS - 1)
    zonal_h(zon_cap, own_groups)
    magnetic(buf, 128, wide - 128, own_groups, (own_groups[-1] + 1,), last=True)
    electric(buf, STEPS - 1, 128, wide - HALO_LANES, HALO_LANES, own_groups, last=True)


def hand_over(*refs):
    count = len(refs) // 2
    copies = [
        pltpu.make_async_copy(refs[i], refs[count + i], refs[-1].at[i]) for i in range(count)
    ]
    for copy in copies:
        copy.start()
    for copy in copies:
        copy.wait()


def body(
    efield_north,
    efield_east,
    efield_up,
    hfield_north,
    hfield_east,
    hfield_up,
    sigma_profile,
    flash_lat,
    flash_lon,
    flash_step,
    flash_amp,
):
    rows, width = efield_north.shape
    layers = sigma_profile.shape[0]
    n_lat, n_lon = lax.axis_size("lat"), lax.axis_size("lon")
    lat_count, lon_count = rows * n_lat, (width // layers) * n_lon
    dims = (
        n_lat,
        n_lon,
        layers,
        time_step(lat_count, lon_count),
        RADIUS_CELLS * math.pi / lat_count,
    )
    wide, tall = width + 2 * HALO_LANES, rows + 2 * HALO_ROWS
    f32 = jnp.float32
    vmem = pl.BlockSpec(memory_space=pltpu.VMEM)
    dma = pltpu.SemaphoreType.DMA
    hbm = pl.BlockSpec(memory_space=pltpu.HBM)
    strokes = flash_lat.shape[0]
    n_live = rows + 16
    outs = [jax.ShapeDtypeStruct((rows, width), f32)] * 6
    outs += [jax.ShapeDtypeStruct((STEPS, 2, layers, rows), f32)]
    held = pl.pallas_call(
        functools.partial(kernel, dims),
        out_shape=outs,
        in_specs=[hbm] * 12,
        out_specs=[vmem] * 7,
        scratch_shapes=[
            pltpu.VMEM((6, tall, wide), f32),
            pltpu.VMEM((2, 4, rows, 128), f32),
            pltpu.VMEM((2, 4, tall, 128), f32),
            pltpu.VMEM((6, tall, wide), f32),
            pltpu.VMEM((STEPS * n_live, wide), f32),
            pltpu.VMEM((10, tall, 128), f32),
            pltpu.VMEM((4, 8, wide), f32),
            pltpu.VMEM((3, tall, 128), f32),
            pltpu.VMEM((3, tall, 128), f32),
            pltpu.VMEM((24, 128), f32),
            pltpu.VMEM((n_lon, 24, 128), f32),
            pltpu.VMEM((2, 24, 128), f32),
            pltpu.VMEM((24, 128), f32),
            pltpu.VMEM((8, 128), f32),
            pltpu.VMEM((1, layers), f32),
            pltpu.VMEM((1, strokes), jnp.int32),
            pltpu.VMEM((1, strokes), jnp.int32),
            pltpu.VMEM((1, strokes), jnp.int32),
            pltpu.VMEM((1, strokes), f32),
            pltpu.VMEM((tall, 128), f32),
            dma((12,)),
            dma((12,)), dma((12,)), dma((2,)), dma((2,)), dma((4,)), dma((4,)),
            dma((16,)), dma((16,)), dma((24,)), dma((24,)),
            dma((n_lon,)), dma((n_lon,)), dma((2,)), dma((2,)),
            pltpu.SemaphoreType.REGULAR((n_lon,)),
            pltpu.SemaphoreType.REGULAR,
            pltpu.SemaphoreType.REGULAR((2,)),
        ],
        compiler_params=pltpu.CompilerParams(
            collective_id=0, has_side_effects=True, vmem_limit_bytes=VMEM_GRANT
        ),
    )(*(pltpu.with_memory_space_constraint(x, pltpu.HBM) for x in (
        efield_north,
        efield_east,
        efield_up,
        hfield_north,
        hfield_east,
        hfield_up,
        sigma_profile[None, :],
        flash_lat[None, :],
        flash_lon[None, :],
        flash_step[None, :],
        flash_amp[None, :],
        jnp.asarray(row_table(lat_count, lon_count)),
    )))
    results = pl.pallas_call(
        hand_over,
        out_shape=outs,
        in_specs=[vmem] * 7,
        out_specs=[hbm] * 7,
        scratch_shapes=[dma((7,))],
        compiler_params=pltpu.CompilerParams(vmem_limit_bytes=VMEM_GRANT),
    )(*held)
    return (*results[:6], jnp.transpose(results[6], (0, 1, 3, 2)))


def solution(mesh):
    fields = P("lat", "lon")
    return jax.shard_map(
        body,
        mesh=mesh,
        in_specs=(fields,) * 6 + (P(),) * 5,
        out_specs=(fields,) * 6 + (P(None, None, "lat", None),),
        check_vma=False,
    )
```

```python
import functools
import math

import jax
import jax.numpy as jnp
import numpy as np
from jax import lax
from jax.experimental import pallas as pl
from jax.experimental.pallas import tpu as pltpu
from jax.sharding import PartitionSpec as P

CHANNEL = 3
STEPS = 9
RADIUS_CELLS = 1529.0
COURANT = 0.9
VMEM_GRANT = 16 * 1024 * 1024

HALO_ROWS = 16
HALO_LANES = 256
MESH = pl.DeviceIdType.MESH
EN, EE, EU, HN, HE, HR = range(6)
(C_AS, C_BE, C_CN, C_DU, C_DT, C_GC, C_IC, C_JN, C_KL, C_LY) = range(10)
C_KEEP = 10
NINTH = (EN, EE, EU, HN, HR)


def time_step(lat_count, lon_count):
    lon_angle = 2.0 * math.pi / lon_count
    lat_angle = math.pi / lat_count
    narrowest = RADIUS_CELLS * lon_angle * math.sin(lat_angle)
    lat_length = RADIUS_CELLS * lat_angle
    return COURANT / math.sqrt(1.0 / narrowest**2 + 1.0 / lat_length**2 + 1.0)


def row_table(lat_count, lon_count):
    f = np.float32
    lon_angle = 2.0 * math.pi / lon_count
    lat_angle = math.pi / lat_count
    dt = time_step(lat_count, lon_count)
    ly = RADIUS_CELLS * math.pi / lat_count
    row = np.arange(lat_count)
    centre = f(-0.5 * math.pi) + (row.astype(f) + f(0.5)) * f(lat_angle)
    north = centre + f(0.5 * lat_angle)
    south = centre - f(0.5 * lat_angle)
    following = centre + f(lat_angle)
    pole = row == lat_count - 1
    scale = RADIUS_CELLS * lon_angle
    band = 2.0 * RADIUS_CELLS * scale * math.sin(0.5 * lat_angle)
    lc = f(scale) * np.cos(centre)
    ln = f(scale) * np.cos(following)
    le = np.where(pole, f(0), f(scale) * np.cos(north))
    ls = np.where(row == 0, f(0), f(scale) * np.cos(south))
    ls[-1] = le[-2]
    ac = f(band) * np.cos(centre)
    ae = np.where(pole, f(1), f(band) * np.cos(north))
    se = np.where(pole, f(1), le)
    keep = np.where(pole, f(0), f(1))
    table = np.zeros((lat_count + 2 * HALO_ROWS, 128), f)
    inner = table[HALO_ROWS:-HALO_ROWS]
    inner[:, C_AS] = dt * ls / ac
    inner[:, C_BE] = dt * le / ac
    inner[:, C_CN] = dt * ly / ac
    inner[:, C_DU] = keep * dt / se
    inner[:, C_DT] = keep * dt
    inner[:, C_GC] = 1.0 / lc
    inner[:, C_IC] = keep * lc / ae
    inner[:, C_JN] = keep * ln / ae
    inner[:, C_KL] = keep * ly / ae
    inner[:, C_LY] = keep / ly
    inner[:, C_KEEP] = keep
    return table


def turn(x, by):
    return pltpu.roll(x, by % x.shape[1], 1)


def div24(x):
    return lax.shift_right_logical(x * 2731, 16)


def spread(x, first, count):
    lane = lax.broadcasted_iota(jnp.int32, (8, 128), 1)
    out = []
    for v in range(first, first + count):
        off = (128 * v - HALO_LANES) % 24
        out.append(jnp.where(lane < 96, turn(x, -off), turn(x, 24 - off)))
    return jnp.concatenate(out, axis=1)


def kernel(
    dims,
    en, ee, eu, hn, he, hr, h_sigma, h_lat, h_lon, h_step, h_amp, h_table,
    o_en, o_ee, o_eu, o_hn, o_he, o_hr, o_zon,
    ext, far_out, far_in, buf, src, coef, lanes, zon, zon_cap,
    sums_out, sums_in, zone_in, strip, small, sigma, f_lat, f_lon, f_step, f_amp, table,
    load, send_b, recv_b, send_f, recv_f, send_l, recv_l, send_c, recv_c, send_r, recv_r,
    send_s, recv_s, send_z, recv_z,
    ack_lon, ack_lat, ack_cross,
):
    n_lat, n_lon, layers, dt, ly = dims
    fields = (en, ee, eu, hn, he, hr)
    rows, width = en.shape
    strokes = h_lat.shape[1]
    wide = width + 2 * HALO_LANES
    tall = rows + 2 * HALO_ROWS
    vregs = wide // 128
    live = rows + 16
    low = HALO_ROWS
    lat, lon = lax.axis_index("lat"), lax.axis_index("lon")
    own_r = pl.ds(low, rows)
    own_c = pl.ds(HALO_LANES, width)

    def at(a, b):
        row = jnp.clip(lat + a, 0, n_lat - 1) if a else lat
        return {"lat": row, "lon": lax.rem(lon + b + n_lon, n_lon)}

    def there(a):
        return lat + a >= 0 if a < 0 else lat + a < n_lat

    def shared(a):
        return lax.rem(lat, 2) == (0 if a > 0 else 1)

    def across(a):
        return jnp.logical_and(there(a), jnp.logical_not(shared(a)))

    def signal(sem, a, b):
        pl.semaphore_signal(sem, inc=1, device_id=at(a, b), device_id_type=MESH)

    barrier = pltpu.get_barrier_semaphore()
    for k in range(1, n_lon):
        pl.when(lon + k < n_lon)(lambda k=k: signal(barrier, 0, k))
    pl.when(there(1))(lambda: signal(barrier, 1, 0))

    def crossing(a, b, later, act):
        wraps = lon == (n_lon - 1 if b > 0 else 0)
        is_later = jnp.logical_not(wraps) if b > 0 else wraps
        wanted = is_later if later else jnp.logical_not(is_later)
        pl.when(jnp.logical_and(across(a), wanted))(act)

    corners = [(a, b) for a in (-1, 1) for b in (-1, 1)]
    for a, b in corners:
        crossing(a, b, True, lambda a=a, b=b: signal(barrier, a, b))

    loads = [
        pltpu.make_async_copy(x, ext.at[f, own_r, own_c], load.at[f])
        for f, x in enumerate(fields)
    ]
    here_rows = h_table.at[pl.ds(pl.multiple_of(lat * rows, 8), tall), :]
    pairs = (
        (here_rows, table), (h_sigma, sigma), (h_lat, f_lat), (h_lon, f_lon),
        (h_step, f_step), (h_amp, f_amp),
    )
    loads += [pltpu.make_async_copy(x, y, load.at[6 + i]) for i, (x, y) in enumerate(pairs)]
    for copy in loads:
        copy.start()

    def lon_copy(b, f):
        i = f if b > 0 else 6 + f
        cut = pl.ds(width - 128, 128) if b > 0 else pl.ds(0, 128)
        land = pl.ds(HALO_LANES - 128, 128) if b > 0 else pl.ds(HALO_LANES + width, 128)
        return pltpu.make_async_remote_copy(
            src_ref=fields[f].at[:, cut],
            dst_ref=ext.at[f, own_r, land],
            send_sem=send_b.at[i],
            recv_sem=recv_b.at[i],
            device_id=at(0, b),
            device_id_type=MESH,
        )

    def far_copy(b):
        i = 0 if b > 0 else 1
        return pltpu.make_async_remote_copy(
            src_ref=far_out.at[i],
            dst_ref=far_in.at[i, :, own_r, :],
            send_sem=send_f.at[i],
            recv_sem=recv_f.at[i],
            device_id=at(0, b),
            device_id_type=MESH,
        )

    class Pieces:
        def __init__(self, a, parts, here, there, sends, recvs, i, b=0, off=0):
            shift = rows if a > 0 else -rows
            self.copies = [
                pltpu.make_async_remote_copy(
                    src_ref=here(pl.ds(row - off, count), pl.ds(col, span)),
                    dst_ref=there(pl.ds(row - shift, count), pl.ds(land, span)),
                    send_sem=sends.at[2 * i + n],
                    recv_sem=recvs.at[2 * i + n],
                    device_id=at(a, b),
                    device_id_type=MESH,
                )
                for n, (row, count, col, land, span) in enumerate(parts)
            ]

        def start(self):
            for copy in self.copies:
                copy.start()

        def wait_recv(self):
            for copy in self.copies:
                copy.wait_recv()

        def wait_send(self):
            for copy in self.copies:
                copy.wait_send()

    def nine(a, col, land, span):
        first, ninth = (low + rows - 8, low + rows - STEPS) if a > 0 else (low, low + STEPS - 1)
        return (first, 8, col, land, span), (ninth, 1, col, land, span)

    def whole(r, c):
        return ext.at[:, r, c]

    def lat_copy(a):
        parts = nine(a, HALO_LANES, HALO_LANES, width)
        return Pieces(a, parts, whole, whole, send_l, recv_l, 0 if a > 0 else 1)

    def corner_near(a, b):
        col = HALO_LANES + width - 128 if b > 0 else HALO_LANES
        land = HALO_LANES - 128 if b > 0 else HALO_LANES + width
        parts = nine(a, col, land, 128)
        parts = parts if a == b else parts[:1]
        return Pieces(a, parts, whole, whole, send_c, recv_c, corners.index((a, b)), b)

    def corner_far(a, b):
        i = 0 if b > 0 else 1
        parts = nine(a, 0, 0, 128)
        if a != b:
            parts = ((low + rows - 4 if a > 0 else low, 4, 0, 0, 128),)

        def here(r, c):
            return far_out.at[i, :, r, c]

        def there(r, c):
            return far_in.at[i, :, r, c]
        return Pieces(
            a, parts, here, there, send_c, recv_c, 4 + corners.index((a, b)), b, off=low
        )

    def relay_near(a, side, part):
        col = HALO_LANES - 128 if side == 0 else HALO_LANES + width
        i = part + 2 * side + (0 if a > 0 else 4)

        def these(r, c):
            return ext.at[pl.ds(3 * part, 3), r, c]
        return Pieces(a, nine(a, col, col, 128), these, these, send_r, recv_r, i)

    def relay_far(a, side):
        def these(r, c):
            return far_in.at[side, :, r, c]
        i = 8 + side + (0 if a > 0 else 2)
        return Pieces(a, nine(a, 0, 0, 128), these, these, send_r, recv_r, i)

    def sum_copy(k):
        return pltpu.make_async_remote_copy(
            src_ref=sums_out,
            dst_ref=sums_in.at[k],
            send_sem=send_s.at[k],
            recv_sem=recv_s.at[k],
            device_id=at(0, k),
            device_id_type=MESH,
        )

    def zone_copy(a):
        i = 0 if a > 0 else 1
        return pltpu.make_async_remote_copy(
            src_ref=strip,
            dst_ref=zone_in.at[i],
            send_sem=send_z.at[i],
            recv_sem=recv_z.at[i],
            device_id=at(a, 0),
            device_id_type=MESH,
        )

    def all_fields(make, side, act):
        for f in range(6):
            getattr(make(side, f), act)()

    crossed = jnp.where(lon == n_lon - 1, 2, jnp.where(lon == 0, 0, 1))
    crossed = jnp.where(jnp.logical_or(across(-1), across(1)), crossed, 0)
    earlier = lon + (lat > 0).astype(jnp.int32) + crossed
    pl.when(earlier > 0)(lambda: pl.semaphore_wait(barrier, earlier))
    for k in range(n_lon - 1, 0, -1):
        pl.when(lon - k >= 0)(lambda k=k: signal(ack_lon.at[k], 0, -k))
    pl.when(there(-1))(lambda: signal(ack_lat, -1, 0))
    for a, b in corners:
        crossing(a, b, False, lambda a=a, b=b: signal(ack_cross.at[0 if b < 0 else 1], a, b))

    pl.when(lon == n_lon - 1)(lambda: all_fields(lon_copy, 1, "start"))
    pl.when(lon > 0)(lambda: all_fields(lon_copy, -1, "start"))

    for a, first in ((-1, 0), (1, low + rows)):
        def clear(first=first):
            ext[:, first:first + low, :] = jnp.zeros((6, low, wide), jnp.float32)
            far_in[:, :, first:first + low, :] = jnp.zeros((2, 4, low, 128), jnp.float32)
        pl.when(jnp.logical_not(there(a)))(clear)

    for copy in loads[:7]:
        copy.wait()

    pl.when(there(-1))(lambda: lat_copy(-1).start())
    for a, b in corners:
        crossing(a, b, False, lambda a=a, b=b: corner_near(a, b).start())

    half = lax.broadcasted_iota(jnp.int32, (rows, 128), 1)
    mid = [ext[f, own_r, pl.ds(HALO_LANES + 128, 128)] for f in range(6)]
    end = [ext[f, own_r, pl.ds(HALO_LANES + width - 256, 128)] for f in range(6)]
    far_out[0, 0] = jnp.where(half >= 64, end[EN], turn(end[EE], 64))
    far_out[0, 1] = jnp.where(half >= 64, end[EU], turn(end[HN], 64))
    far_out[0, 2] = jnp.where(half >= 64, end[HE], turn(end[HR], 64))
    outer = turn(end[NINTH[0]], -40)
    for m in range(1, len(NINTH)):
        outer = jnp.where(half < 24 * m, outer, turn(end[NINTH[m]], 24 * m - 40))
    far_out[0, 3] = outer
    far_out[1, 0] = mid[EN]
    far_out[1, 1] = mid[EU]
    far_out[1, 2] = jnp.where(half < 64, mid[EE], turn(mid[HN], 64))
    far_out[1, 3] = jnp.where(half < 64, mid[HE], turn(mid[HR], 64))
    for a, b in corners:
        crossing(a, b, False, lambda a=a, b=b: corner_far(a, b).start())
    pl.when(lon == n_lon - 1)(lambda: far_copy(1).start())
    pl.when(lon > 0)(lambda: far_copy(-1).start())

    def fold(x):
        for by in (width // 2, width // 4, width // 8, width // 16):
            x = x + turn(x, by)
        return x[:, :128] * (1.0 / (n_lon * (width // layers)))

    lane = lax.broadcasted_iota(jnp.int32, (8, 128), 1)
    kept = jnp.broadcast_to(table[low:low + rows, C_KEEP:C_KEEP + 1], (rows, 128))
    bands = rows // 8
    for n, f in enumerate((EE, HN, HR)):
        folded = fold(ext[f, own_r, own_c])
        if f != HR:
            folded = kept * folded
        packed = folded[0:8]
        for band in range(1, bands):
            packed = jnp.where(lane < layers * band, packed, folded[8 * band:8 * band + 8])
        sums_out[8 * n:8 * n + 8, :] = packed
    for k in range(1, n_lon):
        pl.when(lon + k >= n_lon)(lambda k=k: sum_copy(k).start())

    def to_north():
        pl.semaphore_wait(ack_lat, 1)
        lat_copy(1).start()
    pl.when(there(1))(to_north)

    def serve(k):
        def to_later():
            pl.semaphore_wait(ack_lon.at[k], 1)
            if k == 1:
                all_fields(lon_copy, 1, "start")
                far_copy(1).start()
            if k == n_lon - 1:
                all_fields(lon_copy, -1, "start")
                far_copy(-1).start()
            sum_copy(k).start()
        pl.when(lon + k < n_lon)(to_later)

    serve(1)
    for a, b in corners:
        if b > 0:
            def corner_later(a=a, b=b):
                pl.semaphore_wait(ack_cross.at[0], 1)
                corner_near(a, b).start()
                corner_far(a, b).start()
            crossing(a, b, True, corner_later)
    for copy in loads[7:]:
        copy.wait()
    rows_tab = table[...]
    for c in range(10):
        coef[c] = jnp.broadcast_to(rows_tab[:, c:c + 1], (tall, 128))
    small[...] = jnp.zeros((8, 128), jnp.float32)
    small[0:1, 0:layers] = sigma[...]
    one = jnp.broadcast_to(small[0:1, :], (8, 128))
    pair = one + turn(one, 24)
    sig = pair + turn(pair, 48) + turn(one, 96)
    half = 0.5 * dt * sig
    dec = (1.0 - half) / (1.0 + half)
    drv = dt / (1.0 + half)

    at_lane = lax.broadcasted_iota(jnp.int32, (8, wide), 1) + 8
    layer = at_lane - 24 * div24(at_lane)
    lanes[0] = spread(dec, 0, vregs)
    lanes[1] = spread(drv, 0, vregs)
    lanes[2] = jnp.where(layer == layers - 1, 0.0, 1.0)
    lanes[3] = jnp.where(layer == 0, 0.0, 1.0)

    half_lanes = lax.broadcasted_iota(jnp.int32, (1, 128), 1) < strokes

    def twice(x):
        return jnp.concatenate([x, x], axis=1)

    def column(x):
        return jnp.transpose(jnp.broadcast_to(x.astype(jnp.float32), (128, 2 * strokes)))

    cell = div24(at_lane[0:1]) - 11 + lon * (width // layers)
    total_lon = n_lon * (width // layers)
    cell = jnp.where(cell < 0, cell + total_lon, cell)
    cell = jnp.where(cell >= total_lon, cell - total_lon, cell)
    cell = jnp.where(layer[0:1] < CHANNEL, cell, -1).astype(jnp.float32)
    lon_of = jnp.concatenate([column(twice(f_lon[...]))] * vregs, axis=1)
    cells = (jnp.broadcast_to(cell, (2 * strokes, wide)) == lon_of).astype(jnp.float32)
    cells = cells.astype(jnp.bfloat16)
    row_no = lax.broadcasted_iota(jnp.int32, (live, 2 * strokes), 0) + (lat * rows - 8)
    in_row = jnp.where(
        row_no == twice(f_lat[...]),
        jnp.broadcast_to(twice(f_amp[...]), (live, 2 * strokes)),
        0.0,
    )
    steps_of = twice(f_step[...])
    left, right = [], []
    for s in range(STEPS):
        amps = jnp.where(steps_of == s, in_row, 0.0)
        upper = amps.astype(jnp.bfloat16).astype(jnp.float32)
        middle = (amps - upper).astype(jnp.bfloat16).astype(jnp.float32)
        left.append(jnp.where(half_lanes, upper, middle).astype(jnp.bfloat16))
        right.append(jnp.where(half_lanes, amps - upper - middle, 0.0).astype(jnp.bfloat16))
    total = None
    for part in (left, right):
        term = lax.dot_general(
            jnp.concatenate(part, axis=0), cells, (((1,), (0,)), ((), ())),
            preferred_element_type=jnp.float32,
        )
        total = term if total is None else total + term
    src[...] = total

    for k in range(2, n_lon):
        serve(k)
    for a, b in corners:
        if b < 0:
            def corner_last(a=a, b=b):
                pl.semaphore_wait(ack_cross.at[1], 1)
                corner_near(a, b).start()
                corner_far(a, b).start()
            crossing(a, b, True, corner_last)

    for part in (0, 1):
        for side in (0, 1):
            for f in range(3 * part, 3 * part + 3):
                lon_copy(1 if side == 0 else -1, f).wait_recv()
            for a in (-1, 1):
                pl.when(shared(a))(
                    lambda a=a, side=side, part=part: relay_near(a, side, part).start()
                )
    for side in (0, 1):
        far_copy(1 if side == 0 else -1).wait_recv()
        for a in (-1, 1):
            pl.when(shared(a))(lambda a=a, side=side: relay_far(a, side).start())

    for k in range(1, n_lon):
        sum_copy(k).wait_recv()
    mean = sums_out[...]
    for k in range(1, n_lon):
        mean = mean + sums_in[k]
    strip[...] = mean
    for a in (-1, 1):
        pl.when(there(a))(lambda a=a: zone_copy(a).start())

    def unpack(x, band):
        y = jnp.where(lane < layers, turn(x, -layers * band), 0.0)
        p = y + turn(y, 24)
        return p + turn(p, 48) + turn(y, 96)

    edge = jnp.zeros((3, low, 128), jnp.float32)
    for z in (zon, zon_cap):
        z[:, 0:low, :] = edge
        z[:, low + rows:, :] = edge
    for f in range(3):
        for band in range(bands):
            own = unpack(mean[8 * f:8 * f + 8], band)
            for z in (zon, zon_cap):
                z[f, low + 8 * band:low + 8 * band + 8, :] = own

    half = lax.broadcasted_iota(jnp.int32, (8, 128), 1)

    def unpack_far(r):
        here = slice(r, r + 8)
        one, two, three, outer = [far_in[0, n, here, :] for n in range(4)]
        inside = {
            EN: one, EE: turn(one, 64), EU: two, HN: turn(two, 64), HE: three, HR: turn(three, 64)
        }
        for m, f in enumerate(NINTH):
            inside[f] = jnp.where(half >= 64, inside[f], turn(outer, 40 - 24 * m))
        for f, x in inside.items():
            ext[f, here, 0:128] = x
        one, two, three, outer = [far_in[1, n, here, :] for n in range(4)]
        inside = {
            EN: one, EE: three, EU: two, HN: turn(three, 64), HE: outer, HR: turn(outer, 64)
        }
        for f, x in inside.items():
            ext[f, here, wide - 128:wide] = x

    for r in range(low, low + rows, 8):
        unpack_far(r)

    for a in (-1, 1):
        def take(a=a):
            lat_copy(a).wait_recv()
        pl.when(there(-a))(take)

        def take_corners(a=a):
            for b in (-1, 1):
                corner_near(a, b).wait_recv()
                corner_far(a, b).wait_recv()
        pl.when(across(-a))(take_corners)

        def take_relays(a=a):
            for side in (0, 1):
                for part in (0, 1):
                    relay_near(a, side, part).wait_recv()
                relay_far(a, side).wait_recv()
        pl.when(shared(-a))(take_relays)

    for r in (*range(0, low, 8), *range(low + rows, tall, 8)):
        unpack_far(r)

    def pole():
        last = pl.ds(low + rows - 8, 8)
        keep = jnp.broadcast_to(table[low + rows - 8:low + rows, C_KEEP:C_KEEP + 1], (8, wide))
        for f in (EE, EU, HN):
            ext[f, last, :] = keep * ext[f, last, :]
    pl.when(jnp.logical_not(there(1)))(pole)

    def zone_rows():
        for a in (-1, 1):
            def take_zone(a=a):
                zone_copy(a).wait_recv()
                i, row, band = (0, low - 8, bands - 1) if a > 0 else (1, low + rows, 0)
                for f in range(3):
                    zon[f, row:row + 8, :] = unpack(zone_in[i, 8 * f:8 * f + 8, :], band)
            pl.when(there(-a))(take_zone)

    outs = (o_en, o_ee, o_eu, o_hn, o_he, o_hr)
    march(dims, ext, buf, src, coef, lanes, zon, zon_cap, outs, o_zon, zone_rows)

    for a in (-1, 1):
        def sent(a=a):
            zone_copy(a).wait_send()
            lat_copy(a).wait_send()
        pl.when(there(a))(sent)

        def sent_corners(a=a):
            for b in (-1, 1):
                corner_near(a, b).wait_send()
                corner_far(a, b).wait_send()
        pl.when(across(a))(sent_corners)

        def sent_relays(a=a):
            for side in (0, 1):
                for part in (0, 1):
                    relay_near(a, side, part).wait_send()
                relay_far(a, side).wait_send()
        pl.when(shared(a))(sent_relays)
    for k in range(1, n_lon):
        sum_copy(k).wait_send()
    for b in (-1, 1):
        all_fields(lon_copy, b, "wait_send")
        far_copy(b).wait_send()


def march(dims, ext, buf, src, coef, lanes, zon, zon_cap, outs, o_zon, zone_rows):
    n_lat, n_lon, layers, dt, ly = dims
    tall, wide = buf.shape[1:]
    rows, width = tall - 2 * HALO_ROWS, wide - 2 * HALO_LANES
    groups = tall // 8
    own_groups = range(HALO_ROWS // 8, groups - HALO_ROWS // 8)
    low = HALO_ROWS
    lat = lax.axis_index("lat")
    own_r = slice(low, low + rows)
    z_dec, z_drv, z_top, z_bot = [lanes.at[i, :, HALO_LANES:HALO_LANES + 128] for i in (0, 1, 2, 3)]
    lane = lax.broadcasted_iota(jnp.int32, (rows, 128), 1)

    def record(s):
        both = jnp.where(lane < layers, zon[0, own_r, :], turn(zon[2, own_r, :], layers))
        both = jnp.transpose(both)
        o_zon[s, 0] = both[0:layers]
        o_zon[s, 1] = both[layers:2 * layers]

    def zonal_h(zon, span):
        for g in span:
            r = 8 * g
            east = zon[0, r:r + 8, :]
            zon[2, r:r + 8, :] = (
                zon[2, r:r + 8, :]
                - coef[C_AS, r:r + 8] * zon[0, r - 1:r + 7, :]
                + coef[C_BE, r:r + 8] * east
            )
            zon[1, r:r + 8, :] = zon[1, r:r + 8, :] - coef[C_DT, r:r + 8] * (
                z_top[...] * turn(east, -1) - east
            )

    def zonal_e(zon, span):
        for g in span:
            r = 8 * g
            up, north = zon[2, r:r + 8, :], zon[1, r:r + 8, :]
            zon[0, r:r + 8, :] = z_dec[...] * zon[0, r:r + 8, :] + z_drv[...] * (
                coef[C_LY, r:r + 8] * (zon[2, r + 1:r + 9, :] - up)
                - (north - z_bot[...] * turn(north, 1))
            )

    def magnetic(old, a, b, span, beyond, last=False):
        count = (b - a) // 128

        def rowc(c, g):
            return jnp.concatenate([coef[c, 8 * g:8 * g + 8]] * count, axis=1)

        top = lanes[2, :, a:b]
        for g in (*span, *beyond):
            r = 8 * g
            here, south = slice(r, r + 8), slice(r - 1, r + 7)
            e_n, e_e, e_u = old[EN, here, a:b], old[EE, here, a:b], old[EU, here, a:b]
            up = (
                old[HR, here, a:b]
                - rowc(C_AS, g) * old[EE, south, a:b]
                + rowc(C_BE, g) * e_e
                - rowc(C_CN, g) * (turn(e_n, -layers) - e_n)
            )
            if g in (own_groups[0], own_groups[-1]):
                row = lax.broadcasted_iota(jnp.int32, (8, b - a), 0) + (lat * rows - low + r)
                pole = 0 if g == own_groups[0] else n_lat * rows - 1
                up = jnp.where(row == pole, spread(zon_cap[2, here], a // 128, count), up)
            fresh = {HR: up}
            fresh[HE] = (
                old[HE, here, a:b]
                - (dt / ly) * (e_u - old[EU, south, a:b])
                + dt * (top * turn(e_n, -1) - e_n)
            )
            if g in span:
                fresh[HN] = (
                    old[HN, here, a:b]
                    - rowc(C_DU, g) * (e_u - turn(e_u, -layers))
                    - rowc(C_DT, g) * (top * turn(e_e, -1) - e_e)
                )
            for f, x in fresh.items():
                buf[f, here, a:b] = x
                if last and g in span:
                    outs[f][r - low:r - low + 8, :] = x[:, HALO_LANES - a:HALO_LANES - a + width]

    def electric(old, s, a, b, first, span, last=False):
        count = (b - first) // 128
        skip = first - a

        def rowc(c, g):
            return jnp.concatenate([coef[c, 8 * g:8 * g + 8]] * count, axis=1)

        def turned(x, by):
            return turn(x, by)[:, skip:]

        decay, drive, bot = [lanes[i, :, first:b] for i in (0, 1, 3)]
        for g in span:
            r = 8 * g
            here, north = slice(r, r + 8), slice(r + 1, r + 9)
            w_n, w_e, w_r = buf[HN, here, a:b], buf[HE, here, a:b], buf[HR, here, a:b]
            h_n, h_e, h_r = w_n[:, skip:], w_e[:, skip:], w_r[:, skip:]
            fresh = {}
            fresh[EN] = decay * old[EN, here, first:b] + drive * (
                h_e - bot * turned(w_e, 1) - rowc(C_GC, g) * (h_r - turned(w_r, layers))
            )
            fresh[EE] = decay * old[EE, here, first:b] + drive * (
                rowc(C_LY, g) * (buf[HR, north, first:b] - h_r) - (h_n - bot * turned(w_n, 1))
            )
            fresh[EU] = (
                decay * old[EU, here, first:b]
                + drive
                * (
                    rowc(C_IC, g) * h_e
                    - rowc(C_JN, g) * buf[HE, north, first:b]
                    + rowc(C_KL, g) * (h_n - turned(w_n, layers))
                    + src[pl.ds(pl.multiple_of(s * (rows + 16) + r - 8, 8), 8), first:b]
                )
            )

            for f, x in fresh.items():
                if last:
                    outs[f][r - low:r - low + 8, :] = x
                else:
                    buf[f, here, first:b] = x

    inner = range(1, groups - 1)

    def step(old, s, a, b, beyond):
        zonal_h(zon_cap, own_groups)
        magnetic(old, a, b, inner, beyond)
        zonal_e(zon_cap, own_groups)
        electric(old, s, a, b, a, inner)

    def means(s):
        record(s)
        zonal_h(zon, inner)
        zonal_e(zon, inner)

    middle = STEPS - 1 - STEPS // 2

    def early(s, carry):
        step(buf, s, 0, wide, ())
        return carry

    def late(s, carry):
        means(2 * (s - middle))
        means(2 * (s - middle) + 1)
        step(buf, s, 128, wide - 128, ())
        return carry

    step(ext, 0, 0, wide, (groups - 1,))
    for s in range(1, middle):
        early(s, 0)
    zone_rows()
    for s in range(middle, STEPS - 1):
        late(s, 0)
    record(STEPS - 1)
    zonal_h(zon_cap, own_groups)
    magnetic(buf, 128, wide - 128, own_groups, (own_groups[-1] + 1,), last=True)
    electric(buf, STEPS - 1, 128, wide - HALO_LANES, HALO_LANES, own_groups, last=True)


def hand_over(*refs):
    count = len(refs) // 2
    copies = [
        pltpu.make_async_copy(refs[i], refs[count + i], refs[-1].at[i]) for i in range(count)
    ]
    for copy in copies:
        copy.start()
    for copy in copies:
        copy.wait()


def body(
    efield_north,
    efield_east,
    efield_up,
    hfield_north,
    hfield_east,
    hfield_up,
    sigma_profile,
    flash_lat,
    flash_lon,
    flash_step,
    flash_amp,
):
    rows, width = efield_north.shape
    layers = sigma_profile.shape[0]
    n_lat, n_lon = lax.axis_size("lat"), lax.axis_size("lon")
    lat_count, lon_count = rows * n_lat, (width // layers) * n_lon
    dims = (
        n_lat,
        n_lon,
        layers,
        time_step(lat_count, lon_count),
        RADIUS_CELLS * math.pi / lat_count,
    )
    wide, tall = width + 2 * HALO_LANES, rows + 2 * HALO_ROWS
    f32 = jnp.float32
    vmem = pl.BlockSpec(memory_space=pltpu.VMEM)
    dma = pltpu.SemaphoreType.DMA
    hbm = pl.BlockSpec(memory_space=pltpu.HBM)
    strokes = flash_lat.shape[0]
    n_live = rows + 16
    outs = [jax.ShapeDtypeStruct((rows, width), f32)] * 6
    outs += [jax.ShapeDtypeStruct((STEPS, 2, layers, rows), f32)]
    held = pl.pallas_call(
        functools.partial(kernel, dims),
        out_shape=outs,
        in_specs=[hbm] * 12,
        out_specs=[vmem] * 7,
        scratch_shapes=[
            pltpu.VMEM((6, tall, wide), f32),
            pltpu.VMEM((2, 4, rows, 128), f32),
            pltpu.VMEM((2, 4, tall, 128), f32),
            pltpu.VMEM((6, tall, wide), f32),
            pltpu.VMEM((STEPS * n_live, wide), f32),
            pltpu.VMEM((10, tall, 128), f32),
            pltpu.VMEM((4, 8, wide), f32),
            pltpu.VMEM((3, tall, 128), f32),
            pltpu.VMEM((3, tall, 128), f32),
            pltpu.VMEM((24, 128), f32),
            pltpu.VMEM((n_lon, 24, 128), f32),
            pltpu.VMEM((2, 24, 128), f32),
            pltpu.VMEM((24, 128), f32),
            pltpu.VMEM((8, 128), f32),
            pltpu.VMEM((1, layers), f32),
            pltpu.VMEM((1, strokes), jnp.int32),
            pltpu.VMEM((1, strokes), jnp.int32),
            pltpu.VMEM((1, strokes), jnp.int32),
            pltpu.VMEM((1, strokes), f32),
            pltpu.VMEM((tall, 128), f32),
            dma((12,)),
            dma((12,)), dma((12,)), dma((2,)), dma((2,)), dma((4,)), dma((4,)),
            dma((16,)), dma((16,)), dma((24,)), dma((24,)),
            dma((n_lon,)), dma((n_lon,)), dma((2,)), dma((2,)),
            pltpu.SemaphoreType.REGULAR((n_lon,)),
            pltpu.SemaphoreType.REGULAR,
            pltpu.SemaphoreType.REGULAR((2,)),
        ],
        compiler_params=pltpu.CompilerParams(
            collective_id=0, has_side_effects=True, vmem_limit_bytes=VMEM_GRANT
        ),
    )(*(pltpu.with_memory_space_constraint(x, pltpu.HBM) for x in (
        efield_north,
        efield_east,
        efield_up,
        hfield_north,
        hfield_east,
        hfield_up,
        sigma_profile[None, :],
        flash_lat[None, :],
        flash_lon[None, :],
        flash_step[None, :],
        flash_amp[None, :],
        jnp.asarray(row_table(lat_count, lon_count)),
    )))
    results = pl.pallas_call(
        hand_over,
        out_shape=outs,
        in_specs=[vmem] * 7,
        out_specs=[hbm] * 7,
        scratch_shapes=[dma((7,))],
        compiler_params=pltpu.CompilerParams(vmem_limit_bytes=VMEM_GRANT),
    )(*held)
    return (*results[:6], jnp.transpose(results[6], (0, 1, 3, 2)))


def solution(mesh):
    fields = P("lat", "lon")
    return jax.shard_map(
        body,
        mesh=mesh,
        in_specs=(fields,) * 6 + (P(),) * 5,
        out_specs=(fields,) * 6 + (P(None, None, "lat", None),),
        check_vma=False,
    )
```

```python
import functools
import math

import jax
import jax.numpy as jnp
import numpy as np
from jax import lax
from jax.experimental import pallas as pl
from jax.experimental.pallas import tpu as pltpu
from jax.sharding import PartitionSpec as P

CHANNEL = 3
STEPS = 9
RADIUS_CELLS = 1529.0
COURANT = 0.9
VMEM_GRANT = 16 * 1024 * 1024

HALO_ROWS = 16
HALO_LANES = 256
MESH = pl.DeviceIdType.MESH
EN, EE, EU, HN, HE, HR = range(6)
(C_AS, C_BE, C_CN, C_DU, C_DT, C_GC, C_IC, C_JN, C_KL, C_LY) = range(10)
C_KEEP = 10
NINTH = (EN, EE, EU, HN, HR)


def time_step(lat_count, lon_count):
    lon_angle = 2.0 * math.pi / lon_count
    lat_angle = math.pi / lat_count
    narrowest = RADIUS_CELLS * lon_angle * math.sin(lat_angle)
    lat_length = RADIUS_CELLS * lat_angle
    return COURANT / math.sqrt(1.0 / narrowest**2 + 1.0 / lat_length**2 + 1.0)


def row_table(lat_count, lon_count):
    f = np.float32
    lon_angle = 2.0 * math.pi / lon_count
    lat_angle = math.pi / lat_count
    dt = time_step(lat_count, lon_count)
    ly = RADIUS_CELLS * math.pi / lat_count
    row = np.arange(lat_count)
    centre = f(-0.5 * math.pi) + (row.astype(f) + f(0.5)) * f(lat_angle)
    north = centre + f(0.5 * lat_angle)
    south = centre - f(0.5 * lat_angle)
    following = centre + f(lat_angle)
    pole = row == lat_count - 1
    scale = RADIUS_CELLS * lon_angle
    band = 2.0 * RADIUS_CELLS * scale * math.sin(0.5 * lat_angle)
    lc = f(scale) * np.cos(centre)
    ln = f(scale) * np.cos(following)
    le = np.where(pole, f(0), f(scale) * np.cos(north))
    ls = np.where(row == 0, f(0), f(scale) * np.cos(south))
    ls[-1] = le[-2]
    ac = f(band) * np.cos(centre)
    ae = np.where(pole, f(1), f(band) * np.cos(north))
    se = np.where(pole, f(1), le)
    keep = np.where(pole, f(0), f(1))
    table = np.zeros((lat_count + 2 * HALO_ROWS, 128), f)
    inner = table[HALO_ROWS:-HALO_ROWS]
    inner[:, C_AS] = dt * ls / ac
    inner[:, C_BE] = dt * le / ac
    inner[:, C_CN] = dt * ly / ac
    inner[:, C_DU] = keep * dt / se
    inner[:, C_DT] = keep * dt
    inner[:, C_GC] = 1.0 / lc
    inner[:, C_IC] = keep * lc / ae
    inner[:, C_JN] = keep * ln / ae
    inner[:, C_KL] = keep * ly / ae
    inner[:, C_LY] = keep / ly
    inner[:, C_KEEP] = keep
    return table


def turn(x, by):
    return pltpu.roll(x, by % x.shape[1], 1)


def div24(x):
    return lax.shift_right_logical(x * 2731, 16)


def spread(x, first, count):
    lane = lax.broadcasted_iota(jnp.int32, (8, 128), 1)
    out = []
    for v in range(first, first + count):
        off = (128 * v - HALO_LANES) % 24
        out.append(jnp.where(lane < 96, turn(x, -off), turn(x, 24 - off)))
    return jnp.concatenate(out, axis=1)


def kernel(
    dims,
    en, ee, eu, hn, he, hr, h_sigma, h_lat, h_lon, h_step, h_amp, h_table,
    o_en, o_ee, o_eu, o_hn, o_he, o_hr, o_zon,
    ext, far_out, far_in, buf, src, coef, lanes, zon, zon_cap,
    sums_out, sums_in, zone_in, strip, small, sigma, f_lat, f_lon, f_step, f_amp, table,
    load, send_b, recv_b, send_f, recv_f, send_l, recv_l, send_c, recv_c, send_r, recv_r,
    send_s, recv_s, send_z, recv_z,
    ack_lon, ack_lat, ack_cross,
):
    n_lat, n_lon, layers, dt, ly = dims
    fields = (en, ee, eu, hn, he, hr)
    rows, width = en.shape
    strokes = h_lat.shape[1]
    wide = width + 2 * HALO_LANES
    tall = rows + 2 * HALO_ROWS
    vregs = wide // 128
    live = rows + 16
    low = HALO_ROWS
    lat, lon = lax.axis_index("lat"), lax.axis_index("lon")
    own_r = pl.ds(low, rows)
    own_c = pl.ds(HALO_LANES, width)

    def at(a, b):
        row = jnp.clip(lat + a, 0, n_lat - 1) if a else lat
        return {"lat": row, "lon": lax.rem(lon + b + n_lon, n_lon)}

    def there(a):
        return lat + a >= 0 if a < 0 else lat + a < n_lat

    def shared(a):
        return lax.rem(lat, 2) == (0 if a > 0 else 1)

    def across(a):
        return jnp.logical_and(there(a), jnp.logical_not(shared(a)))

    def signal(sem, a, b):
        pl.semaphore_signal(sem, inc=1, device_id=at(a, b), device_id_type=MESH)

    barrier = pltpu.get_barrier_semaphore()
    for k in range(1, n_lon):
        pl.when(lon + k < n_lon)(lambda k=k: signal(barrier, 0, k))
    pl.when(there(1))(lambda: signal(barrier, 1, 0))

    def crossing(a, b, later, act):
        wraps = lon == (n_lon - 1 if b > 0 else 0)
        is_later = jnp.logical_not(wraps) if b > 0 else wraps
        wanted = is_later if later else jnp.logical_not(is_later)
        pl.when(jnp.logical_and(across(a), wanted))(act)

    corners = [(a, b) for a in (-1, 1) for b in (-1, 1)]
    for a, b in corners:
        crossing(a, b, True, lambda a=a, b=b: signal(barrier, a, b))

    loads = [
        pltpu.make_async_copy(x, ext.at[f, own_r, own_c], load.at[f])
        for f, x in enumerate(fields)
    ]
    here_rows = h_table.at[pl.ds(pl.multiple_of(lat * rows, 8), tall), :]
    pairs = (
        (here_rows, table), (h_sigma, sigma), (h_lat, f_lat), (h_lon, f_lon),
        (h_step, f_step), (h_amp, f_amp),
    )
    loads += [pltpu.make_async_copy(x, y, load.at[6 + i]) for i, (x, y) in enumerate(pairs)]
    for copy in loads:
        copy.start()

    def lon_copy(b, f):
        i = f if b > 0 else 6 + f
        cut = pl.ds(width - 128, 128) if b > 0 else pl.ds(0, 128)
        land = pl.ds(HALO_LANES - 128, 128) if b > 0 else pl.ds(HALO_LANES + width, 128)
        return pltpu.make_async_remote_copy(
            src_ref=fields[f].at[:, cut],
            dst_ref=ext.at[f, own_r, land],
            send_sem=send_b.at[i],
            recv_sem=recv_b.at[i],
            device_id=at(0, b),
            device_id_type=MESH,
        )

    def far_copy(b):
        i = 0 if b > 0 else 1
        return pltpu.make_async_remote_copy(
            src_ref=far_out.at[i],
            dst_ref=far_in.at[i, :, own_r, :],
            send_sem=send_f.at[i],
            recv_sem=recv_f.at[i],
            device_id=at(0, b),
            device_id_type=MESH,
        )

    class Pieces:
        def __init__(self, a, parts, here, there, sends, recvs, i, b=0, off=0):
            shift = rows if a > 0 else -rows
            self.copies = [
                pltpu.make_async_remote_copy(
                    src_ref=here(pl.ds(row - off, count), pl.ds(col, span)),
                    dst_ref=there(pl.ds(row - shift, count), pl.ds(land, span)),
                    send_sem=sends.at[2 * i + n],
                    recv_sem=recvs.at[2 * i + n],
                    device_id=at(a, b),
                    device_id_type=MESH,
                )
                for n, (row, count, col, land, span) in enumerate(parts)
            ]

        def start(self):
            for copy in self.copies:
                copy.start()

        def wait_recv(self):
            for copy in self.copies:
                copy.wait_recv()

        def wait_send(self):
            for copy in self.copies:
                copy.wait_send()

    def nine(a, col, land, span):
        first, ninth = (low + rows - 8, low + rows - STEPS) if a > 0 else (low, low + STEPS - 1)
        return (first, 8, col, land, span), (ninth, 1, col, land, span)

    def whole(r, c):
        return ext.at[:, r, c]

    def lat_copy(a):
        parts = nine(a, HALO_LANES, HALO_LANES, width)
        return Pieces(a, parts, whole, whole, send_l, recv_l, 0 if a > 0 else 1)

    def corner_near(a, b):
        col = HALO_LANES + width - 128 if b > 0 else HALO_LANES
        land = HALO_LANES - 128 if b > 0 else HALO_LANES + width
        parts = nine(a, col, land, 128)
        parts = parts if a == b else parts[:1]
        return Pieces(a, parts, whole, whole, send_c, recv_c, corners.index((a, b)), b)

    def corner_far(a, b):
        i = 0 if b > 0 else 1
        parts = nine(a, 0, 0, 128)
        if a != b:
            parts = ((low + rows - 4 if a > 0 else low, 4, 0, 0, 128),)

        def here(r, c):
            return far_out.at[i, :, r, c]

        def there(r, c):
            return far_in.at[i, :, r, c]
        return Pieces(
            a, parts, here, there, send_c, recv_c, 4 + corners.index((a, b)), b, off=low
        )

    def relay_near(a, side, part):
        col = HALO_LANES - 128 if side == 0 else HALO_LANES + width
        i = part + 2 * side + (0 if a > 0 else 4)

        def these(r, c):
            return ext.at[pl.ds(3 * part, 3), r, c]
        return Pieces(a, nine(a, col, col, 128), these, these, send_r, recv_r, i)

    def relay_far(a, side):
        def these(r, c):
            return far_in.at[side, :, r, c]
        i = 8 + side + (0 if a > 0 else 2)
        return Pieces(a, nine(a, 0, 0, 128), these, these, send_r, recv_r, i)

    def sum_copy(k):
        return pltpu.make_async_remote_copy(
            src_ref=sums_out,
            dst_ref=sums_in.at[k],
            send_sem=send_s.at[k],
            recv_sem=recv_s.at[k],
            device_id=at(0, k),
            device_id_type=MESH,
        )

    def zone_copy(a):
        i = 0 if a > 0 else 1
        return pltpu.make_async_remote_copy(
            src_ref=strip,
            dst_ref=zone_in.at[i],
            send_sem=send_z.at[i],
            recv_sem=recv_z.at[i],
            device_id=at(a, 0),
            device_id_type=MESH,
        )

    def all_fields(make, side, act):
        for f in range(6):
            getattr(make(side, f), act)()

    crossed = jnp.where(lon == n_lon - 1, 2, jnp.where(lon == 0, 0, 1))
    crossed = jnp.where(jnp.logical_or(across(-1), across(1)), crossed, 0)
    earlier = lon + (lat > 0).astype(jnp.int32) + crossed
    pl.when(earlier > 0)(lambda: pl.semaphore_wait(barrier, earlier))
    for k in range(n_lon - 1, 0, -1):
        pl.when(lon - k >= 0)(lambda k=k: signal(ack_lon.at[k], 0, -k))
    pl.when(there(-1))(lambda: signal(ack_lat, -1, 0))
    for a, b in corners:
        crossing(a, b, False, lambda a=a, b=b: signal(ack_cross.at[0 if b < 0 else 1], a, b))

    pl.when(lon == n_lon - 1)(lambda: all_fields(lon_copy, 1, "start"))
    pl.when(lon > 0)(lambda: all_fields(lon_copy, -1, "start"))

    for a, first in ((-1, 0), (1, low + rows)):
        def clear(first=first):
            ext[:, first:first + low, :] = jnp.zeros((6, low, wide), jnp.float32)
            far_in[:, :, first:first + low, :] = jnp.zeros((2, 4, low, 128), jnp.float32)
        pl.when(jnp.logical_not(there(a)))(clear)

    for copy in loads[:7]:
        copy.wait()

    pl.when(there(-1))(lambda: lat_copy(-1).start())
    for a, b in corners:
        crossing(a, b, False, lambda a=a, b=b: corner_near(a, b).start())

    half = lax.broadcasted_iota(jnp.int32, (rows, 128), 1)
    mid = [ext[f, own_r, pl.ds(HALO_LANES + 128, 128)] for f in range(6)]
    end = [ext[f, own_r, pl.ds(HALO_LANES + width - 256, 128)] for f in range(6)]
    far_out[0, 0] = jnp.where(half >= 64, end[EN], turn(end[EE], 64))
    far_out[0, 1] = jnp.where(half >= 64, end[EU], turn(end[HN], 64))
    far_out[0, 2] = jnp.where(half >= 64, end[HE], turn(end[HR], 64))
    outer = turn(end[NINTH[0]], -40)
    for m in range(1, len(NINTH)):
        outer = jnp.where(half < 24 * m, outer, turn(end[NINTH[m]], 24 * m - 40))
    far_out[0, 3] = outer
    far_out[1, 0] = mid[EN]
    far_out[1, 1] = mid[EU]
    far_out[1, 2] = jnp.where(half < 64, mid[EE], turn(mid[HN], 64))
    far_out[1, 3] = jnp.where(half < 64, mid[HE], turn(mid[HR], 64))
    for a, b in corners:
        crossing(a, b, False, lambda a=a, b=b: corner_far(a, b).start())
    pl.when(lon == n_lon - 1)(lambda: far_copy(1).start())
    pl.when(lon > 0)(lambda: far_copy(-1).start())

    def fold(x):
        for by in (width // 2, width // 4, width // 8, width // 16):
            x = x + turn(x, by)
        return x[:, :128] * (1.0 / (n_lon * (width // layers)))

    lane = lax.broadcasted_iota(jnp.int32, (8, 128), 1)
    kept = jnp.broadcast_to(table[low:low + rows, C_KEEP:C_KEEP + 1], (rows, 128))
    bands = rows // 8
    for n, f in enumerate((EE, HN, HR)):
        folded = fold(ext[f, own_r, own_c])
        if f != HR:
            folded = kept * folded
        packed = folded[0:8]
        for band in range(1, bands):
            packed = jnp.where(lane < layers * band, packed, folded[8 * band:8 * band + 8])
        sums_out[8 * n:8 * n + 8, :] = packed
    for k in range(1, n_lon):
        pl.when(lon + k >= n_lon)(lambda k=k: sum_copy(k).start())

    def serve(k):
        def to_later():
            pl.semaphore_wait(ack_lon.at[k], 1)
            if k == 1:
                all_fields(lon_copy, 1, "start")
                far_copy(1).start()
            if k == n_lon - 1:
                all_fields(lon_copy, -1, "start")
                far_copy(-1).start()
            sum_copy(k).start()
        pl.when(lon + k < n_lon)(to_later)

    serve(1)
    def to_north():
        pl.semaphore_wait(ack_lat, 1)
        lat_copy(1).start()
    pl.when(there(1))(to_north)
    for a, b in corners:
        if b > 0:
            def corner_later(a=a, b=b):
                pl.semaphore_wait(ack_cross.at[0], 1)
                corner_near(a, b).start()
                corner_far(a, b).start()
            crossing(a, b, True, corner_later)
    for copy in loads[7:]:
        copy.wait()
    rows_tab = table[...]
    for c in range(10):
        coef[c] = jnp.broadcast_to(rows_tab[:, c:c + 1], (tall, 128))
    small[...] = jnp.zeros((8, 128), jnp.float32)
    small[0:1, 0:layers] = sigma[...]
    one = jnp.broadcast_to(small[0:1, :], (8, 128))
    pair = one + turn(one, 24)
    sig = pair + turn(pair, 48) + turn(one, 96)
    half = 0.5 * dt * sig
    dec = (1.0 - half) / (1.0 + half)
    drv = dt / (1.0 + half)

    at_lane = lax.broadcasted_iota(jnp.int32, (8, wide), 1) + 8
    layer = at_lane - 24 * div24(at_lane)
    lanes[0] = spread(dec, 0, vregs)
    lanes[1] = spread(drv, 0, vregs)
    lanes[2] = jnp.where(layer == layers - 1, 0.0, 1.0)
    lanes[3] = jnp.where(layer == 0, 0.0, 1.0)

    half_lanes = lax.broadcasted_iota(jnp.int32, (1, 128), 1) < strokes

    def twice(x):
        return jnp.concatenate([x, x], axis=1)

    def column(x):
        return jnp.transpose(jnp.broadcast_to(x.astype(jnp.float32), (128, 2 * strokes)))

    cell = div24(at_lane[0:1]) - 11 + lon * (width // layers)
    total_lon = n_lon * (width // layers)
    cell = jnp.where(cell < 0, cell + total_lon, cell)
    cell = jnp.where(cell >= total_lon, cell - total_lon, cell)
    cell = jnp.where(layer[0:1] < CHANNEL, cell, -1).astype(jnp.float32)
    lon_of = jnp.concatenate([column(twice(f_lon[...]))] * vregs, axis=1)
    cells = (jnp.broadcast_to(cell, (2 * strokes, wide)) == lon_of).astype(jnp.float32)
    cells = cells.astype(jnp.bfloat16)
    row_no = lax.broadcasted_iota(jnp.int32, (live, 2 * strokes), 0) + (lat * rows - 8)
    in_row = jnp.where(
        row_no == twice(f_lat[...]),
        jnp.broadcast_to(twice(f_amp[...]), (live, 2 * strokes)),
        0.0,
    )
    steps_of = twice(f_step[...])
    left, right = [], []
    for s in range(STEPS):
        amps = jnp.where(steps_of == s, in_row, 0.0)
        upper = amps.astype(jnp.bfloat16).astype(jnp.float32)
        middle = (amps - upper).astype(jnp.bfloat16).astype(jnp.float32)
        left.append(jnp.where(half_lanes, upper, middle).astype(jnp.bfloat16))
        right.append(jnp.where(half_lanes, amps - upper - middle, 0.0).astype(jnp.bfloat16))
    total = None
    for part in (left, right):
        term = lax.dot_general(
            jnp.concatenate(part, axis=0), cells, (((1,), (0,)), ((), ())),
            preferred_element_type=jnp.float32,
        )
        total = term if total is None else total + term
    src[...] = total

    for k in range(2, n_lon):
        serve(k)
    for a, b in corners:
        if b < 0:
            def corner_last(a=a, b=b):
                pl.semaphore_wait(ack_cross.at[1], 1)
                corner_near(a, b).start()
                corner_far(a, b).start()
            crossing(a, b, True, corner_last)

    for part in (0, 1):
        for side in (0, 1):
            for f in range(3 * part, 3 * part + 3):
                lon_copy(1 if side == 0 else -1, f).wait_recv()
            for a in (-1, 1):
                pl.when(shared(a))(
                    lambda a=a, side=side, part=part: relay_near(a, side, part).start()
                )
    for side in (0, 1):
        far_copy(1 if side == 0 else -1).wait_recv()
        for a in (-1, 1):
            pl.when(shared(a))(lambda a=a, side=side: relay_far(a, side).start())

    for k in range(1, n_lon):
        sum_copy(k).wait_recv()
    mean = sums_out[...]
    for k in range(1, n_lon):
        mean = mean + sums_in[k]
    strip[...] = mean
    for a in (-1, 1):
        pl.when(there(a))(lambda a=a: zone_copy(a).start())

    def unpack(x, band):
        y = jnp.where(lane < layers, turn(x, -layers * band), 0.0)
        p = y + turn(y, 24)
        return p + turn(p, 48) + turn(y, 96)

    edge = jnp.zeros((3, low, 128), jnp.float32)
    for z in (zon, zon_cap):
        z[:, 0:low, :] = edge
        z[:, low + rows:, :] = edge
    for f in range(3):
        for band in range(bands):
            own = unpack(mean[8 * f:8 * f + 8], band)
            for z in (zon, zon_cap):
                z[f, low + 8 * band:low + 8 * band + 8, :] = own

    half = lax.broadcasted_iota(jnp.int32, (8, 128), 1)

    def unpack_far(r):
        here = slice(r, r + 8)
        one, two, three, outer = [far_in[0, n, here, :] for n in range(4)]
        inside = {
            EN: one, EE: turn(one, 64), EU: two, HN: turn(two, 64), HE: three, HR: turn(three, 64)
        }
        for m, f in enumerate(NINTH):
            inside[f] = jnp.where(half >= 64, inside[f], turn(outer, 40 - 24 * m))
        for f, x in inside.items():
            ext[f, here, 0:128] = x
        one, two, three, outer = [far_in[1, n, here, :] for n in range(4)]
        inside = {
            EN: one, EE: three, EU: two, HN: turn(three, 64), HE: outer, HR: turn(outer, 64)
        }
        for f, x in inside.items():
            ext[f, here, wide - 128:wide] = x

    for r in range(low, low + rows, 8):
        unpack_far(r)

    for a in (-1, 1):
        def take(a=a):
            lat_copy(a).wait_recv()
        pl.when(there(-a))(take)

        def take_corners(a=a):
            for b in (-1, 1):
                corner_near(a, b).wait_recv()
                corner_far(a, b).wait_recv()
        pl.when(across(-a))(take_corners)

        def take_relays(a=a):
            for side in (0, 1):
                for part in (0, 1):
                    relay_near(a, side, part).wait_recv()
                relay_far(a, side).wait_recv()
        pl.when(shared(-a))(take_relays)

    for r in (*range(0, low, 8), *range(low + rows, tall, 8)):
        unpack_far(r)

    def pole():
        last = pl.ds(low + rows - 8, 8)
        keep = jnp.broadcast_to(table[low + rows - 8:low + rows, C_KEEP:C_KEEP + 1], (8, wide))
        for f in (EE, EU, HN):
            ext[f, last, :] = keep * ext[f, last, :]
    pl.when(jnp.logical_not(there(1)))(pole)

    def zone_rows():
        for a in (-1, 1):
            def take_zone(a=a):
                zone_copy(a).wait_recv()
                i, row, band = (0, low - 8, bands - 1) if a > 0 else (1, low + rows, 0)
                for f in range(3):
                    zon[f, row:row + 8, :] = unpack(zone_in[i, 8 * f:8 * f + 8, :], band)
            pl.when(there(-a))(take_zone)

    outs = (o_en, o_ee, o_eu, o_hn, o_he, o_hr)
    march(dims, ext, buf, src, coef, lanes, zon, zon_cap, outs, o_zon, zone_rows)

    for a in (-1, 1):
        def sent(a=a):
            zone_copy(a).wait_send()
            lat_copy(a).wait_send()
        pl.when(there(a))(sent)

        def sent_corners(a=a):
            for b in (-1, 1):
                corner_near(a, b).wait_send()
                corner_far(a, b).wait_send()
        pl.when(across(a))(sent_corners)

        def sent_relays(a=a):
            for side in (0, 1):
                for part in (0, 1):
                    relay_near(a, side, part).wait_send()
                relay_far(a, side).wait_send()
        pl.when(shared(a))(sent_relays)
    for k in range(1, n_lon):
        sum_copy(k).wait_send()
    for b in (-1, 1):
        all_fields(lon_copy, b, "wait_send")
        far_copy(b).wait_send()


def march(dims, ext, buf, src, coef, lanes, zon, zon_cap, outs, o_zon, zone_rows):
    n_lat, n_lon, layers, dt, ly = dims
    tall, wide = buf.shape[1:]
    rows, width = tall - 2 * HALO_ROWS, wide - 2 * HALO_LANES
    groups = tall // 8
    own_groups = range(HALO_ROWS // 8, groups - HALO_ROWS // 8)
    low = HALO_ROWS
    lat = lax.axis_index("lat")
    own_r = slice(low, low + rows)
    z_dec, z_drv, z_top, z_bot = [lanes.at[i, :, HALO_LANES:HALO_LANES + 128] for i in (0, 1, 2, 3)]
    lane = lax.broadcasted_iota(jnp.int32, (rows, 128), 1)

    def record(s):
        both = jnp.where(lane < layers, zon[0, own_r, :], turn(zon[2, own_r, :], layers))
        both = jnp.transpose(both)
        o_zon[s, 0] = both[0:layers]
        o_zon[s, 1] = both[layers:2 * layers]

    def zonal_h(zon, span):
        for g in span:
            r = 8 * g
            east = zon[0, r:r + 8, :]
            zon[2, r:r + 8, :] = (
                zon[2, r:r + 8, :]
                - coef[C_AS, r:r + 8] * zon[0, r - 1:r + 7, :]
                + coef[C_BE, r:r + 8] * east
            )
            zon[1, r:r + 8, :] = zon[1, r:r + 8, :] - coef[C_DT, r:r + 8] * (
                z_top[...] * turn(east, -1) - east
            )

    def zonal_e(zon, span):
        for g in span:
            r = 8 * g
            up, north = zon[2, r:r + 8, :], zon[1, r:r + 8, :]
            zon[0, r:r + 8, :] = z_dec[...] * zon[0, r:r + 8, :] + z_drv[...] * (
                coef[C_LY, r:r + 8] * (zon[2, r + 1:r + 9, :] - up)
                - (north - z_bot[...] * turn(north, 1))
            )

    def magnetic(old, a, b, span, beyond, last=False):
        count = (b - a) // 128

        def rowc(c, g):
            return jnp.concatenate([coef[c, 8 * g:8 * g + 8]] * count, axis=1)

        top = lanes[2, :, a:b]
        for g in (*span, *beyond):
            r = 8 * g
            here, south = slice(r, r + 8), slice(r - 1, r + 7)
            e_n, e_e, e_u = old[EN, here, a:b], old[EE, here, a:b], old[EU, here, a:b]
            up = (
                old[HR, here, a:b]
                - rowc(C_AS, g) * old[EE, south, a:b]
                + rowc(C_BE, g) * e_e
                - rowc(C_CN, g) * (turn(e_n, -layers) - e_n)
            )
            if g in (own_groups[0], own_groups[-1]):
                row = lax.broadcasted_iota(jnp.int32, (8, b - a), 0) + (lat * rows - low + r)
                pole = 0 if g == own_groups[0] else n_lat * rows - 1
                up = jnp.where(row == pole, spread(zon_cap[2, here], a // 128, count), up)
            fresh = {HR: up}
            fresh[HE] = (
                old[HE, here, a:b]
                - (dt / ly) * (e_u - old[EU, south, a:b])
                + dt * (top * turn(e_n, -1) - e_n)
            )
            if g in span:
                fresh[HN] = (
                    old[HN, here, a:b]
                    - rowc(C_DU, g) * (e_u - turn(e_u, -layers))
                    - rowc(C_DT, g) * (top * turn(e_e, -1) - e_e)
                )
            for f, x in fresh.items():
                buf[f, here, a:b] = x
                if last and g in span:
                    outs[f][r - low:r - low + 8, :] = x[:, HALO_LANES - a:HALO_LANES - a + width]

    def electric(old, s, a, b, first, span, last=False):
        count = (b - first) // 128
        skip = first - a

        def rowc(c, g):
            return jnp.concatenate([coef[c, 8 * g:8 * g + 8]] * count, axis=1)

        def turned(x, by):
            return turn(x, by)[:, skip:]

        decay, drive, bot = [lanes[i, :, first:b] for i in (0, 1, 3)]
        for g in span:
            r = 8 * g
            here, north = slice(r, r + 8), slice(r + 1, r + 9)
            w_n, w_e, w_r = buf[HN, here, a:b], buf[HE, here, a:b], buf[HR, here, a:b]
            h_n, h_e, h_r = w_n[:, skip:], w_e[:, skip:], w_r[:, skip:]
            fresh = {}
            fresh[EN] = decay * old[EN, here, first:b] + drive * (
                h_e - bot * turned(w_e, 1) - rowc(C_GC, g) * (h_r - turned(w_r, layers))
            )
            fresh[EE] = decay * old[EE, here, first:b] + drive * (
                rowc(C_LY, g) * (buf[HR, north, first:b] - h_r) - (h_n - bot * turned(w_n, 1))
            )
            fresh[EU] = (
                decay * old[EU, here, first:b]
                + drive
                * (
                    rowc(C_IC, g) * h_e
                    - rowc(C_JN, g) * buf[HE, north, first:b]
                    + rowc(C_KL, g) * (h_n - turned(w_n, layers))
                    + src[pl.ds(pl.multiple_of(s * (rows + 16) + r - 8, 8), 8), first:b]
                )
            )

            for f, x in fresh.items():
                if last:
                    outs[f][r - low:r - low + 8, :] = x
                else:
                    buf[f, here, first:b] = x

    inner = range(1, groups - 1)

    def step(old, s, a, b, beyond):
        zonal_h(zon_cap, own_groups)
        magnetic(old, a, b, inner, beyond)
        zonal_e(zon_cap, own_groups)
        electric(old, s, a, b, a, inner)

    def means(s):
        record(s)
        zonal_h(zon, inner)
        zonal_e(zon, inner)

    middle = STEPS - 1 - STEPS // 2

    def early(s, carry):
        step(buf, s, 0, wide, ())
        return carry

    def late(s, carry):
        means(2 * (s - middle))
        means(2 * (s - middle) + 1)
        step(buf, s, 128, wide - 128, ())
        return carry

    step(ext, 0, 0, wide, (groups - 1,))
    for s in range(1, middle):
        early(s, 0)
    zone_rows()
    for s in range(middle, STEPS - 1):
        late(s, 0)
    record(STEPS - 1)
    zonal_h(zon_cap, own_groups)
    magnetic(buf, 128, wide - 128, own_groups, (own_groups[-1] + 1,), last=True)
    electric(buf, STEPS - 1, 128, wide - HALO_LANES, HALO_LANES, own_groups, last=True)


def hand_over(*refs):
    count = len(refs) // 2
    copies = [
        pltpu.make_async_copy(refs[i], refs[count + i], refs[-1].at[i]) for i in range(count)
    ]
    for copy in copies:
        copy.start()
    for copy in copies:
        copy.wait()


def body(
    efield_north,
    efield_east,
    efield_up,
    hfield_north,
    hfield_east,
    hfield_up,
    sigma_profile,
    flash_lat,
    flash_lon,
    flash_step,
    flash_amp,
):
    rows, width = efield_north.shape
    layers = sigma_profile.shape[0]
    n_lat, n_lon = lax.axis_size("lat"), lax.axis_size("lon")
    lat_count, lon_count = rows * n_lat, (width // layers) * n_lon
    dims = (
        n_lat,
        n_lon,
        layers,
        time_step(lat_count, lon_count),
        RADIUS_CELLS * math.pi / lat_count,
    )
    wide, tall = width + 2 * HALO_LANES, rows + 2 * HALO_ROWS
    f32 = jnp.float32
    vmem = pl.BlockSpec(memory_space=pltpu.VMEM)
    dma = pltpu.SemaphoreType.DMA
    hbm = pl.BlockSpec(memory_space=pltpu.HBM)
    strokes = flash_lat.shape[0]
    n_live = rows + 16
    outs = [jax.ShapeDtypeStruct((rows, width), f32)] * 6
    outs += [jax.ShapeDtypeStruct((STEPS, 2, layers, rows), f32)]
    held = pl.pallas_call(
        functools.partial(kernel, dims),
        out_shape=outs,
        in_specs=[hbm] * 12,
        out_specs=[vmem] * 7,
        scratch_shapes=[
            pltpu.VMEM((6, tall, wide), f32),
            pltpu.VMEM((2, 4, rows, 128), f32),
            pltpu.VMEM((2, 4, tall, 128), f32),
            pltpu.VMEM((6, tall, wide), f32),
            pltpu.VMEM((STEPS * n_live, wide), f32),
            pltpu.VMEM((10, tall, 128), f32),
            pltpu.VMEM((4, 8, wide), f32),
            pltpu.VMEM((3, tall, 128), f32),
            pltpu.VMEM((3, tall, 128), f32),
            pltpu.VMEM((24, 128), f32),
            pltpu.VMEM((n_lon, 24, 128), f32),
            pltpu.VMEM((2, 24, 128), f32),
            pltpu.VMEM((24, 128), f32),
            pltpu.VMEM((8, 128), f32),
            pltpu.VMEM((1, layers), f32),
            pltpu.VMEM((1, strokes), jnp.int32),
            pltpu.VMEM((1, strokes), jnp.int32),
            pltpu.VMEM((1, strokes), jnp.int32),
            pltpu.VMEM((1, strokes), f32),
            pltpu.VMEM((tall, 128), f32),
            dma((12,)),
            dma((12,)), dma((12,)), dma((2,)), dma((2,)), dma((4,)), dma((4,)),
            dma((16,)), dma((16,)), dma((24,)), dma((24,)),
            dma((n_lon,)), dma((n_lon,)), dma((2,)), dma((2,)),
            pltpu.SemaphoreType.REGULAR((n_lon,)),
            pltpu.SemaphoreType.REGULAR,
            pltpu.SemaphoreType.REGULAR((2,)),
        ],
        compiler_params=pltpu.CompilerParams(
            collective_id=0, has_side_effects=True, vmem_limit_bytes=VMEM_GRANT
        ),
    )(*(pltpu.with_memory_space_constraint(x, pltpu.HBM) for x in (
        efield_north,
        efield_east,
        efield_up,
        hfield_north,
        hfield_east,
        hfield_up,
        sigma_profile[None, :],
        flash_lat[None, :],
        flash_lon[None, :],
        flash_step[None, :],
        flash_amp[None, :],
        jnp.asarray(row_table(lat_count, lon_count)),
    )))
    results = pl.pallas_call(
        hand_over,
        out_shape=outs,
        in_specs=[vmem] * 7,
        out_specs=[hbm] * 7,
        scratch_shapes=[dma((7,))],
        compiler_params=pltpu.CompilerParams(vmem_limit_bytes=VMEM_GRANT),
    )(*held)
    return (*results[:6], jnp.transpose(results[6], (0, 1, 3, 2)))


def solution(mesh):
    fields = P("lat", "lon")
    return jax.shard_map(
        body,
        mesh=mesh,
        in_specs=(fields,) * 6 + (P(),) * 5,
        out_specs=(fields,) * 6 + (P(None, None, "lat", None),),
        check_vma=False,
    )
```
